128 devices in a mesh: slab: 8 (over x, core), grp: 16 (over y, z).
Axes of the slice: x: 4, y: 4, z: 4, core: 2. Of those that a mesh axis runs over, the one named last changes fastest.
Arguments:
- raw_frames: bfloat16 [512, 96, 10752], P('grp', 'slab'), may hold values from -700 to 700
- mask_index: int32 [229376], P(('slab', 'grp')), may hold values from 0 to 1032191, as said below
- subspace: bfloat16 [1200, 229376], P(None, ('slab', 'grp')), may hold values from -6 to 6
- rotation: bfloat16 [1712, 1200], replicated, may hold values from -0.15625 to 0.15625
Outputs:
- gram: float32 [1712, 1712], P('grp')
- new_subspace: bfloat16 [1200, 229376], P(None, ('slab', 'grp'))
The draws below stay inside these ranges and needn't reach their ends.
Inputs may be any that keep to these rules, and one draw needn't show every extreme that they name: `mask_index`: entries are distinct flat grid positions that come in runs of 128 consecutive positions, each run starting at a multiple of 128; the 28672 entries of aligned block s lie in z planes s * 12 to (s + 1) * 12 - 1 and rise within the block; the first 7168 of a block lie in its lowest 3 planes, the last 7168 in its highest 3 planes, the others in the planes between.
All inputs are finite; a program needn't handle non-finite values.
Results may differ from the reference program's by a relative error of at most 0.006.
Values may be sent and summed in bfloat16 or wider, within the bound.
No kernel may reach another device: no remote copies, remote signals or barrier semaphores. Data moves between devices by JAX's collectives and lax.ppermute only.
A program may use at most 192 MiB of HBM per device.

```python
import math
import jax
import jax.numpy as jnp
from jax import lax

NX = 96
NYX = 10752
RUN = 128
CZ = 12
NZ = 96
RAD = 3
FRAMES = 512
K = 1200
KX = 1712
MV_DEV = 1792
MASKED = 229376
SLAB_ROWS = 28672
RIM_ROWS = 7168


def pick_runs(run_key, run_total, run_count, first_cell):
    chosen = jnp.sort(jax.random.permutation(run_key, run_total)[:run_count]).astype(jnp.int32)
    within = jnp.arange(RUN, dtype=jnp.int32)
    return (chosen[:, None] * RUN + within[None, :]).reshape(-1) + first_cell


def draw_mask_index(key, part):
    slab_count = NZ // CZ
    slab_cells = CZ * NYX
    rim_runs = RAD * NYX // RUN
    middle_runs = (CZ - 2 * RAD) * NYX // RUN
    middle_rows = SLAB_ROWS - 2 * RIM_ROWS

    def per_slab(slab_number):
        slab_key = jax.random.fold_in(key, slab_number)
        lower = pick_runs(jax.random.fold_in(slab_key, 1), rim_runs, RIM_ROWS // RUN, 0)
        upper = pick_runs(jax.random.fold_in(slab_key, 2), rim_runs, RIM_ROWS // RUN, (CZ - RAD) * NYX)
        pieces = [lower]
        if middle_rows > 0:
            pieces.append(pick_runs(jax.random.fold_in(slab_key, 3), middle_runs, middle_rows // RUN, RAD * NYX))
        pieces.append(upper)
        return jnp.concatenate(pieces) + slab_number * slab_cells
    return jax.vmap(per_slab)(jnp.arange(slab_count, dtype=jnp.int32)).reshape(-1).astype(jnp.int32)


def draw_raw_frames(key, part):
    noise_key = jax.random.fold_in(key, 11)
    rough_key = jax.random.fold_in(key, 12)
    depth = jnp.arange(NZ, dtype=jnp.float32) / max(NZ - 1, 1)
    base = jax.random.truncated_normal(noise_key, -4.0, 4.0, (FRAMES, NZ, NYX), jnp.float32)
    depth_scale = jnp.exp(jnp.log(10.0) * depth)
    frame_scale = jnp.exp(jnp.log(3.0) * jnp.arange(FRAMES, dtype=jnp.float32) / max(FRAMES - 1, 1))
    rough = jnp.exp(jax.random.uniform(rough_key, (1, NZ, NYX), jnp.float32, -0.7, 0.7))
    values = base * rough * depth_scale[None, :, None] * frame_scale[:, None, None]
    return values.astype(jnp.bfloat16)


def spiked(result, own_key, source, target, parts, factor):
    owner, partner = [(jnp.arange(result.shape[position]) // (result.shape[position] // parts)).reshape([-1 if axis == position else 1 for axis in range(result.ndim)]) for position in (source, target)]
    chosen = jax.random.permutation(own_key, parts)[partner]
    strong = (owner == chosen) | (owner == (partner + parts // 2) % parts)
    return jnp.where(strong, factor * result, result)


def levels(rng, dims, cuts, smallest, top_value):
    def one(axis_at, blocks):
        steps = jax.random.uniform(jax.random.fold_in(jax.random.fold_in(rng, 6), axis_at), (blocks,), jnp.float32, smallest / len(cuts), top_value / len(cuts))
        return jnp.repeat(jnp.exp(steps), dims[axis_at] // blocks).reshape((-1,) + (1,) * (len(dims) - axis_at - 1))

    gain = one(*cuts[0])
    for cut in cuts[1:]:
        gain = gain * one(*cut)
    return gain


def centred(key, dims, scale, most, split=(), held_as=jnp.bfloat16):
    factor_of = levels(key, dims, split, -0.22, 0.18) if split else 1.0
    entries = jax.random.normal(key, dims, jnp.float32) * scale * factor_of
    return jnp.minimum(jnp.maximum(entries, -most), most).astype(held_as)


def bell_draw_with(key, shape, deviation, most, shards, heavy, kind=jnp.bfloat16):
    drawn = deviation * jax.random.normal(key, shape, jnp.float32)
    if shards:
        drawn = drawn * levels(key, shape, shards, -0.22, 0.18)
    return jnp.clip(spiked(drawn, jax.random.fold_in(key, 3), *heavy), -most, most).astype(kind)


def setup_inputs(seed: int = 0) -> dict:
    splits = jax.random.split(jax.random.key(seed), 5)
    return {
        "raw_frames": draw_raw_frames(jax.random.fold_in(splits[4], 71), 0),
        "mask_index": draw_mask_index(jax.random.fold_in(splits[4], 71), 0),
        "subspace": bell_draw_with(splits[2], (K, MASKED), 1.0, 6.0, ((1, 128),), (1, 0, 16, 2.0)),
        "rotation": centred(splits[3], (KX, K), KX ** -0.5, 0.15625),
    }


smooth_sigma = 1.0617
epsilon = 1e-06

def tap_weights():
    unscaled = [math.exp(-offset * offset / (2.0 * smooth_sigma * smooth_sigma)) for offset in range(-RAD, RAD + 1)]
    summed = sum(unscaled)
    return [weight / summed for weight in unscaled]

def along_rows(volume):
    weights = tap_weights()
    extent = volume.shape[-1]
    column = lax.broadcasted_iota(jnp.int32, (extent,), 0) % NX
    padded = jnp.pad(volume, [(0, 0)] * (volume.ndim - 1) + [(RAD, RAD)])
    summed = jnp.zeros(volume.shape, jnp.float32)
    for offset in range(-RAD, RAD + 1):
        shifted = lax.slice_in_dim(padded, RAD + offset, RAD + offset + extent, axis=volume.ndim - 1)
        inside = (column + offset >= 0) & (column + offset < NX)
        summed = summed + weights[offset + RAD] * jnp.where(inside, shifted, 0.0)
    return summed

def along_columns(volume):
    weights = tap_weights()
    extent = volume.shape[-1]
    reach_cells = RAD * NX
    padded = jnp.pad(volume, [(0, 0)] * (volume.ndim - 1) + [(reach_cells, reach_cells)])
    summed = jnp.zeros(volume.shape, jnp.float32)
    for offset in range(-RAD, RAD + 1):
        begin = reach_cells + offset * NX
        shifted = lax.slice_in_dim(padded, begin, begin + extent, axis=volume.ndim - 1)
        summed = summed + weights[offset + RAD] * shifted
    return summed

def along_depth(padded, slab_depth):
    weights = tap_weights()
    summed = None
    for offset in range(-RAD, RAD + 1):
        shifted = lax.slice_in_dim(padded, RAD + offset, RAD + offset + slab_depth, axis=padded.ndim - 2)
        term = weights[offset + RAD] * shifted
        summed = term if summed is None else summed + term
    return summed

def reference(raw_frames, mask_index, subspace, rotation):

    def one_frame(frame_data):
        planar = along_columns(along_rows(frame_data.astype(jnp.float32)))
        padded = jnp.pad(planar, [(RAD, RAD), (0, 0)])
        volume = along_depth(padded, NZ).reshape(-1)
        return jnp.take(volume, mask_index, axis=0).astype(jnp.bfloat16)
    smoothed = lax.map(one_frame, raw_frames)
    subject_frames = FRAMES // 2
    halves = smoothed.astype(jnp.float32).reshape(2, subject_frames, MASKED)
    centered = (halves - lax.optimization_barrier(jnp.mean(halves, axis=1, keepdims=True))).astype(jnp.bfloat16)
    widened = centered.astype(jnp.float32)
    power = lax.optimization_barrier(jnp.sum(widened * widened, axis=(1, 2)))
    scales = lax.rsqrt(power / (MASKED * subject_frames) + epsilon)
    centered = centered.reshape(FRAMES, MASKED)
    row_scale = jnp.concatenate([jnp.ones((K,), jnp.float32), jnp.repeat(scales, subject_frames)])
    rotation_wide = rotation.astype(jnp.float32)
    basis_rot = rotation_wide[:K]
    first_rot = rotation_wide[K:K + subject_frames]
    second_rot = rotation_wide[K + subject_frames:]
    highest = lax.Precision.HIGHEST
    block_count = MASKED // MV_DEV

    def accumulate(gram_raw, block_index):
        first_col = (block_index * MV_DEV).astype(jnp.int32)
        basis_cols = lax.dynamic_slice_in_dim(subspace, first_col, MV_DEV, 1).astype(jnp.float32)
        data_cols = lax.dynamic_slice_in_dim(centered, first_col, MV_DEV, 1).astype(jnp.float32)
        stacked = jnp.concatenate([basis_cols, data_cols], 0)
        gram_raw = gram_raw + jnp.dot(stacked, stacked.T, precision=highest)
        from_basis = jnp.dot(basis_rot.T, basis_cols, precision=highest)
        from_first = jnp.dot(first_rot.T, data_cols[:subject_frames], precision=highest)
        from_second = jnp.dot(second_rot.T, data_cols[subject_frames:], precision=highest)
        row_block = (from_basis + scales[0] * from_first + scales[1] * from_second).astype(jnp.bfloat16)
        return (gram_raw, row_block)
    gram_raw, pieces = lax.scan(accumulate, jnp.zeros((KX, KX), jnp.float32), jnp.arange(block_count, dtype=jnp.int32))
    new_subspace = jnp.transpose(pieces, (1, 0, 2)).reshape(K, MASKED)
    gram = gram_raw * (row_scale[:, None] * row_scale[None, :]) / MASKED
    return (gram, new_subspace)
```

```python
import functools
import math

import jax
import jax.numpy as jnp
import numpy as np
from jax import lax
from jax.experimental import pallas as pl
from jax.experimental.pallas import tpu as pltpu
from jax.sharding import Mesh
from jax.sharding import PartitionSpec as P

NX = 96
RUN = 128
RAD = 3
K = 1200
KX = 1712
SUBJ = 256
ROWS = 107
WIN = 120
LEAD = 384
BLOCK = 256
PHASES = 3
GRP = 16
TAB = 64
TAB_MID = 31

smooth_sigma = 1.0617
epsilon = 1e-06


def tap_weights():
    unscaled = [
        math.exp(-offset * offset / (2.0 * smooth_sigma * smooth_sigma))
        for offset in range(-RAD, RAD + 1)
    ]
    summed = sum(unscaled)
    return [weight / summed for weight in unscaled]


def plane_matrix():
    taps = np.array(tap_weights())
    cells_in = np.arange(LEAD + BLOCK + LEAD)[:, None]
    cells_out = np.arange(BLOCK)[None, :]
    parts = []
    for phase in range(PHASES):
        column = (phase * BLOCK + cells_out) % NX
        reach = cells_in - LEAD - cells_out
        rows = np.floor((reach + NX // 2) / NX).astype(np.int64)
        along = reach - rows * NX
        ok = (np.abs(rows) <= RAD) & (np.abs(along) <= RAD) & (column + along >= 0) & (column + along < NX)
        weight = taps[np.clip(rows + RAD, 0, 2 * RAD)] * taps[np.clip(along + RAD, 0, 2 * RAD)]
        parts.append(np.where(ok, weight, 0.0))
    return np.stack(parts).astype(np.float32)


def depth_table():
    table = np.zeros((TAB,), np.float32)
    table[TAB_MID - RAD : TAB_MID + RAD + 1] = tap_weights()
    return table


def smooth_kernel(depth, own_ref, near_ref, tab_ref, mat_ref, raw_ref, mid_ref, rim_ref, up_ref, down_ref, pad, planar, sems):
    frames = raw_ref.shape[1]
    extent = raw_ref.shape[2]
    step = PHASES * BLOCK
    steps = extent // step
    tiles = extent // RUN

    def fetch(i):
        return pltpu.make_async_copy(
            raw_ref.at[:, :, pl.ds(i * step, step)],
            pad.at[:, :, pl.ds(LEAD + i * step, step)],
            sems.at[i],
        )

    for i in range(steps):
        fetch(i).start()
    edge = jnp.zeros((depth, frames, LEAD), pad.dtype)
    pad[:, :, :LEAD] = edge
    pad[:, :, LEAD + extent :] = edge
    fetch(0).wait()

    def block(i, carry):
        @pl.when(i + 1 < steps)
        def _():
            fetch(i + 1).wait()

        for phase in range(PHASES):
            start = pl.multiple_of(i * step + phase * BLOCK, BLOCK)
            cells = pad[:, :, pl.ds(start, LEAD + BLOCK + LEAD)].reshape(depth * frames, LEAD + BLOCK + LEAD)
            out = jnp.dot(cells, mat_ref[phase], preferred_element_type=jnp.float32)
            planar[:, :, pl.ds(start, BLOCK)] = out.reshape(depth, frames, BLOCK)
        return carry

    lax.fori_loop(0, steps, block, 0)

    taps = tap_weights()

    def place(tile):
        plane = tile // tiles
        return plane, pl.multiple_of((tile - plane * tiles) * RUN, RUN)

    per = mid_ref.shape[2] // RUN

    def middle(g, carry):
        for j in range(per):
            plane, lane = place(own_ref[(g + GRP // 4) * per + j])
            total = taps[0] * planar[plane - RAD, :, pl.ds(lane, RUN)]
            for k in range(1, 2 * RAD + 1):
                total = total + taps[k] * planar[plane - RAD + k, :, pl.ds(lane, RUN)]
            mid_ref[g, :, j * RUN : (j + 1) * RUN] = total.astype(mid_ref.dtype)
        return carry

    def some(tile, first, count, shift):
        plane, lane = place(tile)
        total = None
        for q in range(first, first + count):
            weight = tab_ref[q - plane + shift + TAB_MID]
            term = weight * planar[q, :, pl.ds(lane, RUN)]
            total = term if total is None else total + term
        return total

    def rims(g, carry):
        for j in range(per):
            cols = slice(j * RUN, (j + 1) * RUN)
            at = g * per + j
            up_ref[g, :, cols] = some(near_ref[at], depth - RAD, RAD, -depth)
            down_ref[g, :, cols] = some(near_ref[GRP // 4 * per + at], 0, RAD, depth)
            rim_ref[g, :, cols] = some(own_ref[at], 0, 2 * RAD, 0)
            rim_ref[GRP // 4 + g, :, cols] = some(own_ref[GRP * 3 // 4 * per + at], depth - 2 * RAD, 2 * RAD, 0)
        return carry

    lax.fori_loop(0, GRP // 4, rims, 0)
    lax.fori_loop(0, GRP // 2, middle, 0)


def smooth(own, near, raw):
    depth, frames, extent = raw.shape
    per_device = own.shape[0] // GRP * RUN
    smem = pl.BlockSpec(memory_space=pltpu.SMEM)
    vmem = pl.BlockSpec(memory_space=pltpu.VMEM)
    quarter = (GRP // 4, frames, per_device)
    half = (GRP // 2, frames, per_device)
    return pl.pallas_call(
        functools.partial(smooth_kernel, depth),
        out_shape=[
            jax.ShapeDtypeStruct(half, jnp.bfloat16),
            jax.ShapeDtypeStruct(half, jnp.float32),
            jax.ShapeDtypeStruct(quarter, jnp.float32),
            jax.ShapeDtypeStruct(quarter, jnp.float32),
        ],
        in_specs=[smem, smem, smem, vmem, pl.BlockSpec(memory_space=pl.ANY)],
        out_specs=[vmem] * 4,
        scratch_shapes=[
            pltpu.VMEM((depth, frames, extent + 2 * LEAD), jnp.bfloat16),
            pltpu.VMEM((depth, frames, extent), jnp.float32),
            pltpu.SemaphoreType.DMA((extent // (PHASES * BLOCK),)),
        ],
        compiler_params=pltpu.CompilerParams(vmem_limit_bytes=48 * 1024 * 1024),
        name="smooth",
    )(own, near, jnp.asarray(depth_table()), jnp.asarray(plane_matrix()).astype(jnp.bfloat16), raw)


def window_starts(length, count, window, total):
    return [min(8 * (length * i // 8), total - window) for i in range(count)]


def copies(value, axis, count):
    return lax.all_to_all(jnp.broadcast_to(value[None], (count, *value.shape)), axis, 0, 0, tiled=True)


def body(raw_frames, mask_index, subspace, rotation):
    depth = raw_frames.shape[1]
    extent = raw_frames.shape[2]
    per_device = subspace.shape[1]
    slab = ("x", "core")
    masked = per_device * 8 * GRP
    slab_at = lax.axis_index("x") * 2 + lax.axis_index("core")
    core = lax.axis_index("core")
    grp = lax.axis_index("grp")
    bf16 = jnp.bfloat16
    f32 = jnp.float32
    swap = [(0, 1), (1, 0)]

    tiles = mask_index.reshape(-1, RUN)[:, 0] // RUN - slab_at * (depth * extent // RUN)
    up = [(i, i + 1) for i in range(7)]
    down = [(i + 1, i) for i in range(7)]
    packed = jnp.stack([tiles, lax.ppermute(tiles, slab, up), lax.ppermute(tiles, slab, down)])
    every = copies(packed, "grp", GRP)
    own = every[:, 0].reshape(-1)
    near = jnp.concatenate([every[: GRP // 4, 2].reshape(-1), every[3 * GRP // 4 :, 1].reshape(-1)])

    mid, rim, to_up, to_down = smooth(own, near, jnp.transpose(raw_frames, (1, 0, 2)))
    from_low = lax.ppermute(to_up, slab, up)
    from_high = lax.ppermute(to_down, slab, down)
    quarter = GRP // 4
    low = (rim[:quarter] + from_low).astype(bf16)
    high = (rim[quarter:] + from_high).astype(bf16)
    regrouped = lax.all_to_all(jnp.concatenate([low, mid, high]), "grp", 0, 0, tiled=True)

    across = (((1,), (1,)), ((), ()))
    col_starts = window_starts(150, 8, 160, K)
    starts = jnp.array(col_starts, jnp.int32)

    def some_rows(which):
        return jnp.concatenate(
            [lax.dynamic_slice_in_dim(subspace, starts[2 * x + which], 160, 0) for x in range(4)]
        )

    other_ss = lax.dot_general(some_rows(1 - core), subspace, across, preferred_element_type=f32).astype(bf16)
    got_ss = lax.ppermute(other_ss, "core", swap)
    own_ss = lax.dot_general(some_rows(core), subspace, across, preferred_element_type=f32)
    pair_ss = (own_ss + got_ss.astype(f32)).astype(bf16).reshape(4, 160, K)
    slab_ss = jnp.sum(lax.all_to_all(pair_ss, "x", 0, 0, tiled=True).astype(f32), axis=0)
    row_starts = window_starts(ROWS, GRP, WIN, KX + 0)
    tall = jnp.pad(slab_ss.astype(bf16).T, ((0, KX - K), (0, 0)))
    by_row = jnp.stack([tall[a : a + WIN] for a in row_starts])
    grp_ss = jnp.sum(lax.all_to_all(by_row, "grp", 0, 0, tiled=True).astype(f32), axis=0).astype(bf16)
    all_ss = copies(grp_ss, slab, 8)
    rows_ss = jnp.concatenate(
        [all_ss[p][:, 150 * p - col_starts[p] : 150 * p - col_starts[p] + 150] for p in range(8)], axis=1
    )

    contract = (((0,), (0,)), ((), ()))
    from_basis = lax.dot_general(rotation[:K], subspace, contract, preferred_element_type=f32)

    halves = regrouped.astype(f32).reshape(2, SUBJ, per_device)
    centered = (halves - jnp.mean(halves, axis=1, keepdims=True)).astype(bf16)
    wide = centered.astype(f32)
    partial_power = jnp.sum(wide * wide, axis=(1, 2))
    power = jnp.sum(copies(partial_power[None], ("x", "core", "grp"), 8 * GRP), axis=(0, 1))
    scales = lax.rsqrt(power / (masked * SUBJ) + epsilon)

    def data_columns(which):
        mine = lax.dynamic_index_in_dim(centered, which, 0, keepdims=False)
        return jnp.concatenate(
            [
                lax.dot_general(subspace, mine, across, preferred_element_type=f32),
                lax.dot_general(centered.reshape(2 * SUBJ, per_device), mine, across, preferred_element_type=f32),
            ]
        )

    got_c = lax.ppermute(data_columns(1 - core).astype(bf16), "core", swap)
    pair_c = (data_columns(core) + got_c.astype(f32)).astype(bf16)
    by_row_c = jnp.stack([pair_c[a : a + WIN] for a in row_starts])
    grp_c = jnp.sum(lax.all_to_all(by_row_c, "grp", 0, 0, tiled=True).astype(f32), axis=0).astype(bf16)
    all_c = copies(grp_c, slab, 8).astype(f32).reshape(4, 2, WIN, SUBJ)
    sum_c = jnp.sum(all_c, axis=0)
    first_row = grp * ROWS
    offset = first_row - jnp.array(row_starts, jnp.int32)[grp]
    rows_c = lax.dynamic_slice_in_dim(jnp.concatenate([sum_c[0], sum_c[1]], axis=1), offset, ROWS, 0)

    first_data = K // ROWS
    data_devices = GRP - first_data
    wanted = np.zeros((data_devices, ROWS, 2 * SUBJ), np.float32)
    for d in range(data_devices):
        for i in range(ROWS):
            at = (first_data + d) * ROWS + i - K
            if at >= 0:
                wanted[d, i, at] = 1.0
    turned = lax.dot_general(
        jnp.asarray(wanted).astype(bf16), rows_c.astype(bf16), (((2,), (1,)), ((), ())), preferred_element_type=f32
    ).astype(bf16)
    turned = jnp.concatenate([jnp.zeros((first_data, ROWS, ROWS), bf16), turned])
    back = lax.all_to_all(turned, "grp", 0, 0, tiled=True)
    rows_t = jnp.transpose(back[: first_data + 1], (1, 0, 2)).reshape(ROWS, (first_data + 1) * ROWS)[:, :K]
    rows_ss = lax.dynamic_slice_in_dim(rows_ss, offset, ROWS, 0)
    row_number = first_row + lax.broadcasted_iota(jnp.int32, (ROWS, 1), 0)
    left = jnp.where(row_number < K, rows_ss.astype(f32), rows_t.astype(f32))
    owned = jnp.concatenate([left, rows_c], axis=1)

    row_scale = jnp.concatenate([jnp.ones((K,), f32), jnp.repeat(scales, SUBJ)])
    owned_scale = lax.dynamic_slice_in_dim(row_scale, first_row, ROWS, 0)
    gram_rows = owned * (owned_scale[:, None] * row_scale[None, :]) / masked

    from_first = lax.dot_general(rotation[K : K + SUBJ], centered[0], contract, preferred_element_type=f32)
    from_second = lax.dot_general(rotation[K + SUBJ :], centered[1], contract, preferred_element_type=f32)
    new_subspace = (from_basis + scales[0] * from_first + scales[1] * from_second).astype(bf16)
    return (gram_rows, new_subspace)


def solution(mesh):
    fine = Mesh(mesh.devices.reshape(4, 2, GRP), ("x", "core", "grp"))
    slab = ("x", "core")
    placed = (P("grp", slab, None), P((*slab, "grp")), P(None, (*slab, "grp")), P())
    return jax.shard_map(
        body,
        mesh=fine,
        in_specs=placed,
        out_specs=(P("grp", None), P(None, (*slab, "grp"))),
        check_vma=False,
    )
```

```python
import functools
import math

import jax
import jax.numpy as jnp
import numpy as np
from jax import lax
from jax.experimental import pallas as pl
from jax.experimental.pallas import tpu as pltpu
from jax.sharding import Mesh
from jax.sharding import PartitionSpec as P

NX = 96
RUN = 128
RAD = 3
K = 1200
KX = 1712
SUBJ = 256
ROWS = 107
WIN = 120
TALL = 128
PART = 150
WIDE = 176
LEAD = 384
BLOCK = 256
PHASES = 3
GRP = 16
TAB = 64
TAB_MID = 31

smooth_sigma = 1.0617
epsilon = 1e-06


def tap_weights():
    unscaled = [
        math.exp(-offset * offset / (2.0 * smooth_sigma * smooth_sigma))
        for offset in range(-RAD, RAD + 1)
    ]
    summed = sum(unscaled)
    return [weight / summed for weight in unscaled]


def plane_matrix():
    taps = np.array(tap_weights())
    cells_in = np.arange(LEAD + BLOCK + LEAD)[:, None]
    cells_out = np.arange(BLOCK)[None, :]
    parts = []
    for phase in range(PHASES):
        column = (phase * BLOCK + cells_out) % NX
        reach = cells_in - LEAD - cells_out
        rows = np.floor((reach + NX // 2) / NX).astype(np.int64)
        along = reach - rows * NX
        ok = (np.abs(rows) <= RAD) & (np.abs(along) <= RAD) & (column + along >= 0) & (column + along < NX)
        weight = taps[np.clip(rows + RAD, 0, 2 * RAD)] * taps[np.clip(along + RAD, 0, 2 * RAD)]
        parts.append(np.where(ok, weight, 0.0))
    return np.stack(parts).astype(np.float32)


def depth_table():
    table = np.zeros((TAB,), np.float32)
    table[TAB_MID - RAD : TAB_MID + RAD + 1] = tap_weights()
    return table


def smooth_kernel(depth, own_ref, near_ref, tab_ref, mat_ref, raw_ref, mid_ref, rim_ref, up_ref, down_ref, pad, planar, sems):
    frames = raw_ref.shape[1]
    extent = raw_ref.shape[2]
    step = PHASES * BLOCK
    steps = extent // step
    tiles = extent // RUN

    def fetch(i):
        return pltpu.make_async_copy(
            raw_ref.at[:, :, pl.ds(i * step, step)],
            pad.at[:, :, pl.ds(LEAD + i * step, step)],
            sems.at[i],
        )

    for i in range(steps):
        fetch(i).start()
    edge = jnp.zeros((depth, frames, LEAD), pad.dtype)
    pad[:, :, :LEAD] = edge
    pad[:, :, LEAD + extent :] = edge
    fetch(0).wait()

    def block(i, carry):
        @pl.when(i + 1 < steps)
        def _():
            fetch(i + 1).wait()

        for phase in range(PHASES):
            start = pl.multiple_of(i * step + phase * BLOCK, BLOCK)
            cells = pad[:, :, pl.ds(start, LEAD + BLOCK + LEAD)].reshape(depth * frames, LEAD + BLOCK + LEAD)
            out = jnp.dot(cells, mat_ref[phase], preferred_element_type=jnp.float32)
            planar[:, :, pl.ds(start, BLOCK)] = out.reshape(depth, frames, BLOCK)
        return carry

    lax.fori_loop(0, steps, block, 0)

    taps = tap_weights()

    def place(tile):
        plane = tile // tiles
        return plane, pl.multiple_of((tile - plane * tiles) * RUN, RUN)

    per = mid_ref.shape[2] // RUN

    def middle(g, carry):
        for j in range(per):
            plane, lane = place(own_ref[(g + GRP // 4) * per + j])
            total = taps[0] * planar[plane - RAD, :, pl.ds(lane, RUN)]
            for k in range(1, 2 * RAD + 1):
                total = total + taps[k] * planar[plane - RAD + k, :, pl.ds(lane, RUN)]
            mid_ref[g, :, j * RUN : (j + 1) * RUN] = total.astype(mid_ref.dtype)
        return carry

    def some(tile, first, count, shift):
        plane, lane = place(tile)
        total = None
        for q in range(first, first + count):
            weight = tab_ref[q - plane + shift + TAB_MID]
            term = weight * planar[q, :, pl.ds(lane, RUN)]
            total = term if total is None else total + term
        return total

    def rims(g, carry):
        for j in range(per):
            cols = slice(j * RUN, (j + 1) * RUN)
            at = g * per + j
            up_ref[g, :, cols] = some(near_ref[at], depth - RAD, RAD, -depth)
            down_ref[g, :, cols] = some(near_ref[GRP // 4 * per + at], 0, RAD, depth)
            rim_ref[g, :, cols] = some(own_ref[at], 0, 2 * RAD, 0)
            rim_ref[GRP // 4 + g, :, cols] = some(own_ref[GRP * 3 // 4 * per + at], depth - 2 * RAD, 2 * RAD, 0)
        return carry

    lax.fori_loop(0, GRP // 4, rims, 0)
    lax.fori_loop(0, GRP // 2, middle, 0)


def smooth(own, near, raw):
    depth, frames, extent = raw.shape
    per_device = own.shape[0] // GRP * RUN
    smem = pl.BlockSpec(memory_space=pltpu.SMEM)
    vmem = pl.BlockSpec(memory_space=pltpu.VMEM)
    quarter = (GRP // 4, frames, per_device)
    half = (GRP // 2, frames, per_device)
    return pl.pallas_call(
        functools.partial(smooth_kernel, depth),
        out_shape=[
            jax.ShapeDtypeStruct(half, jnp.bfloat16),
            jax.ShapeDtypeStruct(half, jnp.float32),
            jax.ShapeDtypeStruct(quarter, jnp.float32),
            jax.ShapeDtypeStruct(quarter, jnp.float32),
        ],
        in_specs=[smem, smem, smem, vmem, pl.BlockSpec(memory_space=pl.ANY)],
        out_specs=[vmem] * 4,
        scratch_shapes=[
            pltpu.VMEM((depth, frames, extent + 2 * LEAD), jnp.bfloat16),
            pltpu.VMEM((depth, frames, extent), jnp.float32),
            pltpu.SemaphoreType.DMA((extent // (PHASES * BLOCK),)),
        ],
        compiler_params=pltpu.CompilerParams(vmem_limit_bytes=48 * 1024 * 1024),
        name="smooth",
    )(own, near, jnp.asarray(depth_table()), jnp.asarray(plane_matrix()).astype(jnp.bfloat16), raw)


NT = (((1,), (1,)), ((), ()))


def row_start(first):
    return min(first // 8 * 8, KX - WIN) if isinstance(first, int) else jnp.minimum(first // 8 * 8, KX - WIN)


def part_start(part):
    return jnp.minimum(part * PART // 16 * 16, K - WIDE)


def vmem(count):
    return [pl.BlockSpec(memory_space=pltpu.VMEM)] * count


def smem():
    return pl.BlockSpec(memory_space=pltpu.SMEM)


def params(mib):
    return pltpu.CompilerParams(vmem_limit_bytes=mib * 1024 * 1024)


def gather_parts(x, which, sub_ref, left):
    for k in range(4):
        start = pl.multiple_of(part_start((x + k) % 4 * 2 + which), 16)
        left[k * WIDE : (k + 1) * WIDE, :] = sub_ref[pl.ds(start, WIDE), :]


def basis_other_kernel(at_ref, sub_ref, out_ref, left):
    gather_parts(at_ref[0], 1 - at_ref[1], sub_ref, left)
    out_ref[...] = lax.dot_general(left[...], sub_ref[...], NT, preferred_element_type=jnp.float32).astype(out_ref.dtype)


def basis_own_kernel(at_ref, sub_ref, got_ref, *refs):
    left = refs[-1]
    gather_parts(at_ref[0], at_ref[1], sub_ref, left)
    for k in range(4):
        rows = slice(k * WIDE, (k + 1) * WIDE)
        made = lax.dot_general(left[rows, :], sub_ref[...], NT, preferred_element_type=jnp.float32)
        refs[k][...] = (made + got_ref[rows, :].astype(jnp.float32)).astype(refs[k].dtype)


def basis_rows_kernel(a_ref, b_ref, c_ref, d_ref, out_ref, flat):
    flat[...] = jnp.zeros_like(flat)
    total = a_ref[...].astype(jnp.float32) + b_ref[...].astype(jnp.float32)
    flat[:WIDE, :K] = total + c_ref[...].astype(jnp.float32) + d_ref[...].astype(jnp.float32)
    turned = flat[...].T
    for g in range(GRP):
        first = row_start(g * ROWS)
        if first + WIN <= turned.shape[0]:
            out_ref[g] = turned[first : first + WIN, :WIDE].astype(out_ref.dtype)
        else:
            out_ref[g] = jnp.zeros((WIN, WIDE), out_ref.dtype)


def columns_kernel(at_ref, got_ref, sub_ref, cen_ref, other_ref, own_ref, power_ref):
    per_device = sub_ref.shape[1]
    core = at_ref[1]
    each = GRP // 2

    def centre(i, sums):
        cols = pl.ds(pl.multiple_of(i * RUN, RUN), RUN)
        new = []
        for s in range(2):
            wide = got_ref[s * each : (s + 1) * each, :, cols].reshape(SUBJ, RUN).astype(jnp.float32)
            mean = jnp.sum(wide, axis=0, keepdims=True) * (1.0 / SUBJ)
            cen = (wide - mean).astype(cen_ref.dtype)
            cen_ref[s, :, cols] = cen
            back = cen.astype(jnp.float32)
            new.append(sums[s] + jnp.sum((back * back).reshape(SUBJ // 8, 8, RUN), axis=0))
        return tuple(new)

    zero = jnp.zeros((8, RUN), jnp.float32)
    sums = lax.fori_loop(0, per_device // RUN, centre, (zero, zero))
    line = lax.broadcasted_iota(jnp.int32, (8, RUN), 0)
    first = jnp.sum(sums[0], keepdims=True)
    second = jnp.sum(sums[1], keepdims=True)
    power_ref[...] = jnp.where(line == 0, first, jnp.where(line == 1, second, 0.0))

    for which, out in ((1 - core, other_ref), (core, own_ref)):
        right = cen_ref[which]
        for lo in range(0, K, 400):
            out[lo : lo + 400, :] = lax.dot_general(
                sub_ref[lo : lo + 400, :], right, NT, preferred_element_type=jnp.float32
            ).astype(out.dtype)
        for s in range(2):
            lo = K + s * SUBJ
            out[lo : lo + SUBJ, :] = lax.dot_general(
                cen_ref[s], right, NT, preferred_element_type=jnp.float32
            ).astype(out.dtype)


def write_power(power, out_ref, at):
    high = power.astype(jnp.bfloat16)
    low = (power - high.astype(jnp.float32)).astype(jnp.bfloat16)
    out_ref[at, WIN:, :RUN] = high
    out_ref[at, WIN:, RUN:] = low


def windows_kernel(own_ref, got_ref, power_ref, out_ref, whole):
    whole[...] = own_ref[...] + got_ref[...].astype(jnp.float32)
    for g in range(GRP):
        first = row_start(g * ROWS)
        out_ref[g, :WIN, :] = whole[first : first + WIN, :].astype(out_ref.dtype)
        write_power(power_ref[...], out_ref, g)


def total_kernel(got_ref, out_ref):
    total = got_ref[0].astype(jnp.float32)
    for g in range(1, GRP):
        total = total + got_ref[g].astype(jnp.float32)
    power = total[WIN:, :RUN] + total[WIN:, RUN:]
    rows = total[:WIN].astype(out_ref.dtype)
    for p in range(8):
        out_ref[p, :WIN, :] = rows
        write_power(power, out_ref, p)


def finish_kernel(count, at_ref, got_ref, rows_ref, scale_ref, turned_ref):
    halves = []
    power = jnp.zeros((8, RUN), jnp.float32)
    for c in range(2):
        total = got_ref[c].astype(jnp.float32)
        for x in range(1, 4):
            total = total + got_ref[2 * x + c].astype(jnp.float32)
        power = power + total[WIN:, :RUN] + total[WIN:, RUN:]
        halves.append(total)
    scale_ref[...] = lax.rsqrt(power / count + epsilon)
    first = at_ref[2] * ROWS
    shift = (TALL - (first - row_start(first))) % TALL
    rows = pltpu.roll(jnp.concatenate(halves, axis=1), shift, 0)
    rows_ref[...] = rows
    narrow = rows.astype(jnp.bfloat16)
    turned_ref[: K // ROWS] = jnp.zeros((K // ROWS, TALL, TALL), turned_ref.dtype)
    line = lax.broadcasted_iota(jnp.int32, (TALL, 2 * SUBJ), 0)
    lane = lax.broadcasted_iota(jnp.int32, (TALL, 2 * SUBJ), 1)
    for g in range(K // ROWS, GRP):
        pick = jnp.where(line + (g * ROWS - K) == lane, 1.0, 0.0).astype(jnp.bfloat16)
        turned_ref[g] = lax.dot_general(pick, narrow, NT, preferred_element_type=jnp.float32).astype(turned_ref.dtype)


def assemble_kernel(masked, at_ref, back_ref, rows_ref, scale_ref, *refs):
    out_ref, basis, cross = refs[-3:]
    x, core, grp = at_ref[0], at_ref[1], at_ref[2]
    first = grp * ROWS
    basis[...] = jnp.zeros_like(basis)
    cross[...] = jnp.zeros_like(cross)
    line = lax.broadcasted_iota(jnp.int32, (WIDE, 384), 0)
    lane = lax.broadcasted_iota(jnp.int32, (WIDE, 384), 1)
    for k in range(4):
        for c in range(2):
            part = (x - k + 4) % 4 * 2 + (core if c == 0 else 1 - core)
            begin = part * PART // RUN * RUN
            cell = line + (part_start(part) - begin)
            ok = (cell == lane) & (cell >= part * PART - begin) & (cell < part * PART - begin + PART)
            put = jnp.where(ok, 1.0, 0.0).astype(jnp.bfloat16)
            cols = pl.ds(pl.multiple_of(begin, RUN), 384)
            basis[:WIN, cols] += jnp.dot(refs[k][c], put, preferred_element_type=jnp.float32)
    line = lax.broadcasted_iota(jnp.int32, (TALL, 256), 0)
    lane = lax.broadcasted_iota(jnp.int32, (TALL, 256), 1)
    for g in range(K // ROWS + 1):
        begin = g * ROWS // RUN * RUN
        ok = (line + (g * ROWS - begin) == lane) & (line < ROWS) & (line + g * ROWS < K)
        put = jnp.where(ok, 1.0, 0.0).astype(jnp.bfloat16)
        cross[:, begin : begin + 256] += jnp.dot(back_ref[g], put, preferred_element_type=jnp.float32)
    shift = (TALL - (first - row_start(first))) % TALL
    width = 1792
    row = first + lax.broadcasted_iota(jnp.int32, (TALL, 1), 0)
    left = jnp.where(row < K, pltpu.roll(basis[...], shift, 0), cross[...])
    base = K // RUN * RUN
    right = pltpu.roll(
        jnp.concatenate([rows_ref[...], jnp.zeros((TALL, RUN), jnp.float32)], axis=1), K - base, 1
    )
    zero, one = scale_ref[0:1, 0:1], scale_ref[1:2, 0:1]
    of_row = jnp.where(row < K, 1.0, jnp.where(row < K + SUBJ, zero, one))
    col = lax.broadcasted_iota(jnp.int32, (1, width), 1)
    of_col = jnp.where(col < K, 1.0, jnp.where(col < K + SUBJ, zero, one))
    out_ref[:, :base] = (left[:, :base] * (of_row * of_col[:, :base]) / masked)[:ROWS]
    edge = jnp.concatenate([left[:, base:], jnp.zeros((TALL, width - left.shape[1]), jnp.float32)], axis=1)
    values = jnp.where(col[:, base:] < K, edge, right)
    out_ref[:, base:] = (values * (of_row * of_col[:, base:]) / masked)[:ROWS, : KX - base]


def rotate_kernel(scale_ref, base_ref, turn_ref, cen_ref, out_ref):
    first = jnp.dot(turn_ref[:, :SUBJ], cen_ref[0], preferred_element_type=jnp.float32)
    second = jnp.dot(turn_ref[:, SUBJ:], cen_ref[1], preferred_element_type=jnp.float32)
    out_ref[...] = (base_ref[...] + scale_ref[0:1, 0:1] * first + scale_ref[1:2, 0:1] * second).astype(out_ref.dtype)


def copies(value, axis, count):
    return lax.all_to_all(jnp.broadcast_to(value[None], (count, *value.shape)), axis, 0, 0, tiled=True)


def body(raw_frames, mask_index, subspace, rotation):
    depth = raw_frames.shape[1]
    extent = raw_frames.shape[2]
    per_device = subspace.shape[1]
    slab = ("x", "core")
    masked = per_device * 8 * GRP
    bf16 = jnp.bfloat16
    f32 = jnp.float32
    like = jax.ShapeDtypeStruct
    swap = [(0, 1), (1, 0)]
    turns = [[(i, (i + k) % 4) for i in range(4)] for k in range(4)]
    at = jnp.stack([lax.axis_index("x"), lax.axis_index("core"), lax.axis_index("grp")]).astype(jnp.int32)

    slab_at = lax.axis_index("x") * 2 + lax.axis_index("core")
    tiles = mask_index.reshape(-1, RUN)[:, 0] // RUN - slab_at * (depth * extent // RUN)
    up = [(i, i + 1) for i in range(7)]
    down = [(i + 1, i) for i in range(7)]
    packed = jnp.stack([tiles, lax.ppermute(tiles, slab, up), lax.ppermute(tiles, slab, down)])
    every = copies(packed, "grp", GRP)
    own = every[:, 0].reshape(-1)
    near = jnp.concatenate([every[: GRP // 4, 2].reshape(-1), every[3 * GRP // 4 :, 1].reshape(-1)])

    mid, rim, to_up, to_down = smooth(own, near, jnp.transpose(raw_frames, (1, 0, 2)))
    from_low = lax.ppermute(to_up, slab, up)
    from_high = lax.ppermute(to_down, slab, down)
    quarter = GRP // 4
    low = (rim[:quarter] + from_low).astype(bf16)
    high = (rim[quarter:] + from_high).astype(bf16)
    placed = jnp.concatenate([low, mid, high])
    regrouped = lax.all_to_all(placed, "grp", 0, 0, tiled=True)

    at_ss, _ = lax.optimization_barrier((at, to_down))
    left = pltpu.VMEM((4 * WIDE, per_device), bf16)
    other_ss = pl.pallas_call(
        basis_other_kernel,
        out_shape=like((4 * WIDE, K), bf16),
        in_specs=[smem(), *vmem(1)],
        out_specs=vmem(1)[0],
        scratch_shapes=[left],
        compiler_params=params(24),
        name="basis_other",
    )(at_ss, subspace)
    got_ss = lax.ppermute(other_ss, "core", swap)
    parts = pl.pallas_call(
        basis_own_kernel,
        out_shape=[like((WIDE, K), bf16)] * 4,
        in_specs=[smem(), *vmem(2)],
        out_specs=vmem(4),
        scratch_shapes=[left],
        compiler_params=params(24),
        name="basis_own",
    )(at_ss, subspace, got_ss)
    parts = [parts[0]] + [lax.ppermute(parts[k], "x", turns[k]) for k in range(1, 4)]
    by_row = pl.pallas_call(
        basis_rows_kernel,
        out_shape=like((GRP, WIN, WIDE), bf16),
        in_specs=vmem(4),
        out_specs=vmem(1)[0],
        scratch_shapes=[pltpu.VMEM((256, 1408), f32)],
        compiler_params=params(16),
        name="basis_rows",
    )(*parts)
    grp_ss = jnp.sum(lax.all_to_all(by_row, "grp", 0, 0, tiled=True).astype(f32), axis=0).astype(bf16)
    pair_ss = jnp.stack([grp_ss, lax.ppermute(grp_ss, "core", swap)])
    all_ss = [pair_ss] + [lax.ppermute(pair_ss, "x", turns[k]) for k in range(1, 4)]

    rotation_b, _ = lax.optimization_barrier((rotation, placed))
    contract = (((0,), (0,)), ((), ()))
    from_basis = lax.optimization_barrier(
        lax.dot_general(rotation_b[:K], subspace, contract, preferred_element_type=f32)
    )
    turn = lax.optimization_barrier(rotation_b[K:].T)

    centered, other_c, own_c, power = pl.pallas_call(
        columns_kernel,
        out_shape=[like((2, SUBJ, per_device), bf16), like((KX, SUBJ), bf16), like((KX, SUBJ), f32), like((8, RUN), f32)],
        in_specs=[smem(), *vmem(2)],
        out_specs=vmem(4),
        compiler_params=params(24),
        name="columns",
    )(at, regrouped, subspace)
    got_c = lax.ppermute(other_c, "core", swap)
    by_row_c = pl.pallas_call(
        windows_kernel,
        out_shape=like((GRP, TALL, SUBJ), bf16),
        in_specs=vmem(3),
        out_specs=vmem(1)[0],
        scratch_shapes=[pltpu.VMEM((KX, SUBJ), f32)],
        compiler_params=params(16),
        name="windows",
    )(own_c, got_c, power)
    sum_c = pl.pallas_call(
        total_kernel,
        out_shape=like((8, TALL, SUBJ), bf16),
        in_specs=vmem(1),
        out_specs=vmem(1)[0],
        compiler_params=params(16),
        name="total",
    )(lax.all_to_all(by_row_c, "grp", 0, 0, tiled=True))
    rows_c, scales, turned = pl.pallas_call(
        functools.partial(finish_kernel, float(masked * SUBJ)),
        out_shape=[like((TALL, 2 * SUBJ), f32), like((8, RUN), f32), like((GRP, TALL, TALL), bf16)],
        in_specs=[smem(), *vmem(1)],
        out_specs=vmem(3),
        compiler_params=params(16),
        name="finish",
    )(at, lax.all_to_all(sum_c, slab, 0, 0, tiled=True))

    back = lax.all_to_all(turned, "grp", 0, 0, tiled=True)
    gram_rows = pl.pallas_call(
        functools.partial(assemble_kernel, float(masked)),
        out_shape=like((ROWS, KX), f32),
        in_specs=[smem(), *vmem(7)],
        out_specs=vmem(1)[0],
        scratch_shapes=[pltpu.VMEM((TALL, 1408), f32), pltpu.VMEM((TALL, 1408), f32)],
        compiler_params=params(16),
        name="assemble",
    )(at, back, rows_c, scales, *all_ss)

    tile = 256
    new_subspace = pl.pallas_call(
        rotate_kernel,
        out_shape=like((K, per_device), bf16),
        grid=(per_device // tile,),
        in_specs=[
            pl.BlockSpec((8, RUN), lambda i: (0, 0)),
            pl.BlockSpec((K, tile), lambda i: (0, i)),
            pl.BlockSpec((K, 2 * SUBJ), lambda i: (0, 0)),
            pl.BlockSpec((2, SUBJ, tile), lambda i: (0, 0, i)),
        ],
        out_specs=pl.BlockSpec((K, tile), lambda i: (0, i)),
        compiler_params=params(24),
        name="rotate",
    )(scales, from_basis, turn, centered)
    return (gram_rows, new_subspace)


def solution(mesh):
    fine = Mesh(mesh.devices.reshape(4, 2, GRP), ("x", "core", "grp"))
    slab = ("x", "core")
    placed = (P("grp", slab, None), P((*slab, "grp")), P(None, (*slab, "grp")), P())
    return jax.shard_map(
        body,
        mesh=fine,
        in_specs=placed,
        out_specs=(P("grp", None), P(None, (*slab, "grp"))),
        check_vma=False,
    )
```

```python
import functools
import math

import jax
import jax.numpy as jnp
import numpy as np
from jax import lax
from jax.experimental import pallas as pl
from jax.experimental.pallas import tpu as pltpu
from jax.sharding import Mesh
from jax.sharding import PartitionSpec as P

NX = 96
RUN = 128
RAD = 3
K = 1200
KX = 1712
SUBJ = 256
ROWS = 107
WIN = 120
TALL = 128
PART = 150
WIDE = 176
SHARE = 152
LEAD = 384
BLOCK = 256
PHASES = 3
GRP = 16
TAB = 64
TAB_MID = 31

smooth_sigma = 1.0617
epsilon = 1e-06


def tap_weights():
    unscaled = [
        math.exp(-offset * offset / (2.0 * smooth_sigma * smooth_sigma))
        for offset in range(-RAD, RAD + 1)
    ]
    summed = sum(unscaled)
    return [weight / summed for weight in unscaled]


def plane_matrix():
    taps = np.array(tap_weights())
    cells_in = np.arange(LEAD + BLOCK + LEAD)[:, None]
    cells_out = np.arange(BLOCK)[None, :]
    parts = []
    for phase in range(PHASES):
        column = (phase * BLOCK + cells_out) % NX
        reach = cells_in - LEAD - cells_out
        rows = np.floor((reach + NX // 2) / NX).astype(np.int64)
        along = reach - rows * NX
        ok = (np.abs(rows) <= RAD) & (np.abs(along) <= RAD) & (column + along >= 0) & (column + along < NX)
        weight = taps[np.clip(rows + RAD, 0, 2 * RAD)] * taps[np.clip(along + RAD, 0, 2 * RAD)]
        parts.append(np.where(ok, weight, 0.0))
    return np.stack(parts).astype(np.float32)


def depth_table():
    table = np.zeros((TAB,), np.float32)
    table[TAB_MID - RAD : TAB_MID + RAD + 1] = tap_weights()
    return table


def smooth_kernel(depth, own_ref, near_ref, tab_ref, mat_ref, raw_ref, all_ref, rim_ref, up_ref, down_ref, pad, planar, mid_ref, sems, mid_sem):
    frames = raw_ref.shape[1]
    extent = raw_ref.shape[2]
    step = PHASES * BLOCK
    steps = extent // step
    tiles = extent // RUN

    def fetch(i):
        return pltpu.make_async_copy(
            raw_ref.at[:, :, pl.ds(i * step, step)],
            pad.at[:, :, pl.ds(LEAD + i * step, step)],
            sems.at[i],
        )

    for i in range(steps):
        fetch(i).start()
    edge = jnp.zeros((depth, frames, LEAD), pad.dtype)
    pad[:, :, :LEAD] = edge
    pad[:, :, LEAD + extent :] = edge
    fetch(0).wait()

    def block(i, carry):
        @pl.when(i + 1 < steps)
        def _():
            fetch(i + 1).wait()

        for phase in range(PHASES):
            start = pl.multiple_of(i * step + phase * BLOCK, BLOCK)
            cells = pad[:, :, pl.ds(start, LEAD + BLOCK + LEAD)].reshape(depth * frames, LEAD + BLOCK + LEAD)
            out = jnp.dot(cells, mat_ref[phase], preferred_element_type=jnp.float32)
            planar[:, :, pl.ds(start, BLOCK)] = out.reshape(depth, frames, BLOCK)
        return carry

    lax.fori_loop(0, steps, block, 0)

    taps = tap_weights()

    def place(tile):
        plane = tile // tiles
        return plane, pl.multiple_of((tile - plane * tiles) * RUN, RUN)

    per = mid_ref.shape[2] // RUN

    def middle(g, carry):
        for j in range(per):
            plane, lane = place(own_ref[(g + GRP // 4) * per + j])
            total = taps[0] * planar[plane - RAD, :, pl.ds(lane, RUN)]
            for k in range(1, 2 * RAD + 1):
                total = total + taps[k] * planar[plane - RAD + k, :, pl.ds(lane, RUN)]
            mid_ref[g, :, j * RUN : (j + 1) * RUN] = total.astype(mid_ref.dtype)
        return carry

    def some(tile, first, count, shift):
        plane, lane = place(tile)
        total = None
        for q in range(first, first + count):
            weight = tab_ref[q - plane + shift + TAB_MID]
            term = weight * planar[q, :, pl.ds(lane, RUN)]
            total = term if total is None else total + term
        return total

    def rims(g, carry):
        for j in range(per):
            cols = slice(j * RUN, (j + 1) * RUN)
            at = g * per + j
            up_ref[g, :, cols] = some(near_ref[at], depth - RAD, RAD, -depth).astype(up_ref.dtype)
            down_ref[g, :, cols] = some(near_ref[GRP // 4 * per + at], 0, RAD, depth).astype(down_ref.dtype)
            rim_ref[g, :, cols] = some(own_ref[at], 0, 2 * RAD, 0)
            rim_ref[GRP // 4 + g, :, cols] = some(own_ref[GRP * 3 // 4 * per + at], depth - 2 * RAD, 2 * RAD, 0)
        return carry

    lax.fori_loop(0, GRP // 2, middle, 0)
    keep = pltpu.make_async_copy(mid_ref, all_ref.at[GRP // 4 : GRP * 3 // 4], mid_sem)
    keep.start()
    lax.fori_loop(0, GRP // 4, rims, 0)
    keep.wait()


def smooth(own, near, raw):
    depth, frames, extent = raw.shape
    per_device = own.shape[0] // GRP * RUN
    smem = pl.BlockSpec(memory_space=pltpu.SMEM)
    vmem = pl.BlockSpec(memory_space=pltpu.VMEM)
    quarter = (GRP // 4, frames, per_device)
    half = (GRP // 2, frames, per_device)
    return pl.pallas_call(
        functools.partial(smooth_kernel, depth),
        out_shape=[
            jax.ShapeDtypeStruct((GRP, frames, per_device), jnp.bfloat16),
            jax.ShapeDtypeStruct(half, jnp.float32),
            jax.ShapeDtypeStruct(quarter, jnp.bfloat16),
            jax.ShapeDtypeStruct(quarter, jnp.bfloat16),
        ],
        in_specs=[smem, smem, smem, vmem, pl.BlockSpec(memory_space=pl.ANY)],
        out_specs=[pl.BlockSpec(memory_space=pltpu.HBM), vmem, vmem, vmem],
        scratch_shapes=[
            pltpu.VMEM((depth, frames, extent + 2 * LEAD), jnp.bfloat16),
            pltpu.VMEM((depth, frames, extent), jnp.float32),
            pltpu.VMEM(half, jnp.bfloat16),
            pltpu.SemaphoreType.DMA((extent // (PHASES * BLOCK),)),
            pltpu.SemaphoreType.DMA,
        ],
        compiler_params=pltpu.CompilerParams(vmem_limit_bytes=48 * 1024 * 1024),
        name="smooth",
    )(own, near, jnp.asarray(depth_table()), jnp.asarray(plane_matrix()).astype(jnp.bfloat16), raw)


NT = (((1,), (1,)), ((), ()))


def row_start(first):
    return min(first // 8 * 8, KX - WIN) if isinstance(first, int) else jnp.minimum(first // 8 * 8, KX - WIN)


def part_start(part):
    return jnp.minimum(part * PART // 16 * 16, K - WIDE)


def vmem(count):
    return [pl.BlockSpec(memory_space=pltpu.VMEM)] * count


def smem():
    return pl.BlockSpec(memory_space=pltpu.SMEM)


def params(mib):
    return pltpu.CompilerParams(vmem_limit_bytes=mib * 1024 * 1024)


def hbm():
    return pl.BlockSpec(memory_space=pltpu.HBM)


PIECE = 400
PIECES = K // PIECE


def basis_copies(x, which, sub_ref, left, right, sems):
    made = []
    for k in range(4):
        start = pl.multiple_of(part_start((x + k) % 4 * 2 + which), 16)
        made.append(
            pltpu.make_async_copy(sub_ref.at[pl.ds(start, WIDE)], left.at[k * WIDE : (k + 1) * WIDE], sems.at[k])
        )
    for i in range(PIECES):
        rows = slice(i * PIECE, (i + 1) * PIECE)
        made.append(pltpu.make_async_copy(sub_ref.at[rows], right.at[rows], sems.at[4 + i]))
    for copy in made:
        copy.start()
    return made


def basis_other_kernel(at_ref, sub_ref, out_ref, left, right, sems):
    made = basis_copies(at_ref[0], 1 - at_ref[1], sub_ref, left, right, sems)
    for copy in made:
        copy.wait()
    out_ref[...] = lax.dot_general(left[...], right[...], NT, preferred_element_type=jnp.float32).astype(out_ref.dtype)


def basis_own_kernel(at_ref, sub_ref, got_ref, *refs):
    left, right, sems = refs[-3:]
    made = basis_copies(at_ref[0], at_ref[1], sub_ref, left, right, sems)
    for copy in made:
        copy.wait()
    for k in range(4):
        rows = slice(k * WIDE, (k + 1) * WIDE)
        part = lax.dot_general(left[rows, :], right[...], NT, preferred_element_type=jnp.float32)
        refs[k][...] = (part + got_ref[rows, :].astype(jnp.float32)).astype(refs[k].dtype)


def basis_rows_kernel(at_ref, a_ref, b_ref, c_ref, d_ref, out_ref, flat):
    part = at_ref[0] * 2 + at_ref[1]
    total = a_ref[...].astype(jnp.float32) + b_ref[...].astype(jnp.float32)
    total = total + c_ref[...].astype(jnp.float32) + d_ref[...].astype(jnp.float32)
    flat[:, K // RUN * RUN :] = jnp.zeros((flat.shape[0], flat.shape[1] - K // RUN * RUN), jnp.float32)
    flat[:, :K] = total
    shift = (WIDE - (part * PART - part_start(part))) % WIDE
    narrow = pltpu.roll(flat[...], shift, 0)[:SHARE].astype(jnp.bfloat16)
    line = lax.broadcasted_iota(jnp.int32, (256, RUN), 0)
    lane = lax.broadcasted_iota(jnp.int32, (256, RUN), 1)
    for g in range(GRP):
        begin = g * ROWS // RUN * RUN
        if g * ROWS < K:
            pick = jnp.where((line == lane + (g * ROWS - begin)) & (lane < ROWS), 1.0, 0.0).astype(jnp.bfloat16)
            out_ref[g] = jnp.dot(narrow[:, begin : begin + 256], pick, preferred_element_type=jnp.float32).astype(
                out_ref.dtype
            )
        else:
            out_ref[g] = jnp.zeros((SHARE, RUN), out_ref.dtype)


def rim_kernel(rim_ref, low_ref, high_ref, all_ref, out_ref, made, sems):
    del all_ref
    quarter = GRP // 4
    made[:quarter] = (rim_ref[:quarter] + low_ref[...].astype(jnp.float32)).astype(made.dtype)
    first = pltpu.make_async_copy(made.at[:quarter], out_ref.at[:quarter], sems.at[0])
    first.start()
    made[quarter:] = (rim_ref[quarter:] + high_ref[...].astype(jnp.float32)).astype(made.dtype)
    second = pltpu.make_async_copy(made.at[quarter:], out_ref.at[3 * quarter :], sems.at[1])
    second.start()
    first.wait()
    second.wait()


def columns_kernel(at_ref, got_ref, basis_ref, cen_out, other_ref, own_out, power_ref, sub_ref, cen_ref, own_ref, sems):
    per_device = sub_ref.shape[1]
    core = at_ref[1]
    each = GRP // 2
    fetch = pltpu.make_async_copy(basis_ref, sub_ref, sems.at[0])
    fetch.start()

    def centre(i, sums):
        cols = pl.ds(pl.multiple_of(i * RUN, RUN), RUN)
        new = []
        for s in range(2):
            wide = got_ref[s * each : (s + 1) * each, :, cols].reshape(SUBJ, RUN).astype(jnp.float32)
            mean = jnp.sum(wide, axis=0, keepdims=True) * (1.0 / SUBJ)
            cen = (wide - mean).astype(cen_ref.dtype)
            cen_ref[s, :, cols] = cen
            back = cen.astype(jnp.float32)
            new.append(sums[s] + jnp.sum((back * back).reshape(SUBJ // 8, 8, RUN), axis=0))
        return tuple(new)

    zero = jnp.zeros((8, RUN), jnp.float32)
    sums = lax.fori_loop(0, per_device // RUN, centre, (zero, zero))
    keep = pltpu.make_async_copy(cen_ref, cen_out, sems.at[1])
    keep.start()
    line = lax.broadcasted_iota(jnp.int32, (8, RUN), 0)
    first = jnp.sum(sums[0], keepdims=True)
    second = jnp.sum(sums[1], keepdims=True)
    power_ref[...] = jnp.where(line == 0, first, jnp.where(line == 1, second, 0.0))

    fetch.wait()
    for which, out in ((core, own_ref), (1 - core, other_ref)):
        right = cen_ref[which]
        for lo in range(0, K, 400):
            out[lo : lo + 400, :] = lax.dot_general(
                sub_ref[lo : lo + 400, :], right, NT, preferred_element_type=jnp.float32
            ).astype(out.dtype)
        for s in range(2):
            lo = K + s * SUBJ
            out[lo : lo + SUBJ, :] = lax.dot_general(
                cen_ref[s], right, NT, preferred_element_type=jnp.float32
            ).astype(out.dtype)
        if out is own_ref:
            leave = pltpu.make_async_copy(own_ref, own_out, sems.at[2])
            leave.start()
    leave.wait()
    keep.wait()


def write_power(power, put):
    high = power.astype(jnp.bfloat16)
    put(slice(WIN, TALL), high)
    put(slice(TALL + WIN, 2 * TALL), (power - high.astype(jnp.float32)).astype(jnp.bfloat16))


def windows_kernel(own_ref, got_ref, power_ref, basis_ref, out_ref, whole, sem):
    fetch = pltpu.make_async_copy(own_ref, whole, sem)
    fetch.start()
    for g in range(GRP):
        out_ref[g, 2 * TALL :, :] = basis_ref[g]

        def put(rows, value, g=g):
            out_ref[g, rows, :] = value

        write_power(power_ref[...], put)
    fetch.wait()
    whole[...] = whole[...] + got_ref[...].astype(jnp.float32)
    for g in range(GRP):
        first = row_start(g * ROWS)
        for half in range(2):
            out_ref[g, half * TALL : half * TALL + WIN, :] = whole[
                first : first + WIN, half * RUN : (half + 1) * RUN
            ].astype(out_ref.dtype)


def total_kernel(got_ref, out_ref):
    total = got_ref[0].astype(jnp.float32)
    for g in range(1, GRP):
        total = total + got_ref[g].astype(jnp.float32)
    out_ref[...] = total.astype(out_ref.dtype)

    def put(rows, value):
        out_ref[rows, :] = value

    write_power(total[WIN:TALL] + total[TALL + WIN : 2 * TALL], put)


def slab_kernel(a_ref, b_ref, c_ref, d_ref, sum_ref, parts_ref):
    refs = (a_ref, b_ref, c_ref, d_ref)
    total = refs[0][: 2 * TALL].astype(jnp.float32)
    for ref in refs[1:]:
        total = total + ref[: 2 * TALL].astype(jnp.float32)
    sum_ref[...] = total
    for k in range(4):
        parts_ref[k] = refs[k][2 * TALL :]


def finish_kernel(count, at_ref, own_ref, got_ref, rows_ref, scale_ref, turned_ref):
    own, got = own_ref[...], got_ref[...]
    both = own + got
    scale_ref[...] = lax.rsqrt((both[WIN:TALL] + both[TALL + WIN :]) / count + epsilon)
    is_first = at_ref[1] == 0
    zero = jnp.where(is_first, own, got)
    one = jnp.where(is_first, got, own)
    rows = jnp.concatenate([zero[:TALL], zero[TALL:], one[:TALL], one[TALL:]], axis=1)
    first = at_ref[2] * ROWS
    shift = (TALL - (first - row_start(first))) % TALL
    rows = pltpu.roll(rows, shift, 0)
    rows_ref[...] = rows
    narrow = rows.astype(jnp.bfloat16)
    turned_ref[: K // ROWS] = jnp.zeros((K // ROWS, TALL, TALL), turned_ref.dtype)
    line = lax.broadcasted_iota(jnp.int32, (TALL, 2 * SUBJ), 0)
    lane = lax.broadcasted_iota(jnp.int32, (TALL, 2 * SUBJ), 1)
    for g in range(K // ROWS, GRP):
        pick = jnp.where(line + (g * ROWS - K) == lane, 1.0, 0.0).astype(jnp.bfloat16)
        turned_ref[g] = lax.dot_general(pick, narrow, NT, preferred_element_type=jnp.float32).astype(turned_ref.dtype)


def assemble_kernel(masked, at_ref, back_ref, rows_ref, scale_ref, own_ref, got_ref, out_ref, basis, cross):
    x, core, grp = at_ref[0], at_ref[1], at_ref[2]
    first = grp * ROWS
    basis[...] = jnp.zeros_like(basis)
    cross[...] = jnp.zeros_like(cross)
    line = lax.broadcasted_iota(jnp.int32, (SHARE, 384), 0)
    lane = lax.broadcasted_iota(jnp.int32, (SHARE, 384), 1)
    for k in range(4):
        for ref, which in ((own_ref, core), (got_ref, 1 - core)):
            part = (x - k + 4) % 4 * 2 + which
            begin = part * PART // RUN * RUN
            put = jnp.where((line + (part * PART - begin) == lane) & (line < PART), 1.0, 0.0).astype(jnp.bfloat16)
            cols = pl.ds(pl.multiple_of(begin, RUN), 384)
            basis[:, cols] += lax.dot_general(
                ref[k], put, (((0,), (0,)), ((), ())), preferred_element_type=jnp.float32
            )
    line = lax.broadcasted_iota(jnp.int32, (TALL, 256), 0)
    lane = lax.broadcasted_iota(jnp.int32, (TALL, 256), 1)
    for g in range(K // ROWS + 1):
        begin = g * ROWS // RUN * RUN
        ok = (line + (g * ROWS - begin) == lane) & (line < ROWS) & (line + g * ROWS < K)
        put = jnp.where(ok, 1.0, 0.0).astype(jnp.bfloat16)
        cross[:, begin : begin + 256] += jnp.dot(back_ref[g], put, preferred_element_type=jnp.float32)
    width = 1792
    row = first + lax.broadcasted_iota(jnp.int32, (TALL, 1), 0)
    left = jnp.where(row < K, basis[...], cross[...])
    base = K // RUN * RUN
    right = pltpu.roll(
        jnp.concatenate([rows_ref[...], jnp.zeros((TALL, RUN), jnp.float32)], axis=1), K - base, 1
    )
    zero, one = scale_ref[0:1, 0:1], scale_ref[1:2, 0:1]
    of_row = jnp.where(row < K, 1.0, jnp.where(row < K + SUBJ, zero, one))
    col = lax.broadcasted_iota(jnp.int32, (1, width), 1)
    of_col = jnp.where(col < K, 1.0, jnp.where(col < K + SUBJ, zero, one))
    out_ref[:, :base] = (left[:, :base] * (of_row * of_col[:, :base]) / masked)[:ROWS]
    edge = jnp.concatenate([left[:, base:], jnp.zeros((TALL, width - left.shape[1]), jnp.float32)], axis=1)
    values = jnp.where(col[:, base:] < K, edge, right)
    out_ref[:, base:] = (values * (of_row * of_col[:, base:]) / masked)[:ROWS, : KX - base]


def rotate_kernel(tile, scale_ref, base_ref, turn_ref, cen_ref, out_ref, held, sems):
    step = pl.program_id(0)
    steps = pl.num_programs(0)

    def fetch(i):
        cols = pl.ds(pl.multiple_of(i * tile, tile), tile)
        return pltpu.make_async_copy(base_ref.at[:, cols], held.at[i % 2], sems.at[i % 2])

    @pl.when(step == 0)
    def _():
        fetch(step).start()

    @pl.when(step + 1 < steps)
    def _():
        fetch(step + 1).start()

    first = jnp.dot(turn_ref[:, :SUBJ], cen_ref[0], preferred_element_type=jnp.float32)
    second = jnp.dot(turn_ref[:, SUBJ:], cen_ref[1], preferred_element_type=jnp.float32)
    fetch(step).wait()
    base = held[step % 2]
    out_ref[...] = (base + scale_ref[0:1, 0:1] * first + scale_ref[1:2, 0:1] * second).astype(out_ref.dtype)


def copies(value, axis, count):
    return lax.all_to_all(jnp.broadcast_to(value[None], (count, *value.shape)), axis, 0, 0, tiled=True)


def body(raw_frames, mask_index, subspace, rotation):
    depth = raw_frames.shape[1]
    extent = raw_frames.shape[2]
    per_device = subspace.shape[1]
    slab = ("x", "core")
    masked = per_device * 8 * GRP
    bf16 = jnp.bfloat16
    f32 = jnp.float32
    like = jax.ShapeDtypeStruct
    swap = [(0, 1), (1, 0)]
    turns = [[(i, (i + k) % 4) for i in range(4)] for k in range(4)]
    at = jnp.stack([lax.axis_index("x"), lax.axis_index("core"), lax.axis_index("grp")]).astype(jnp.int32)

    slab_at = lax.axis_index("x") * 2 + lax.axis_index("core")
    tiles = mask_index.reshape(-1, RUN)[:, 0] // RUN - slab_at * (depth * extent // RUN)
    up = [(i, i + 1) for i in range(7)]
    down = [(i + 1, i) for i in range(7)]
    packed = jnp.stack([tiles, lax.ppermute(tiles, slab, up), lax.ppermute(tiles, slab, down)])
    every = copies(packed, "grp", GRP)
    own = every[:, 0].reshape(-1)
    near = jnp.concatenate([every[: GRP // 4, 2].reshape(-1), every[3 * GRP // 4 :, 1].reshape(-1)])

    middles, rim, to_up, to_down = smooth(own, near, jnp.transpose(raw_frames, (1, 0, 2)))
    placed = pl.pallas_call(
        rim_kernel,
        out_shape=like(middles.shape, bf16),
        in_specs=[*vmem(3), hbm()],
        out_specs=hbm(),
        scratch_shapes=[pltpu.VMEM(rim.shape, bf16), pltpu.SemaphoreType.DMA((2,))],
        input_output_aliases={3: 0},
        compiler_params=params(16),
        name="rim",
    )(rim, lax.ppermute(to_up, slab, up), lax.ppermute(to_down, slab, down), middles)
    regrouped = lax.all_to_all(placed, "grp", 0, 0, tiled=True)

    at_ss, _ = lax.optimization_barrier((at, to_down))
    held = [pltpu.VMEM((4 * WIDE, per_device), bf16), pltpu.VMEM((K, per_device), bf16), pltpu.SemaphoreType.DMA((4 + PIECES,))]
    other_ss = pl.pallas_call(
        basis_other_kernel,
        out_shape=like((4 * WIDE, K), bf16),
        in_specs=[smem(), hbm()],
        out_specs=vmem(1)[0],
        scratch_shapes=held,
        compiler_params=params(24),
        name="basis_other",
    )(at_ss, subspace)
    got_ss = lax.ppermute(other_ss, "core", swap)
    parts = pl.pallas_call(
        basis_own_kernel,
        out_shape=[like((WIDE, K), bf16)] * 4,
        in_specs=[smem(), hbm(), *vmem(1)],
        out_specs=vmem(4),
        scratch_shapes=held,
        compiler_params=params(24),
        name="basis_own",
    )(at_ss, subspace, got_ss)
    parts = [parts[0]] + [lax.ppermute(parts[k], "x", turns[k]) for k in range(1, 4)]
    by_row = pl.pallas_call(
        basis_rows_kernel,
        out_shape=like((GRP, SHARE, RUN), bf16),
        in_specs=[smem(), *vmem(4)],
        out_specs=vmem(1)[0],
        scratch_shapes=[pltpu.VMEM((WIDE, 1408), f32)],
        compiler_params=params(16),
        name="basis_rows",
    )(at, *parts)

    centered, other_c, own_c, power = pl.pallas_call(
        columns_kernel,
        out_shape=[like((2, SUBJ, per_device), bf16), like((KX, SUBJ), bf16), like((KX, SUBJ), f32), like((8, RUN), f32)],
        in_specs=[smem(), *vmem(1), hbm()],
        out_specs=[hbm(), *vmem(1), hbm(), *vmem(1)],
        scratch_shapes=[
            pltpu.VMEM((K, per_device), bf16),
            pltpu.VMEM((2, SUBJ, per_device), bf16),
            pltpu.VMEM((KX, SUBJ), f32),
            pltpu.SemaphoreType.DMA((3,)),
        ],
        compiler_params=params(24),
        name="columns",
    )(at, regrouped, subspace)
    sent = pl.pallas_call(
        windows_kernel,
        out_shape=like((GRP, 2 * TALL + SHARE, RUN), bf16),
        in_specs=[hbm(), *vmem(3)],
        out_specs=vmem(1)[0],
        scratch_shapes=[pltpu.VMEM((KX, SUBJ), f32), pltpu.SemaphoreType.DMA],
        compiler_params=params(16),
        name="windows",
    )(own_c, lax.ppermute(other_c, "core", swap), power, by_row)
    summed = lax.all_to_all(sent, "grp", 0, 0, tiled=True)

    rotation_b, _ = lax.optimization_barrier((rotation, sent))
    contract = (((0,), (0,)), ((), ()))
    from_basis = lax.dot_general(rotation_b[:K], subspace, contract, preferred_element_type=f32)
    summed, from_basis, turn = lax.optimization_barrier((summed, from_basis, rotation_b[K:].T))

    total = pl.pallas_call(
        total_kernel,
        out_shape=like((2 * TALL + SHARE, RUN), bf16),
        in_specs=vmem(1),
        out_specs=vmem(1)[0],
        compiler_params=params(16),
        name="total",
    )(summed)
    sum_c, parts_ss = pl.pallas_call(
        slab_kernel,
        out_shape=[like((2 * TALL, RUN), f32), like((4, SHARE, RUN), bf16)],
        in_specs=vmem(4),
        out_specs=vmem(2),
        compiler_params=params(16),
        name="slab",
    )(total, *[lax.ppermute(total, "x", turns[k]) for k in range(1, 4)])
    rows_c, scales, turned = pl.pallas_call(
        functools.partial(finish_kernel, float(masked * SUBJ)),
        out_shape=[like((TALL, 2 * SUBJ), f32), like((8, RUN), f32), like((GRP, TALL, TALL), bf16)],
        in_specs=[smem(), *vmem(2)],
        out_specs=vmem(3),
        compiler_params=params(16),
        name="finish",
    )(at, sum_c, lax.ppermute(sum_c, "core", swap))

    back = lax.all_to_all(turned, "grp", 0, 0, tiled=True)
    gram_rows = pl.pallas_call(
        functools.partial(assemble_kernel, float(masked)),
        out_shape=like((ROWS, KX), f32),
        in_specs=[smem(), *vmem(5)],
        out_specs=vmem(1)[0],
        scratch_shapes=[pltpu.VMEM((TALL, 1408), f32), pltpu.VMEM((TALL, 1408), f32)],
        compiler_params=params(16),
        name="assemble",
    )(at, back, rows_c, scales, parts_ss, lax.ppermute(parts_ss, "core", swap))

    tile = 256
    new_subspace = pl.pallas_call(
        functools.partial(rotate_kernel, tile),
        out_shape=like((K, per_device), bf16),
        grid=(per_device // tile,),
        in_specs=[
            pl.BlockSpec((8, RUN), lambda i: (0, 0)),
            hbm(),
            pl.BlockSpec((K, 2 * SUBJ), lambda i: (0, 0)),
            pl.BlockSpec((2, SUBJ, tile), lambda i: (0, 0, i)),
        ],
        out_specs=pl.BlockSpec((K, tile), lambda i: (0, i)),
        scratch_shapes=[pltpu.VMEM((2, K, tile), f32), pltpu.SemaphoreType.DMA((2,))],
        compiler_params=params(24),
        name="rotate",
    )(scales, from_basis, turn, centered)
    return (gram_rows, new_subspace)


def solution(mesh):
    fine = Mesh(mesh.devices.reshape(4, 2, GRP), ("x", "core", "grp"))
    slab = ("x", "core")
    placed = (P("grp", slab, None), P((*slab, "grp")), P(None, (*slab, "grp")), P())
    return jax.shard_map(
        body,
        mesh=fine,
        in_specs=placed,
        out_specs=(P("grp", None), P(None, (*slab, "grp"))),
        check_vma=False,
    )
```

```python
import functools
import math

import jax
import jax.numpy as jnp
import numpy as np
from jax import lax
from jax.experimental import pallas as pl
from jax.experimental.pallas import tpu as pltpu
from jax.sharding import Mesh
from jax.sharding import PartitionSpec as P

NX = 96
RUN = 128
RAD = 3
K = 1200
KX = 1712
SUBJ = 256
ROWS = 107
WIN = 120
TALL = 128
PART = 150
WIDE = 176
SHARE = 152
BIG = 56
LEAD = 384
BLOCK = 256
PHASES = 3
GRP = 16
TAB = 64
TAB_MID = 31

smooth_sigma = 1.0617
epsilon = 1e-06


def tap_weights():
    unscaled = [
        math.exp(-offset * offset / (2.0 * smooth_sigma * smooth_sigma))
        for offset in range(-RAD, RAD + 1)
    ]
    summed = sum(unscaled)
    return [weight / summed for weight in unscaled]


def plane_matrix():
    taps = np.array(tap_weights())
    cells_in = np.arange(LEAD + BLOCK + LEAD)[:, None]
    cells_out = np.arange(BLOCK)[None, :]
    parts = []
    for phase in range(PHASES):
        column = (phase * BLOCK + cells_out) % NX
        reach = cells_in - LEAD - cells_out
        rows = np.floor((reach + NX // 2) / NX).astype(np.int64)
        along = reach - rows * NX
        ok = (np.abs(rows) <= RAD) & (np.abs(along) <= RAD) & (column + along >= 0) & (column + along < NX)
        weight = taps[np.clip(rows + RAD, 0, 2 * RAD)] * taps[np.clip(along + RAD, 0, 2 * RAD)]
        parts.append(np.where(ok, weight, 0.0))
    return np.stack(parts).astype(np.float32)


def depth_table():
    table = np.zeros((TAB,), np.float32)
    table[TAB_MID - RAD : TAB_MID + RAD + 1] = tap_weights()
    return table


def smooth_kernel(depth, own_ref, near_ref, tab_ref, taps_ref, raw_ref, all_ref, rim_ref, up_ref, down_ref, pad, planar, mid_ref, mat_ref, sems, mid_sem, mat_sem):
    frames = raw_ref.shape[1]
    extent = raw_ref.shape[2]
    step = PHASES * BLOCK
    steps = extent // step
    tiles = extent // RUN

    def fetch(i):
        return pltpu.make_async_copy(
            raw_ref.at[:, :, pl.ds(i * step, step)],
            pad.at[:, :, pl.ds(LEAD + i * step, step)],
            sems.at[i],
        )

    plan = pltpu.make_async_copy(taps_ref, mat_ref, mat_sem)
    plan.start()
    for i in range(steps):
        fetch(i).start()
    edge = jnp.zeros((depth, frames, LEAD), pad.dtype)
    pad[:, :, :LEAD] = edge
    pad[:, :, LEAD + extent :] = edge
    plan.wait()
    fetch(0).wait()

    def block(i, carry):
        @pl.when(i + 1 < steps)
        def _():
            fetch(i + 1).wait()

        for phase in range(PHASES):
            start = pl.multiple_of(i * step + phase * BLOCK, BLOCK)
            cells = pad[:, :, pl.ds(start, LEAD + BLOCK + LEAD)].reshape(depth * frames, LEAD + BLOCK + LEAD)
            out = jnp.dot(cells, mat_ref[phase], preferred_element_type=jnp.float32)
            planar[:, :, pl.ds(start, BLOCK)] = out.reshape(depth, frames, BLOCK)
        return carry

    lax.fori_loop(0, steps, block, 0)

    taps = tap_weights()

    def place(tile):
        plane = tile // tiles
        return plane, pl.multiple_of((tile - plane * tiles) * RUN, RUN)

    per = mid_ref.shape[2] // RUN

    def middle(g, carry):
        for j in range(per):
            plane, lane = place(own_ref[(g + GRP // 4) * per + j])
            total = taps[0] * planar[plane - RAD, :, pl.ds(lane, RUN)]
            for k in range(1, 2 * RAD + 1):
                total = total + taps[k] * planar[plane - RAD + k, :, pl.ds(lane, RUN)]
            mid_ref[g, :, j * RUN : (j + 1) * RUN] = total.astype(mid_ref.dtype)
        return carry

    def some(tile, first, count, shift):
        plane, lane = place(tile)
        total = None
        for q in range(first, first + count):
            weight = tab_ref[q - plane + shift + TAB_MID]
            term = weight * planar[q, :, pl.ds(lane, RUN)]
            total = term if total is None else total + term
        return total

    def rims(g, carry):
        for j in range(per):
            cols = slice(j * RUN, (j + 1) * RUN)
            at = g * per + j
            up_ref[g, :, cols] = some(near_ref[at], depth - RAD, RAD, -depth).astype(up_ref.dtype)
            down_ref[g, :, cols] = some(near_ref[GRP // 4 * per + at], 0, RAD, depth).astype(down_ref.dtype)
            rim_ref[g, :, cols] = some(own_ref[at], 0, 2 * RAD, 0)
            rim_ref[GRP // 4 + g, :, cols] = some(own_ref[GRP * 3 // 4 * per + at], depth - 2 * RAD, 2 * RAD, 0)
        return carry

    lax.fori_loop(0, GRP // 2, middle, 0)
    keep = pltpu.make_async_copy(mid_ref, all_ref.at[GRP // 4 : GRP * 3 // 4], mid_sem)
    keep.start()
    lax.fori_loop(0, GRP // 4, rims, 0)
    keep.wait()


def smooth(own, near, raw):
    depth, frames, extent = raw.shape
    per_device = own.shape[0] // GRP * RUN
    smem = pl.BlockSpec(memory_space=pltpu.SMEM)
    vmem = pl.BlockSpec(memory_space=pltpu.VMEM)
    quarter = (GRP // 4, frames, per_device)
    half = (GRP // 2, frames, per_device)
    return pl.pallas_call(
        functools.partial(smooth_kernel, depth),
        out_shape=[
            jax.ShapeDtypeStruct((GRP, frames, per_device), jnp.bfloat16),
            jax.ShapeDtypeStruct(half, jnp.float32),
            jax.ShapeDtypeStruct(quarter, jnp.bfloat16),
            jax.ShapeDtypeStruct(quarter, jnp.bfloat16),
        ],
        in_specs=[smem, smem, smem, pl.BlockSpec(memory_space=pltpu.HBM), pl.BlockSpec(memory_space=pltpu.HBM)],
        out_specs=[pl.BlockSpec(memory_space=pltpu.HBM), vmem, vmem, vmem],
        scratch_shapes=[
            pltpu.VMEM((depth, frames, extent + 2 * LEAD), jnp.bfloat16),
            pltpu.VMEM((depth, frames, extent), jnp.float32),
            pltpu.VMEM(half, jnp.bfloat16),
            pltpu.VMEM((PHASES, LEAD + BLOCK + LEAD, BLOCK), jnp.bfloat16),
            pltpu.SemaphoreType.DMA((extent // (PHASES * BLOCK),)),
            pltpu.SemaphoreType.DMA,
            pltpu.SemaphoreType.DMA,
        ],
        compiler_params=pltpu.CompilerParams(vmem_limit_bytes=59 * 1024 * 1024),
        name="smooth",
    )(own, near, jnp.asarray(depth_table()), jnp.asarray(plane_matrix()).astype(jnp.bfloat16), raw)


NT = (((1,), (1,)), ((), ()))


def row_start(first):
    return min(first // 8 * 8, KX - WIN) if isinstance(first, int) else jnp.minimum(first // 8 * 8, KX - WIN)


def part_start(part):
    return jnp.minimum(part * PART // 16 * 16, K - WIDE)


def vmem(count):
    return [pl.BlockSpec(memory_space=pltpu.VMEM)] * count


def smem():
    return pl.BlockSpec(memory_space=pltpu.SMEM)


def params(mib):
    return pltpu.CompilerParams(vmem_limit_bytes=mib * 1024 * 1024)


def hbm():
    return pl.BlockSpec(memory_space=pltpu.HBM)


PIECES = ((0, 512), (512, 1024), (1024, K))
HALF = WIDE // 2


def basis_copies(x, which, sub_ref, left, right, sems):
    made = []
    for k in range(4):
        start = pl.multiple_of(part_start((x + k) % 4 * 2 + which), 16)
        made.append(
            pltpu.make_async_copy(sub_ref.at[pl.ds(start, WIDE)], left.at[k * WIDE : (k + 1) * WIDE], sems.at[k])
        )
    for i, (lo, hi) in enumerate(PIECES):
        rows = slice(lo, hi)
        made.append(pltpu.make_async_copy(sub_ref.at[rows], right.at[rows], sems.at[4 + i]))
    for copy in made:
        copy.start()
    return made


def basis_other_kernel(at_ref, sub_ref, out_ref, left, right, sems):
    made = basis_copies(at_ref[0], 1 - at_ref[1], sub_ref, left, right, sems)
    for copy in made[:4]:
        copy.wait()
    for i, (lo, hi) in enumerate(PIECES):
        made[4 + i].wait()
        out_ref[:, lo:hi] = lax.dot_general(
            left[...], right[lo:hi, :], NT, preferred_element_type=jnp.float32
        ).astype(out_ref.dtype)


def basis_own_kernel(at_ref, sub_ref, got_ref, own_ref, next_ref, far_ref, back_ref, left, right, sems):
    made = basis_copies(at_ref[0], at_ref[1], sub_ref, left, right, sems)
    for copy in made[:4]:
        copy.wait()
    for i, (lo, hi) in enumerate(PIECES):
        made[4 + i].wait()
        part = lax.dot_general(left[...], right[lo:hi, :], NT, preferred_element_type=jnp.float32)
        part = (part + got_ref[:, lo:hi].astype(jnp.float32)).astype(own_ref.dtype)
        own_ref[:, lo:hi] = part[:WIDE]
        next_ref[:, lo:hi] = part[WIDE : 2 * WIDE]
        far_ref[:, :, lo:hi] = part[2 * WIDE : 3 * WIDE].reshape(2, HALF, hi - lo)
        back_ref[:, lo:hi] = part[3 * WIDE :]


def basis_relay_kernel(next_ref, back_ref, low_ref, high_ref, next_out, back_out):
    next_out[:HALF] = (next_ref[:HALF].astype(jnp.float32) + low_ref[...].astype(jnp.float32)).astype(next_out.dtype)
    next_out[HALF:] = next_ref[HALF:]
    back_out[:HALF] = back_ref[:HALF]
    back_out[HALF:] = (back_ref[HALF:].astype(jnp.float32) + high_ref[...].astype(jnp.float32)).astype(back_out.dtype)


def basis_rows_kernel(at_ref, a_ref, b_ref, c_ref, out_ref, flat):
    part = at_ref[0] * 2 + at_ref[1]
    total = a_ref[...].astype(jnp.float32) + b_ref[...].astype(jnp.float32) + c_ref[...].astype(jnp.float32)
    flat[:, K // RUN * RUN :] = jnp.zeros((flat.shape[0], flat.shape[1] - K // RUN * RUN), jnp.float32)
    flat[:, :K] = total
    shift = (WIDE - (part * PART - part_start(part))) % WIDE
    narrow = pltpu.roll(flat[...], shift, 0)[:SHARE].astype(jnp.bfloat16)
    line = lax.broadcasted_iota(jnp.int32, (256, RUN), 0)
    lane = lax.broadcasted_iota(jnp.int32, (256, RUN), 1)
    for g in range(GRP):
        begin = g * ROWS // RUN * RUN
        if g * ROWS < K:
            pick = jnp.where((line == lane + (g * ROWS - begin)) & (lane < ROWS), 1.0, 0.0).astype(jnp.bfloat16)
            out_ref[g] = jnp.dot(narrow[:, begin : begin + 256], pick, preferred_element_type=jnp.float32).astype(
                out_ref.dtype
            )
        else:
            out_ref[g] = jnp.zeros((SHARE, RUN), out_ref.dtype)


def rim_kernel(rim_ref, low_ref, high_ref, all_ref, out_ref, made, sems):
    del all_ref
    quarter = GRP // 4
    made[:quarter] = (rim_ref[:quarter] + low_ref[...].astype(jnp.float32)).astype(made.dtype)
    first = pltpu.make_async_copy(made.at[:quarter], out_ref.at[:quarter], sems.at[0])
    first.start()
    made[quarter:] = (rim_ref[quarter:] + high_ref[...].astype(jnp.float32)).astype(made.dtype)
    second = pltpu.make_async_copy(made.at[quarter:], out_ref.at[3 * quarter :], sems.at[1])
    second.start()
    first.wait()
    second.wait()


def columns_kernel(at_ref, got_ref, basis_ref, cen_out, other_ref, own_out, power_ref, sub_ref, cen_ref, own_ref, sems):
    per_device = sub_ref.shape[1]
    core = at_ref[1]
    each = GRP // 2
    fetch = pltpu.make_async_copy(basis_ref, sub_ref, sems.at[0])
    fetch.start()

    def centre(i, sums):
        cols = pl.ds(pl.multiple_of(i * RUN, RUN), RUN)
        new = []
        for s in range(2):
            wide = got_ref[s * each : (s + 1) * each, :, cols].reshape(SUBJ, RUN).astype(jnp.float32)
            mean = jnp.sum(wide, axis=0, keepdims=True) * (1.0 / SUBJ)
            cen = (wide - mean).astype(cen_ref.dtype)
            cen_ref[s, :, cols] = cen
            back = cen.astype(jnp.float32)
            new.append(sums[s] + jnp.sum((back * back).reshape(SUBJ // 8, 8, RUN), axis=0))
        return tuple(new)

    zero = jnp.zeros((8, RUN), jnp.float32)
    sums = lax.fori_loop(0, per_device // RUN, centre, (zero, zero))
    keep = pltpu.make_async_copy(cen_ref, cen_out, sems.at[1])
    keep.start()
    line = lax.broadcasted_iota(jnp.int32, (8, RUN), 0)
    first = jnp.sum(sums[0], keepdims=True)
    second = jnp.sum(sums[1], keepdims=True)
    power_ref[...] = jnp.where(line == 0, first, jnp.where(line == 1, second, 0.0))

    fetch.wait()
    for which, out in ((core, own_ref), (1 - core, other_ref)):
        right = cen_ref[which]
        for lo in range(0, K, 400):
            out[lo : lo + 400, :] = lax.dot_general(
                sub_ref[lo : lo + 400, :], right, NT, preferred_element_type=jnp.float32
            ).astype(out.dtype)
        for s in range(2):
            lo = K + s * SUBJ
            out[lo : lo + SUBJ, :] = lax.dot_general(
                cen_ref[s], right, NT, preferred_element_type=jnp.float32
            ).astype(out.dtype)
        if out is own_ref:
            leave = pltpu.make_async_copy(own_ref, own_out, sems.at[2])
            leave.start()
    leave.wait()
    keep.wait()


def write_power(power, put):
    high = power.astype(jnp.bfloat16)
    put(slice(WIN, TALL), high)
    put(slice(TALL + WIN, 2 * TALL), (power - high.astype(jnp.float32)).astype(jnp.bfloat16))


def windows_kernel(own_ref, got_ref, power_ref, basis_ref, out_ref, whole, sem):
    fetch = pltpu.make_async_copy(own_ref, whole, sem)
    fetch.start()
    for g in range(GRP):
        out_ref[g, 2 * TALL :, :] = basis_ref[g]

        def put(rows, value, g=g):
            out_ref[g, rows, :] = value

        write_power(power_ref[...], put)
    fetch.wait()
    whole[...] = whole[...] + got_ref[...].astype(jnp.float32)
    for g in range(GRP):
        first = row_start(g * ROWS)
        for half in range(2):
            out_ref[g, half * TALL : half * TALL + WIN, :] = whole[
                first : first + WIN, half * RUN : (half + 1) * RUN
            ].astype(out_ref.dtype)


def total_kernel(got_ref, out_ref, share_ref):
    total = got_ref[0].astype(jnp.float32)
    for g in range(1, GRP):
        total = total + got_ref[g].astype(jnp.float32)
    out_ref[...] = total[: 2 * TALL].astype(out_ref.dtype)
    share_ref[...] = total[2 * TALL :].astype(share_ref.dtype)

    def put(rows, value):
        out_ref[rows, :] = value

    write_power(total[WIN:TALL] + total[TALL + WIN : 2 * TALL], put)


def slab_kernel(a_ref, b_ref, c_ref, d_ref, sum_ref):
    total = a_ref[...].astype(jnp.float32) + b_ref[...].astype(jnp.float32)
    sum_ref[...] = total + c_ref[...].astype(jnp.float32) + d_ref[...].astype(jnp.float32)


def finish_kernel(count, at_ref, own_ref, got_ref, rows_ref, scale_ref, turned_ref):
    own, got = own_ref[...], got_ref[...]
    both = own + got
    scale_ref[...] = lax.rsqrt((both[WIN:TALL] + both[TALL + WIN :]) / count + epsilon)
    is_first = at_ref[1] == 0
    zero = jnp.where(is_first, own, got)
    one = jnp.where(is_first, got, own)
    rows = jnp.concatenate([zero[:TALL], zero[TALL:], one[:TALL], one[TALL:]], axis=1)
    first = at_ref[2] * ROWS
    shift = (TALL - (first - row_start(first))) % TALL
    rows = pltpu.roll(rows, shift, 0)
    rows_ref[...] = rows
    narrow = rows.astype(jnp.bfloat16)
    turned_ref[: K // ROWS] = jnp.zeros((K // ROWS, TALL, TALL), turned_ref.dtype)
    line = lax.broadcasted_iota(jnp.int32, (TALL, 2 * SUBJ), 0)
    lane = lax.broadcasted_iota(jnp.int32, (TALL, 2 * SUBJ), 1)
    for g in range(K // ROWS, GRP):
        pick = jnp.where(line + (g * ROWS - K) == lane, 1.0, 0.0).astype(jnp.bfloat16)
        turned_ref[g] = lax.dot_general(pick, narrow, NT, preferred_element_type=jnp.float32).astype(turned_ref.dtype)


def assemble_kernel(masked, at_ref, back_ref, rows_ref, scale_ref, zero_ref, one_ref, two_ref, three_ref, out_ref, basis, cross):
    x, core, grp = at_ref[0], at_ref[1], at_ref[2]
    first = grp * ROWS
    shares = (zero_ref, one_ref, two_ref, three_ref)
    basis[...] = jnp.zeros_like(basis)
    cross[...] = jnp.zeros_like(cross)
    line = lax.broadcasted_iota(jnp.int32, (SHARE, 384), 0)
    lane = lax.broadcasted_iota(jnp.int32, (SHARE, 384), 1)
    for k in range(4):
        for c, which in ((0, core), (1, 1 - core)):
            part = (x - k + 4) % 4 * 2 + which
            begin = part * PART // RUN * RUN
            put = jnp.where((line + (part * PART - begin) == lane) & (line < PART), 1.0, 0.0).astype(jnp.bfloat16)
            cols = pl.ds(pl.multiple_of(begin, RUN), 384)
            basis[:, cols] += lax.dot_general(
                shares[k][c], put, (((0,), (0,)), ((), ())), preferred_element_type=jnp.float32
            )
    line = lax.broadcasted_iota(jnp.int32, (TALL, 256), 0)
    lane = lax.broadcasted_iota(jnp.int32, (TALL, 256), 1)
    for g in range(K // ROWS + 1):
        begin = g * ROWS // RUN * RUN
        ok = (line + (g * ROWS - begin) == lane) & (line < ROWS) & (line + g * ROWS < K)
        put = jnp.where(ok, 1.0, 0.0).astype(jnp.bfloat16)
        cross[:, begin : begin + 256] += jnp.dot(back_ref[g], put, preferred_element_type=jnp.float32)
    width = 1792
    row = first + lax.broadcasted_iota(jnp.int32, (TALL, 1), 0)
    left = jnp.where(row < K, basis[...], cross[...])
    base = K // RUN * RUN
    right = pltpu.roll(
        jnp.concatenate([rows_ref[...], jnp.zeros((TALL, RUN), jnp.float32)], axis=1), K - base, 1
    )
    zero, one = scale_ref[0:1, 0:1], scale_ref[1:2, 0:1]
    of_row = jnp.where(row < K, 1.0, jnp.where(row < K + SUBJ, zero, one))
    col = lax.broadcasted_iota(jnp.int32, (1, width), 1)
    of_col = jnp.where(col < K, 1.0, jnp.where(col < K + SUBJ, zero, one))
    out_ref[:, :base] = (left[:, :base] * (of_row * of_col[:, :base]) / masked)[:ROWS]
    edge = jnp.concatenate([left[:, base:], jnp.zeros((TALL, width - left.shape[1]), jnp.float32)], axis=1)
    values = jnp.where(col[:, base:] < K, edge, right)
    out_ref[:, base:] = (values * (of_row * of_col[:, base:]) / masked)[:ROWS, : KX - base]


def rotate_kernel(tile, scale_ref, base_ref, turn_ref, cen_ref, out_ref, held, sems):
    step = pl.program_id(0)
    steps = pl.num_programs(0)

    def fetch(i):
        cols = pl.ds(pl.multiple_of(i * tile, tile), tile)
        return pltpu.make_async_copy(base_ref.at[:, cols], held.at[i % 2], sems.at[i % 2])

    @pl.when(step == 0)
    def _():
        fetch(step).start()

    @pl.when(step + 1 < steps)
    def _():
        fetch(step + 1).start()

    first = jnp.dot(turn_ref[:, :SUBJ], cen_ref[0], preferred_element_type=jnp.float32)
    second = jnp.dot(turn_ref[:, SUBJ:], cen_ref[1], preferred_element_type=jnp.float32)
    fetch(step).wait()
    base = held[step % 2]
    out_ref[...] = (base + scale_ref[0:1, 0:1] * first + scale_ref[1:2, 0:1] * second).astype(out_ref.dtype)


def copies(value, axis, count):
    return lax.all_to_all(jnp.broadcast_to(value[None], (count, *value.shape)), axis, 0, 0, tiled=True)


def body(raw_frames, mask_index, subspace, rotation):
    depth = raw_frames.shape[1]
    extent = raw_frames.shape[2]
    per_device = subspace.shape[1]
    slab = ("x", "core")
    masked = per_device * 8 * GRP
    bf16 = jnp.bfloat16
    f32 = jnp.float32
    like = jax.ShapeDtypeStruct
    swap = [(0, 1), (1, 0)]
    turns = [[(i, (i + k) % 4) for i in range(4)] for k in range(4)]
    at = jnp.stack([lax.axis_index("x"), lax.axis_index("core"), lax.axis_index("grp")]).astype(jnp.int32)

    slab_at = lax.axis_index("x") * 2 + lax.axis_index("core")
    tiles = mask_index.reshape(-1, RUN)[:, 0] // RUN - slab_at * (depth * extent // RUN)
    up = [(i, i + 1) for i in range(7)]
    down = [(i + 1, i) for i in range(7)]
    packed = jnp.stack([tiles, lax.ppermute(tiles, slab, up), lax.ppermute(tiles, slab, down)])
    every = copies(packed, "grp", GRP)
    own = every[:, 0].reshape(-1)
    near = jnp.concatenate([every[: GRP // 4, 2].reshape(-1), every[3 * GRP // 4 :, 1].reshape(-1)])

    middles, rim, to_up, to_down = smooth(own, near, jnp.transpose(raw_frames, (1, 0, 2)))
    at_ss, _ = lax.optimization_barrier((at, to_down))
    held = [
        pltpu.VMEM((4 * WIDE, per_device), bf16),
        pltpu.VMEM((K, per_device), bf16),
        pltpu.SemaphoreType.DMA((4 + len(PIECES),)),
    ]
    other_ss = pl.pallas_call(
        basis_other_kernel,
        out_shape=like((4 * WIDE, K), bf16),
        in_specs=[smem(), hbm()],
        out_specs=vmem(1)[0],
        scratch_shapes=held,
        compiler_params=params(BIG),
        name="basis_other",
    )(at_ss, subspace)
    from_low, from_high, other_ss = lax.optimization_barrier(
        (lax.ppermute(to_up, slab, up), lax.ppermute(to_down, slab, down), other_ss)
    )
    placed = pl.pallas_call(
        rim_kernel,
        out_shape=like(middles.shape, bf16),
        in_specs=[*vmem(3), hbm()],
        out_specs=hbm(),
        scratch_shapes=[pltpu.VMEM(rim.shape, bf16), pltpu.SemaphoreType.DMA((2,))],
        input_output_aliases={3: 0},
        compiler_params=params(16),
        name="rim",
    )(rim, from_low, from_high, middles)
    regrouped = lax.all_to_all(placed, "grp", 0, 0, tiled=True)

    got_ss = lax.ppermute(other_ss, "core", swap)
    own_ss, next_ss, far_ss, back_ss = pl.pallas_call(
        basis_own_kernel,
        out_shape=[like((WIDE, K), bf16), like((WIDE, K), bf16), like((2, HALF, K), bf16), like((WIDE, K), bf16)],
        in_specs=[smem(), hbm(), *vmem(1)],
        out_specs=vmem(4),
        scratch_shapes=held,
        compiler_params=params(BIG),
        name="basis_own",
    )(at_ss, subspace, got_ss)
    ahead, behind = turns[1], turns[3]
    next_ss, back_ss = pl.pallas_call(
        basis_relay_kernel,
        out_shape=[like((WIDE, K), bf16)] * 2,
        in_specs=vmem(4),
        out_specs=vmem(2),
        compiler_params=params(16),
        name="basis_relay",
    )(next_ss, back_ss, lax.ppermute(far_ss[0], "x", ahead), lax.ppermute(far_ss[1], "x", behind))
    regrouped, next_ss, back_ss = lax.optimization_barrier((regrouped, next_ss, back_ss))
    by_row = pl.pallas_call(
        basis_rows_kernel,
        out_shape=like((GRP, SHARE, RUN), bf16),
        in_specs=[smem(), *vmem(3)],
        out_specs=vmem(1)[0],
        scratch_shapes=[pltpu.VMEM((WIDE, 1408), f32)],
        compiler_params=params(16),
        name="basis_rows",
    )(at, own_ss, lax.ppermute(next_ss, "x", ahead), lax.ppermute(back_ss, "x", behind))

    centered, other_c, own_c, power = pl.pallas_call(
        columns_kernel,
        out_shape=[like((2, SUBJ, per_device), bf16), like((KX, SUBJ), bf16), like((KX, SUBJ), f32), like((8, RUN), f32)],
        in_specs=[smem(), *vmem(1), hbm()],
        out_specs=[hbm(), *vmem(1), hbm(), *vmem(1)],
        scratch_shapes=[
            pltpu.VMEM((K, per_device), bf16),
            pltpu.VMEM((2, SUBJ, per_device), bf16),
            pltpu.VMEM((KX, SUBJ), f32),
            pltpu.SemaphoreType.DMA((3,)),
        ],
        compiler_params=params(47),
        name="columns",
    )(at, regrouped, subspace)
    sent = pl.pallas_call(
        windows_kernel,
        out_shape=like((GRP, 2 * TALL + SHARE, RUN), bf16),
        in_specs=[hbm(), *vmem(3)],
        out_specs=vmem(1)[0],
        scratch_shapes=[pltpu.VMEM((KX, SUBJ), f32), pltpu.SemaphoreType.DMA],
        compiler_params=params(16),
        name="windows",
    )(own_c, lax.ppermute(other_c, "core", swap), power, by_row)
    summed = lax.all_to_all(sent, "grp", 0, 0, tiled=True)

    rotation_b, _ = lax.optimization_barrier((rotation, sent))
    contract = (((0,), (0,)), ((), ()))
    from_basis = lax.dot_general(rotation_b[:K], subspace, contract, preferred_element_type=f32)
    summed, from_basis, turn = lax.optimization_barrier((summed, from_basis, rotation_b[K:].T))

    total, share = pl.pallas_call(
        total_kernel,
        out_shape=[like((2 * TALL, RUN), bf16), like((SHARE, RUN), bf16)],
        in_specs=vmem(1),
        out_specs=vmem(2),
        compiler_params=params(16),
        name="total",
    )(summed)
    sum_c = pl.pallas_call(
        slab_kernel,
        out_shape=like((2 * TALL, RUN), f32),
        in_specs=vmem(4),
        out_specs=vmem(1)[0],
        compiler_params=params(16),
        name="slab",
    )(total, *[lax.ppermute(total, "x", turns[k]) for k in range(1, 4)])
    share = jnp.stack([share, lax.ppermute(share, "core", swap)])
    rows_c, scales, turned = pl.pallas_call(
        functools.partial(finish_kernel, float(masked * SUBJ)),
        out_shape=[like((TALL, 2 * SUBJ), f32), like((8, RUN), f32), like((GRP, TALL, TALL), bf16)],
        in_specs=[smem(), *vmem(2)],
        out_specs=vmem(3),
        compiler_params=params(16),
        name="finish",
    )(at, sum_c, lax.ppermute(sum_c, "core", swap))

    back = lax.all_to_all(turned, "grp", 0, 0, tiled=True)
    share, _ = lax.optimization_barrier((share, turned))
    gram_rows = pl.pallas_call(
        functools.partial(assemble_kernel, float(masked)),
        out_shape=like((ROWS, KX), f32),
        in_specs=[smem(), *vmem(7)],
        out_specs=vmem(1)[0],
        scratch_shapes=[pltpu.VMEM((TALL, 1408), f32), pltpu.VMEM((TALL, 1408), f32)],
        compiler_params=params(16),
        name="assemble",
    )(at, back, rows_c, scales, share, *[lax.ppermute(share, "x", turns[k]) for k in range(1, 4)])

    tile = 256
    new_subspace = pl.pallas_call(
        functools.partial(rotate_kernel, tile),
        out_shape=like((K, per_device), bf16),
        grid=(per_device // tile,),
        in_specs=[
            pl.BlockSpec((8, RUN), lambda i: (0, 0)),
            hbm(),
            pl.BlockSpec((K, 2 * SUBJ), lambda i: (0, 0)),
            pl.BlockSpec((2, SUBJ, tile), lambda i: (0, 0, i)),
        ],
        out_specs=pl.BlockSpec((K, tile), lambda i: (0, i)),
        scratch_shapes=[pltpu.VMEM((2, K, tile), f32), pltpu.SemaphoreType.DMA((2,))],
        compiler_params=params(BIG),
        name="rotate",
    )(scales, from_basis, turn, centered)
    return (gram_rows, new_subspace)


def solution(mesh):
    fine = Mesh(mesh.devices.reshape(4, 2, GRP), ("x", "core", "grp"))
    slab = ("x", "core")
    placed = (P("grp", slab, None), P((*slab, "grp")), P(None, (*slab, "grp")), P())
    return jax.shard_map(
        body,
        mesh=fine,
        in_specs=placed,
        out_specs=(P("grp", None), P(None, (*slab, "grp"))),
        check_vma=False,
    )
```

```python
import functools
import math

import jax
import jax.numpy as jnp
import numpy as np
from jax import lax
from jax.experimental import pallas as pl
from jax.experimental.pallas import tpu as pltpu
from jax.sharding import Mesh
from jax.sharding import PartitionSpec as P

NX = 96
RUN = 128
RAD = 3
K = 1200
KX = 1712
SUBJ = 256
ROWS = 107
WIN = 120
TALL = 128
PART = 150
WIDE = 176
SHARE = 152
BIG = 56
LEAD = 384
BLOCK = 256
PHASES = 3
GRP = 16
TAB = 64
TAB_MID = 31

smooth_sigma = 1.0617
epsilon = 1e-06


def tap_weights():
    unscaled = [
        math.exp(-offset * offset / (2.0 * smooth_sigma * smooth_sigma))
        for offset in range(-RAD, RAD + 1)
    ]
    summed = sum(unscaled)
    return [weight / summed for weight in unscaled]


def plane_matrix():
    taps = np.array(tap_weights())
    cells_in = np.arange(LEAD + BLOCK + LEAD)[:, None]
    cells_out = np.arange(BLOCK)[None, :]
    parts = []
    for phase in range(PHASES):
        column = (phase * BLOCK + cells_out) % NX
        reach = cells_in - LEAD - cells_out
        rows = np.floor((reach + NX // 2) / NX).astype(np.int64)
        along = reach - rows * NX
        ok = (np.abs(rows) <= RAD) & (np.abs(along) <= RAD) & (column + along >= 0) & (column + along < NX)
        weight = taps[np.clip(rows + RAD, 0, 2 * RAD)] * taps[np.clip(along + RAD, 0, 2 * RAD)]
        parts.append(np.where(ok, weight, 0.0))
    return np.stack(parts).astype(np.float32)


def depth_table():
    table = np.zeros((TAB,), np.float32)
    table[TAB_MID - RAD : TAB_MID + RAD + 1] = tap_weights()
    return table


def planes_kernel(taps_ref, raw_ref, planar, pad, mat_ref, made, sems, mat_sem, out_sems):
    depth, frames, extent = raw_ref.shape
    step = PHASES * BLOCK
    steps = extent // step

    def fetch(i):
        return pltpu.make_async_copy(
            raw_ref.at[:, :, pl.ds(i * step, step)],
            pad.at[:, :, pl.ds(LEAD + i * step, step)],
            sems.at[i],
        )

    def leave(i):
        slot = i % 2
        return pltpu.make_async_copy(made.at[slot], planar.at[:, :, pl.ds(i * step, step)], out_sems.at[slot])

    plan = pltpu.make_async_copy(taps_ref, mat_ref, mat_sem)
    plan.start()
    for i in range(steps):
        fetch(i).start()
    edge = jnp.zeros((depth, frames, LEAD), pad.dtype)
    pad[:, :, :LEAD] = edge
    pad[:, :, LEAD + extent :] = edge
    plan.wait()
    fetch(0).wait()

    def block(i, carry):
        @pl.when(i + 1 < steps)
        def _():
            fetch(i + 1).wait()

        @pl.when(i >= 2)
        def _():
            leave(i - 2).wait()

        for phase in range(PHASES):
            start = pl.multiple_of(i * step + phase * BLOCK, BLOCK)
            cells = pad[:, :, pl.ds(start, LEAD + BLOCK + LEAD)].reshape(depth * frames, LEAD + BLOCK + LEAD)
            out = jnp.dot(cells, mat_ref[phase], preferred_element_type=jnp.float32)
            made[i % 2, :, :, phase * BLOCK : (phase + 1) * BLOCK] = out.reshape(depth, frames, BLOCK)
        leave(i).start()
        return carry

    lax.fori_loop(0, steps, block, 0)
    leave(steps - 2).wait()
    leave(steps - 1).wait()


def depth_kernel(own_ref, near_ref, tab_ref, made_ref, all_ref, rim_ref, up_ref, down_ref, planar, mid_ref, sems, mid_sem):
    depth, _, extent = planar.shape

    def fetch(q):
        return pltpu.make_async_copy(made_ref.at[q], planar.at[q], sems.at[q])

    def more(q, carry):
        fetch(q).wait()
        return carry

    for q in range(depth):
        fetch(q).start()
    tiles = extent // RUN
    taps = tap_weights()

    def place(tile):
        plane = tile // tiles
        return plane, pl.multiple_of((tile - plane * tiles) * RUN, RUN)

    per = mid_ref.shape[2] // RUN

    def middle(g, have):
        last = own_ref[(g + GRP // 4) * per + per - 1] // tiles + RAD + 1
        lax.fori_loop(have, last, more, 0)
        for j in range(per):
            plane, lane = place(own_ref[(g + GRP // 4) * per + j])
            total = taps[0] * planar[plane - RAD, :, pl.ds(lane, RUN)]
            for k in range(1, 2 * RAD + 1):
                total = total + taps[k] * planar[plane - RAD + k, :, pl.ds(lane, RUN)]
            mid_ref[g, :, j * RUN : (j + 1) * RUN] = total.astype(mid_ref.dtype)
        return jnp.maximum(have, last)

    def some(tile, first, count, shift):
        plane, lane = place(tile)
        total = None
        for q in range(first, first + count):
            weight = tab_ref[q - plane + shift + TAB_MID]
            term = weight * planar[q, :, pl.ds(lane, RUN)]
            total = term if total is None else total + term
        return total

    def lower(g, carry):
        for j in range(per):
            cols = slice(j * RUN, (j + 1) * RUN)
            at = g * per + j
            down_ref[g, :, cols] = some(near_ref[GRP // 4 * per + at], 0, RAD, depth).astype(down_ref.dtype)
            rim_ref[g, :, cols] = some(own_ref[at], 0, 2 * RAD, 0)
        return carry

    def upper(g, carry):
        for j in range(per):
            cols = slice(j * RUN, (j + 1) * RUN)
            at = g * per + j
            up_ref[g, :, cols] = some(near_ref[at], depth - RAD, RAD, -depth).astype(up_ref.dtype)
            rim_ref[GRP // 4 + g, :, cols] = some(own_ref[GRP * 3 // 4 * per + at], depth - 2 * RAD, 2 * RAD, 0)
        return carry

    lax.fori_loop(0, 2 * RAD, more, 0)
    lax.fori_loop(0, GRP // 4, lower, 0)
    have = lax.fori_loop(0, GRP // 2, middle, jnp.int32(2 * RAD))
    keep = pltpu.make_async_copy(mid_ref, all_ref.at[GRP // 4 : GRP * 3 // 4], mid_sem)
    keep.start()
    lax.fori_loop(have, depth, more, 0)
    lax.fori_loop(0, GRP // 4, upper, 0)
    keep.wait()


def filter_planes(raw):
    depth, frames, extent = raw.shape
    return pl.pallas_call(
        planes_kernel,
        out_shape=jax.ShapeDtypeStruct((depth, frames, extent), jnp.float32),
        in_specs=[hbm(), hbm()],
        out_specs=hbm(),
        scratch_shapes=[
            pltpu.VMEM((depth, frames, extent + 2 * LEAD), jnp.bfloat16),
            pltpu.VMEM((PHASES, LEAD + BLOCK + LEAD, BLOCK), jnp.bfloat16),
            pltpu.VMEM((2, depth, frames, PHASES * BLOCK), jnp.float32),
            pltpu.SemaphoreType.DMA((extent // (PHASES * BLOCK),)),
            pltpu.SemaphoreType.DMA,
            pltpu.SemaphoreType.DMA((2,)),
        ],
        compiler_params=params(58),
        name="planes",
    )(jnp.asarray(plane_matrix()).astype(jnp.bfloat16), raw)


def filter_depth(own, near, planar):
    frames = planar.shape[1]
    per_device = own.shape[0] // GRP * RUN
    quarter = (GRP // 4, frames, per_device)
    half = (GRP // 2, frames, per_device)
    return pl.pallas_call(
        depth_kernel,
        out_shape=[
            jax.ShapeDtypeStruct((GRP, frames, per_device), jnp.bfloat16),
            jax.ShapeDtypeStruct(half, jnp.float32),
            jax.ShapeDtypeStruct(quarter, jnp.bfloat16),
            jax.ShapeDtypeStruct(quarter, jnp.bfloat16),
        ],
        in_specs=[smem()] * 3 + [hbm()],
        out_specs=[hbm(), *vmem(3)],
        scratch_shapes=[
            pltpu.VMEM(planar.shape, jnp.float32),
            pltpu.VMEM(half, jnp.bfloat16),
            pltpu.SemaphoreType.DMA(planar.shape[:1]),
            pltpu.SemaphoreType.DMA,
        ],
        compiler_params=params(44),
        name="depth",
    )(own, near, jnp.asarray(depth_table()), planar)


NT = (((1,), (1,)), ((), ()))


def row_start(first):
    return min(first // 8 * 8, KX - WIN) if isinstance(first, int) else jnp.minimum(first // 8 * 8, KX - WIN)


def part_start(part):
    return jnp.minimum(part * PART // 16 * 16, K - WIDE)


def vmem(count):
    return [pl.BlockSpec(memory_space=pltpu.VMEM)] * count


def smem():
    return pl.BlockSpec(memory_space=pltpu.SMEM)


def params(mib):
    return pltpu.CompilerParams(vmem_limit_bytes=mib * 1024 * 1024)


def hbm():
    return pl.BlockSpec(memory_space=pltpu.HBM)


HALF = WIDE // 2


def gather_parts(x, which, sub_ref, left):
    for k in range(4):
        start = pl.multiple_of(part_start((x + k) % 4 * 2 + which), 16)
        left[k * WIDE : (k + 1) * WIDE, :] = sub_ref[pl.ds(start, WIDE), :]


def basis_other_kernel(at_ref, sub_ref, out_ref, left):
    gather_parts(at_ref[0], 1 - at_ref[1], sub_ref, left)
    out_ref[...] = lax.dot_general(left[...], sub_ref[...], NT, preferred_element_type=jnp.float32).astype(out_ref.dtype)


def basis_own_kernel(at_ref, sub_ref, got_ref, own_ref, next_ref, far_ref, back_ref, left):
    gather_parts(at_ref[0], at_ref[1], sub_ref, left)
    part = lax.dot_general(left[...], sub_ref[...], NT, preferred_element_type=jnp.float32)
    part = (part + got_ref[...].astype(jnp.float32)).astype(own_ref.dtype)
    own_ref[...] = part[:WIDE]
    next_ref[...] = part[WIDE : 2 * WIDE]
    far_ref[...] = part[2 * WIDE : 3 * WIDE].reshape(2, HALF, K)
    back_ref[...] = part[3 * WIDE :]


def basis_relay_kernel(next_ref, back_ref, low_ref, high_ref, next_out, back_out):
    next_out[:HALF] = (next_ref[:HALF].astype(jnp.float32) + low_ref[...].astype(jnp.float32)).astype(next_out.dtype)
    next_out[HALF:] = next_ref[HALF:]
    back_out[:HALF] = back_ref[:HALF]
    back_out[HALF:] = (back_ref[HALF:].astype(jnp.float32) + high_ref[...].astype(jnp.float32)).astype(back_out.dtype)


def basis_rows_kernel(at_ref, a_ref, b_ref, c_ref, out_ref, flat):
    part = at_ref[0] * 2 + at_ref[1]
    total = a_ref[...].astype(jnp.float32) + b_ref[...].astype(jnp.float32) + c_ref[...].astype(jnp.float32)
    flat[:, K // RUN * RUN :] = jnp.zeros((flat.shape[0], flat.shape[1] - K // RUN * RUN), jnp.float32)
    flat[:, :K] = total
    shift = (WIDE - (part * PART - part_start(part))) % WIDE
    narrow = pltpu.roll(flat[...], shift, 0)[:SHARE].astype(jnp.bfloat16)
    line = lax.broadcasted_iota(jnp.int32, (256, RUN), 0)
    lane = lax.broadcasted_iota(jnp.int32, (256, RUN), 1)
    for g in range(GRP):
        begin = g * ROWS // RUN * RUN
        if g * ROWS < K:
            pick = jnp.where((line == lane + (g * ROWS - begin)) & (lane < ROWS), 1.0, 0.0).astype(jnp.bfloat16)
            out_ref[g] = jnp.dot(narrow[:, begin : begin + 256], pick, preferred_element_type=jnp.float32).astype(
                out_ref.dtype
            )
        else:
            out_ref[g] = jnp.zeros((SHARE, RUN), out_ref.dtype)


def rim_kernel(rim_ref, low_ref, high_ref, all_ref, out_ref, made, sems):
    del all_ref
    quarter = GRP // 4
    made[:quarter] = (rim_ref[:quarter] + low_ref[...].astype(jnp.float32)).astype(made.dtype)
    first = pltpu.make_async_copy(made.at[:quarter], out_ref.at[:quarter], sems.at[0])
    first.start()
    made[quarter:] = (rim_ref[quarter:] + high_ref[...].astype(jnp.float32)).astype(made.dtype)
    second = pltpu.make_async_copy(made.at[quarter:], out_ref.at[3 * quarter :], sems.at[1])
    second.start()
    first.wait()
    second.wait()


def columns_kernel(at_ref, got_ref, basis_ref, cen_out, other_ref, own_out, power_ref, sub_ref, cen_ref, own_ref, sems):
    per_device = sub_ref.shape[1]
    core = at_ref[1]
    each = GRP // 2
    fetch = pltpu.make_async_copy(basis_ref, sub_ref, sems.at[0])
    fetch.start()

    def centre(i, sums):
        cols = pl.ds(pl.multiple_of(i * RUN, RUN), RUN)
        new = []
        for s in range(2):
            wide = got_ref[s * each : (s + 1) * each, :, cols].reshape(SUBJ, RUN).astype(jnp.float32)
            mean = jnp.sum(wide, axis=0, keepdims=True) * (1.0 / SUBJ)
            cen = (wide - mean).astype(cen_ref.dtype)
            cen_ref[s, :, cols] = cen
            back = cen.astype(jnp.float32)
            new.append(sums[s] + jnp.sum((back * back).reshape(SUBJ // 8, 8, RUN), axis=0))
        return tuple(new)

    zero = jnp.zeros((8, RUN), jnp.float32)
    sums = lax.fori_loop(0, per_device // RUN, centre, (zero, zero))
    keep = pltpu.make_async_copy(cen_ref, cen_out, sems.at[1])
    keep.start()
    line = lax.broadcasted_iota(jnp.int32, (8, RUN), 0)
    first = jnp.sum(sums[0], keepdims=True)
    second = jnp.sum(sums[1], keepdims=True)
    power_ref[...] = jnp.where(line == 0, first, jnp.where(line == 1, second, 0.0))

    fetch.wait()
    for which, out in ((core, own_ref), (1 - core, other_ref)):
        right = cen_ref[which]
        for lo in range(0, K, 400):
            out[lo : lo + 400, :] = lax.dot_general(
                sub_ref[lo : lo + 400, :], right, NT, preferred_element_type=jnp.float32
            ).astype(out.dtype)
        for s in range(2):
            lo = K + s * SUBJ
            out[lo : lo + SUBJ, :] = lax.dot_general(
                cen_ref[s], right, NT, preferred_element_type=jnp.float32
            ).astype(out.dtype)
        if out is own_ref:
            leave = pltpu.make_async_copy(own_ref, own_out, sems.at[2])
            leave.start()
    leave.wait()
    keep.wait()


def write_power(power, put):
    high = power.astype(jnp.bfloat16)
    put(slice(WIN, TALL), high)
    put(slice(TALL + WIN, 2 * TALL), (power - high.astype(jnp.float32)).astype(jnp.bfloat16))


def windows_kernel(own_ref, got_ref, power_ref, basis_ref, out_ref, whole, sem):
    fetch = pltpu.make_async_copy(own_ref, whole, sem)
    fetch.start()
    for g in range(GRP):
        out_ref[g, 2 * TALL :, :] = basis_ref[g]

        def put(rows, value, g=g):
            out_ref[g, rows, :] = value

        write_power(power_ref[...], put)
    fetch.wait()
    whole[...] = whole[...] + got_ref[...].astype(jnp.float32)
    for g in range(GRP):
        first = row_start(g * ROWS)
        for half in range(2):
            out_ref[g, half * TALL : half * TALL + WIN, :] = whole[
                first : first + WIN, half * RUN : (half + 1) * RUN
            ].astype(out_ref.dtype)


def total_kernel(got_ref, out_ref, share_ref):
    total = got_ref[0].astype(jnp.float32)
    for g in range(1, GRP):
        total = total + got_ref[g].astype(jnp.float32)
    out_ref[...] = total[: 2 * TALL].astype(out_ref.dtype)
    share_ref[...] = total[2 * TALL :].astype(share_ref.dtype)

    def put(rows, value):
        out_ref[rows, :] = value

    write_power(total[WIN:TALL] + total[TALL + WIN : 2 * TALL], put)


def slab_kernel(a_ref, b_ref, c_ref, d_ref, sum_ref):
    total = a_ref[...].astype(jnp.float32) + b_ref[...].astype(jnp.float32)
    sum_ref[...] = total + c_ref[...].astype(jnp.float32) + d_ref[...].astype(jnp.float32)


def finish_kernel(count, at_ref, own_ref, got_ref, rows_ref, scale_ref, turned_ref):
    own, got = own_ref[...], got_ref[...]
    both = own + got
    scale_ref[...] = lax.rsqrt((both[WIN:TALL] + both[TALL + WIN :]) / count + epsilon)
    is_first = at_ref[1] == 0
    zero = jnp.where(is_first, own, got)
    one = jnp.where(is_first, got, own)
    rows = jnp.concatenate([zero[:TALL], zero[TALL:], one[:TALL], one[TALL:]], axis=1)
    first = at_ref[2] * ROWS
    shift = (TALL - (first - row_start(first))) % TALL
    rows = pltpu.roll(rows, shift, 0)
    rows_ref[...] = rows
    narrow = rows.astype(jnp.bfloat16)
    turned_ref[: K // ROWS] = jnp.zeros((K // ROWS, TALL, TALL), turned_ref.dtype)
    line = lax.broadcasted_iota(jnp.int32, (TALL, 2 * SUBJ), 0)
    lane = lax.broadcasted_iota(jnp.int32, (TALL, 2 * SUBJ), 1)
    for g in range(K // ROWS, GRP):
        pick = jnp.where(line + (g * ROWS - K) == lane, 1.0, 0.0).astype(jnp.bfloat16)
        turned_ref[g] = lax.dot_general(pick, narrow, NT, preferred_element_type=jnp.float32).astype(turned_ref.dtype)


def assemble_kernel(masked, at_ref, back_ref, rows_ref, scale_ref, zero_ref, one_ref, two_ref, three_ref, out_ref, basis, cross):
    x, core, grp = at_ref[0], at_ref[1], at_ref[2]
    first = grp * ROWS
    shares = (zero_ref, one_ref, two_ref, three_ref)
    basis[...] = jnp.zeros_like(basis)
    cross[...] = jnp.zeros_like(cross)
    line = lax.broadcasted_iota(jnp.int32, (SHARE, 384), 0)
    lane = lax.broadcasted_iota(jnp.int32, (SHARE, 384), 1)
    for k in range(4):
        for c, which in ((0, core), (1, 1 - core)):
            part = (x - k + 4) % 4 * 2 + which
            begin = part * PART // RUN * RUN
            put = jnp.where((line + (part * PART - begin) == lane) & (line < PART), 1.0, 0.0).astype(jnp.bfloat16)
            cols = pl.ds(pl.multiple_of(begin, RUN), 384)
            basis[:, cols] += lax.dot_general(
                shares[k][c], put, (((0,), (0,)), ((), ())), preferred_element_type=jnp.float32
            )
    line = lax.broadcasted_iota(jnp.int32, (TALL, 256), 0)
    lane = lax.broadcasted_iota(jnp.int32, (TALL, 256), 1)
    for g in range(K // ROWS + 1):
        begin = g * ROWS // RUN * RUN
        ok = (line + (g * ROWS - begin) == lane) & (line < ROWS) & (line + g * ROWS < K)
        put = jnp.where(ok, 1.0, 0.0).astype(jnp.bfloat16)
        cross[:, begin : begin + 256] += jnp.dot(back_ref[g], put, preferred_element_type=jnp.float32)
    width = 1792
    row = first + lax.broadcasted_iota(jnp.int32, (TALL, 1), 0)
    left = jnp.where(row < K, basis[...], cross[...])
    base = K // RUN * RUN
    right = pltpu.roll(
        jnp.concatenate([rows_ref[...], jnp.zeros((TALL, RUN), jnp.float32)], axis=1), K - base, 1
    )
    zero, one = scale_ref[0:1, 0:1], scale_ref[1:2, 0:1]
    of_row = jnp.where(row < K, 1.0, jnp.where(row < K + SUBJ, zero, one))
    col = lax.broadcasted_iota(jnp.int32, (1, width), 1)
    of_col = jnp.where(col < K, 1.0, jnp.where(col < K + SUBJ, zero, one))
    out_ref[:, :base] = (left[:, :base] * (of_row * of_col[:, :base]) / masked)[:ROWS]
    edge = jnp.concatenate([left[:, base:], jnp.zeros((TALL, width - left.shape[1]), jnp.float32)], axis=1)
    values = jnp.where(col[:, base:] < K, edge, right)
    out_ref[:, base:] = (values * (of_row * of_col[:, base:]) / masked)[:ROWS, : KX - base]


def rotate_kernel(tile, scale_ref, base_ref, turn_ref, cen_ref, out_ref, held, sems):
    step = pl.program_id(0)
    steps = pl.num_programs(0)

    def fetch(i):
        rows = pl.ds(pl.multiple_of(i * tile, 8), tile)
        return pltpu.make_async_copy(base_ref.at[rows], held.at[i % 2], sems.at[i % 2])

    @pl.when(step == 0)
    def _():
        fetch(step).start()

    @pl.when(step + 1 < steps)
    def _():
        fetch(step + 1).start()

    fetch(step).wait()
    slot = step % 2
    for lo in range(0, out_ref.shape[1], 256):
        cols = slice(lo, lo + 256)
        first = jnp.dot(turn_ref[:, :SUBJ], cen_ref[0, :, cols], preferred_element_type=jnp.float32)
        second = jnp.dot(turn_ref[:, SUBJ:], cen_ref[1, :, cols], preferred_element_type=jnp.float32)
        base = held[slot, :, cols]
        out_ref[:, cols] = (base + scale_ref[0:1, 0:1] * first + scale_ref[1:2, 0:1] * second).astype(out_ref.dtype)


def copies(value, axis, count):
    return lax.all_to_all(jnp.broadcast_to(value[None], (count, *value.shape)), axis, 0, 0, tiled=True)


def body(raw_frames, mask_index, subspace, rotation):
    depth = raw_frames.shape[1]
    extent = raw_frames.shape[2]
    per_device = subspace.shape[1]
    slab = ("x", "core")
    masked = per_device * 8 * GRP
    bf16 = jnp.bfloat16
    f32 = jnp.float32
    like = jax.ShapeDtypeStruct
    swap = [(0, 1), (1, 0)]
    turns = [[(i, (i + k) % 4) for i in range(4)] for k in range(4)]
    at = jnp.stack([lax.axis_index("x"), lax.axis_index("core"), lax.axis_index("grp")]).astype(jnp.int32)

    slab_at = lax.axis_index("x") * 2 + lax.axis_index("core")
    tiles = mask_index.reshape(-1, RUN)[:, 0] // RUN - slab_at * (depth * extent // RUN)
    up = [(i, i + 1) for i in range(7)]
    down = [(i + 1, i) for i in range(7)]
    packed = jnp.stack([tiles, lax.ppermute(tiles, slab, up), lax.ppermute(tiles, slab, down)])
    raw, _ = lax.optimization_barrier((jnp.transpose(raw_frames, (1, 0, 2)), packed))
    planar = filter_planes(raw)
    every, planar = lax.optimization_barrier((copies(packed, "grp", GRP), planar))
    own = every[:, 0].reshape(-1)
    near = jnp.concatenate([every[: GRP // 4, 2].reshape(-1), every[3 * GRP // 4 :, 1].reshape(-1)])

    middles, rim, to_up, to_down = filter_depth(own, near, planar)
    at_ss, _ = lax.optimization_barrier((at, to_down))
    held = [pltpu.VMEM((4 * WIDE, per_device), bf16)]
    other_ss = pl.pallas_call(
        basis_other_kernel,
        out_shape=like((4 * WIDE, K), bf16),
        in_specs=[smem(), *vmem(1)],
        out_specs=vmem(1)[0],
        scratch_shapes=held,
        compiler_params=params(24),
        name="basis_other",
    )(at_ss, subspace)
    from_low, from_high, other_ss = lax.optimization_barrier(
        (lax.ppermute(to_up, slab, up), lax.ppermute(to_down, slab, down), other_ss)
    )
    placed = pl.pallas_call(
        rim_kernel,
        out_shape=like(middles.shape, bf16),
        in_specs=[*vmem(3), hbm()],
        out_specs=hbm(),
        scratch_shapes=[pltpu.VMEM(rim.shape, bf16), pltpu.SemaphoreType.DMA((2,))],
        input_output_aliases={3: 0},
        compiler_params=params(16),
        name="rim",
    )(rim, from_low, from_high, middles)
    regrouped = lax.all_to_all(placed, "grp", 0, 0, tiled=True)

    got_ss = lax.ppermute(other_ss, "core", swap)
    own_ss, next_ss, far_ss, back_ss = pl.pallas_call(
        basis_own_kernel,
        out_shape=[like((WIDE, K), bf16), like((WIDE, K), bf16), like((2, HALF, K), bf16), like((WIDE, K), bf16)],
        in_specs=[smem(), *vmem(2)],
        out_specs=vmem(4),
        scratch_shapes=held,
        compiler_params=params(24),
        name="basis_own",
    )(at_ss, subspace, got_ss)
    ahead, behind = turns[1], turns[3]
    next_ss, back_ss = pl.pallas_call(
        basis_relay_kernel,
        out_shape=[like((WIDE, K), bf16)] * 2,
        in_specs=vmem(4),
        out_specs=vmem(2),
        compiler_params=params(16),
        name="basis_relay",
    )(next_ss, back_ss, lax.ppermute(far_ss[0], "x", ahead), lax.ppermute(far_ss[1], "x", behind))
    regrouped, _, _ = lax.optimization_barrier((regrouped, next_ss, back_ss))
    by_row = pl.pallas_call(
        basis_rows_kernel,
        out_shape=like((GRP, SHARE, RUN), bf16),
        in_specs=[smem(), *vmem(3)],
        out_specs=vmem(1)[0],
        scratch_shapes=[pltpu.VMEM((WIDE, 1408), f32)],
        compiler_params=params(16),
        name="basis_rows",
    )(at, own_ss, lax.ppermute(next_ss, "x", ahead), lax.ppermute(back_ss, "x", behind))

    centered, other_c, own_c, power = pl.pallas_call(
        columns_kernel,
        out_shape=[like((2, SUBJ, per_device), bf16), like((KX, SUBJ), bf16), like((KX, SUBJ), f32), like((8, RUN), f32)],
        in_specs=[smem(), *vmem(1), hbm()],
        out_specs=[hbm(), *vmem(1), hbm(), *vmem(1)],
        scratch_shapes=[
            pltpu.VMEM((K, per_device), bf16),
            pltpu.VMEM((2, SUBJ, per_device), bf16),
            pltpu.VMEM((KX, SUBJ), f32),
            pltpu.SemaphoreType.DMA((3,)),
        ],
        compiler_params=params(47),
        name="columns",
    )(at, regrouped, subspace)
    sent = pl.pallas_call(
        windows_kernel,
        out_shape=like((GRP, 2 * TALL + SHARE, RUN), bf16),
        in_specs=[hbm(), *vmem(3)],
        out_specs=vmem(1)[0],
        scratch_shapes=[pltpu.VMEM((KX, SUBJ), f32), pltpu.SemaphoreType.DMA],
        compiler_params=params(16),
        name="windows",
    )(own_c, lax.ppermute(other_c, "core", swap), power, by_row)
    summed = lax.all_to_all(sent, "grp", 0, 0, tiled=True)

    rotation_b, _ = lax.optimization_barrier((rotation, sent))
    contract = (((0,), (0,)), ((), ()))
    from_basis = lax.dot_general(rotation_b[:K], subspace, contract, preferred_element_type=f32)
    summed, from_basis, turn = lax.optimization_barrier((summed, from_basis, rotation_b[K:].T))

    total, share = pl.pallas_call(
        total_kernel,
        out_shape=[like((2 * TALL, RUN), bf16), like((SHARE, RUN), bf16)],
        in_specs=vmem(1),
        out_specs=vmem(2),
        compiler_params=params(16),
        name="total",
    )(summed)
    sum_c = pl.pallas_call(
        slab_kernel,
        out_shape=like((2 * TALL, RUN), f32),
        in_specs=vmem(4),
        out_specs=vmem(1)[0],
        compiler_params=params(16),
        name="slab",
    )(total, *[lax.ppermute(total, "x", turns[k]) for k in range(1, 4)])
    share = jnp.stack([share, lax.ppermute(share, "core", swap)])
    rows_c, scales, turned = pl.pallas_call(
        functools.partial(finish_kernel, float(masked * SUBJ)),
        out_shape=[like((TALL, 2 * SUBJ), f32), like((8, RUN), f32), like((GRP, TALL, TALL), bf16)],
        in_specs=[smem(), *vmem(2)],
        out_specs=vmem(3),
        compiler_params=params(16),
        name="finish",
    )(at, sum_c, lax.ppermute(sum_c, "core", swap))

    back = lax.all_to_all(turned, "grp", 0, 0, tiled=True)
    share, _ = lax.optimization_barrier((share, turned))
    gram_rows = pl.pallas_call(
        functools.partial(assemble_kernel, float(masked)),
        out_shape=like((ROWS, KX), f32),
        in_specs=[smem(), *vmem(7)],
        out_specs=vmem(1)[0],
        scratch_shapes=[pltpu.VMEM((TALL, 1408), f32), pltpu.VMEM((TALL, 1408), f32)],
        compiler_params=params(16),
        name="assemble",
    )(at, back, rows_c, scales, share, *[lax.ppermute(share, "x", turns[k]) for k in range(1, 4)])

    tile = 240
    new_subspace = pl.pallas_call(
        functools.partial(rotate_kernel, tile),
        out_shape=like((K, per_device), bf16),
        grid=(K // tile,),
        in_specs=[
            pl.BlockSpec((8, RUN), lambda i: (0, 0)),
            hbm(),
            pl.BlockSpec((tile, 2 * SUBJ), lambda i: (i, 0)),
            pl.BlockSpec((2, SUBJ, per_device), lambda i: (0, 0, 0)),
        ],
        out_specs=pl.BlockSpec((tile, per_device), lambda i: (i, 0)),
        scratch_shapes=[pltpu.VMEM((2, tile, per_device), f32), pltpu.SemaphoreType.DMA((2,))],
        compiler_params=params(BIG),
        name="rotate",
    )(scales, from_basis, turn, centered)
    return (gram_rows, new_subspace)


def solution(mesh):
    fine = Mesh(mesh.devices.reshape(4, 2, GRP), ("x", "core", "grp"))
    slab = ("x", "core")
    placed = (P("grp", slab, None), P((*slab, "grp")), P(None, (*slab, "grp")), P())
    return jax.shard_map(
        body,
        mesh=fine,
        in_specs=placed,
        out_specs=(P("grp", None), P(None, (*slab, "grp"))),
        check_vma=False,
    )
```

```python
import functools
import math

import jax
import jax.numpy as jnp
import numpy as np
from jax import lax
from jax.experimental import pallas as pl
from jax.experimental.pallas import tpu as pltpu
from jax.sharding import Mesh
from jax.sharding import PartitionSpec as P


NX = 96
RUN = 128
RAD = 3
K = 1200
KX = 1712
SUBJ = 256
ROWS = 107
WIN = 120
TALL = 128
PART = 150
WIDE = 176
SHARE = 152
SMOOTH_MIB = 48
BIG = 56
LEAD = 384
BLOCK = 256
PHASES = 3
GRP = 16
TAB = 64
TAB_MID = 31

smooth_sigma = 1.0617
epsilon = 1e-06


def tap_weights():
    unscaled = [
        math.exp(-offset * offset / (2.0 * smooth_sigma * smooth_sigma))
        for offset in range(-RAD, RAD + 1)
    ]
    summed = sum(unscaled)
    return [weight / summed for weight in unscaled]


def plane_matrix():
    taps = np.array(tap_weights())
    cells_in = np.arange(LEAD + BLOCK + LEAD)[:, None]
    cells_out = np.arange(BLOCK)[None, :]
    parts = []
    for phase in range(PHASES):
        column = (phase * BLOCK + cells_out) % NX
        reach = cells_in - LEAD - cells_out
        rows = np.floor((reach + NX // 2) / NX).astype(np.int64)
        along = reach - rows * NX
        ok = (np.abs(rows) <= RAD) & (np.abs(along) <= RAD) & (column + along >= 0) & (column + along < NX)
        weight = taps[np.clip(rows + RAD, 0, 2 * RAD)] * taps[np.clip(along + RAD, 0, 2 * RAD)]
        parts.append(np.where(ok, weight, 0.0))
    return np.stack(parts).astype(np.float32)


def depth_table():
    table = np.zeros((TAB,), np.float32)
    table[TAB_MID - RAD : TAB_MID + RAD + 1] = tap_weights()
    return table


def smooth_kernel(own_ref, near_ref, tab_ref, taps_ref, raw_ref, all_ref, rim_ref, up_ref, down_ref, pad, planar, mid_ref, mat_ref, sems, mid_sem, mat_sem):
    depth, frames, extent = raw_ref.shape
    step = PHASES * BLOCK
    steps = extent // step
    tiles = extent // RUN

    def fetch(i):
        return pltpu.make_async_copy(
            raw_ref.at[:, :, pl.ds(i * step, step)],
            pad.at[:, :, pl.ds(LEAD + i * step, step)],
            sems.at[i],
        )

    plan = pltpu.make_async_copy(taps_ref, mat_ref, mat_sem)
    plan.start()
    for i in range(steps):
        fetch(i).start()
    edge = jnp.zeros((depth, frames, LEAD), pad.dtype)
    pad[:, :, :LEAD] = edge
    pad[:, :, LEAD + extent :] = edge
    plan.wait()
    fetch(0).wait()

    def block(i, carry):
        @pl.when(i + 1 < steps)
        def _():
            fetch(i + 1).wait()

        for phase in range(PHASES):
            start = pl.multiple_of(i * step + phase * BLOCK, BLOCK)
            cells = pad[:, :, pl.ds(start, LEAD + BLOCK + LEAD)].reshape(depth * frames, LEAD + BLOCK + LEAD)
            out = jnp.dot(cells, mat_ref[phase], preferred_element_type=jnp.float32)
            planar[:, :, pl.ds(start, BLOCK)] = out.reshape(depth, frames, BLOCK)
        return carry

    lax.fori_loop(0, steps, block, 0)

    taps = tap_weights()

    def place(tile):
        plane = tile // tiles
        return plane, pl.multiple_of((tile - plane * tiles) * RUN, RUN)

    per = mid_ref.shape[2] // RUN

    def middle(g, carry):
        for j in range(per):
            plane, lane = place(own_ref[(g + GRP // 4) * per + j])
            total = taps[0] * planar[plane - RAD, :, pl.ds(lane, RUN)]
            for k in range(1, 2 * RAD + 1):
                total = total + taps[k] * planar[plane - RAD + k, :, pl.ds(lane, RUN)]
            mid_ref[g, :, j * RUN : (j + 1) * RUN] = total.astype(mid_ref.dtype)
        return carry

    def some(tile, first, count, shift):
        plane, lane = place(tile)
        total = None
        for q in range(first, first + count):
            weight = tab_ref[q - plane + shift + TAB_MID]
            term = weight * planar[q, :, pl.ds(lane, RUN)]
            total = term if total is None else total + term
        return total

    def rims(g, carry):
        for j in range(per):
            cols = slice(j * RUN, (j + 1) * RUN)
            at = g * per + j
            up_ref[g, :, cols] = some(near_ref[at], depth - RAD, RAD, -depth).astype(up_ref.dtype)
            down_ref[g, :, cols] = some(near_ref[GRP // 4 * per + at], 0, RAD, depth).astype(down_ref.dtype)
            rim_ref[g, :, cols] = some(own_ref[at], 0, 2 * RAD, 0)
            rim_ref[GRP // 4 + g, :, cols] = some(own_ref[GRP * 3 // 4 * per + at], depth - 2 * RAD, 2 * RAD, 0)
        return carry

    lax.fori_loop(0, GRP // 2, middle, 0)
    keep = pltpu.make_async_copy(mid_ref, all_ref.at[GRP // 4 : GRP * 3 // 4], mid_sem)
    keep.start()
    lax.fori_loop(0, GRP // 4, rims, 0)
    keep.wait()


def smooth(own, near, raw):
    depth, frames, extent = raw.shape
    per_device = own.shape[0] // GRP * RUN
    quarter = (GRP // 4, frames, per_device)
    half = (GRP // 2, frames, per_device)
    return pl.pallas_call(
        smooth_kernel,
        out_shape=[
            jax.ShapeDtypeStruct((GRP, frames, per_device), jnp.bfloat16),
            jax.ShapeDtypeStruct(half, jnp.float32),
            jax.ShapeDtypeStruct(quarter, jnp.bfloat16),
            jax.ShapeDtypeStruct(quarter, jnp.bfloat16),
        ],
        in_specs=[smem()] * 3 + [hbm(), hbm()],
        out_specs=[hbm(), *vmem(3)],
        scratch_shapes=[
            pltpu.VMEM((depth, frames, extent + 2 * LEAD), jnp.bfloat16),
            pltpu.VMEM((depth, frames, extent), jnp.float32),
            pltpu.VMEM(half, jnp.bfloat16),
            pltpu.VMEM((PHASES, LEAD + BLOCK + LEAD, BLOCK), jnp.bfloat16),
            pltpu.SemaphoreType.DMA((extent // (PHASES * BLOCK),)),
            pltpu.SemaphoreType.DMA,
            pltpu.SemaphoreType.DMA,
        ],
        compiler_params=params(SMOOTH_MIB),
        name="smooth",
    )(own, near, jnp.asarray(depth_table()), jnp.asarray(plane_matrix()).astype(jnp.bfloat16), raw)


NT = (((1,), (1,)), ((), ()))


def row_start(first):
    return min(first // 8 * 8, KX - WIN) if isinstance(first, int) else jnp.minimum(first // 8 * 8, KX - WIN)


def part_start(part):
    return jnp.minimum(part * PART // 16 * 16, K - WIDE)


def vmem(count):
    return [pl.BlockSpec(memory_space=pltpu.VMEM)] * count


def smem():
    return pl.BlockSpec(memory_space=pltpu.SMEM)


def params(mib):
    return pltpu.CompilerParams(vmem_limit_bytes=mib * 1024 * 1024)


def hbm():
    return pl.BlockSpec(memory_space=pltpu.HBM)


HALF = WIDE // 2


def gather_parts(x, which, sub_ref, left):
    for k in range(4):
        start = pl.multiple_of(part_start((x + k) % 4 * 2 + which), 16)
        left[k * WIDE : (k + 1) * WIDE, :] = sub_ref[pl.ds(start, WIDE), :]


def basis_other_kernel(at_ref, sub_ref, out_ref, left):
    gather_parts(at_ref[0], 1 - at_ref[1], sub_ref, left)
    out_ref[...] = lax.dot_general(left[...], sub_ref[...], NT, preferred_element_type=jnp.float32).astype(out_ref.dtype)


def basis_own_kernel(at_ref, sub_ref, got_ref, own_ref, next_ref, far_ref, back_ref, left):
    gather_parts(at_ref[0], at_ref[1], sub_ref, left)
    part = lax.dot_general(left[...], sub_ref[...], NT, preferred_element_type=jnp.float32)
    part = (part + got_ref[...].astype(jnp.float32)).astype(own_ref.dtype)
    own_ref[...] = part[:WIDE]
    next_ref[...] = part[WIDE : 2 * WIDE]
    far_ref[...] = part[2 * WIDE : 3 * WIDE].reshape(2, HALF, K)
    back_ref[...] = part[3 * WIDE :]


def basis_relay_kernel(next_ref, back_ref, low_ref, high_ref, next_out, back_out):
    next_out[:HALF] = (next_ref[:HALF].astype(jnp.float32) + low_ref[...].astype(jnp.float32)).astype(next_out.dtype)
    next_out[HALF:] = next_ref[HALF:]
    back_out[:HALF] = back_ref[:HALF]
    back_out[HALF:] = (back_ref[HALF:].astype(jnp.float32) + high_ref[...].astype(jnp.float32)).astype(back_out.dtype)


def basis_rows_kernel(at_ref, a_ref, b_ref, c_ref, out_ref, flat):
    part = at_ref[0] * 2 + at_ref[1]
    total = a_ref[...].astype(jnp.float32) + b_ref[...].astype(jnp.float32) + c_ref[...].astype(jnp.float32)
    flat[:, K // RUN * RUN :] = jnp.zeros((flat.shape[0], flat.shape[1] - K // RUN * RUN), jnp.float32)
    flat[:, :K] = total
    shift = (WIDE - (part * PART - part_start(part))) % WIDE
    narrow = pltpu.roll(flat[...], shift, 0)[:SHARE].astype(jnp.bfloat16)
    line = lax.broadcasted_iota(jnp.int32, (256, RUN), 0)
    lane = lax.broadcasted_iota(jnp.int32, (256, RUN), 1)
    for g in range(GRP):
        begin = g * ROWS // RUN * RUN
        if g * ROWS < K:
            pick = jnp.where((line == lane + (g * ROWS - begin)) & (lane < ROWS), 1.0, 0.0).astype(jnp.bfloat16)
            out_ref[g] = jnp.dot(narrow[:, begin : begin + 256], pick, preferred_element_type=jnp.float32).astype(
                out_ref.dtype
            )
        else:
            out_ref[g] = jnp.zeros((SHARE, RUN), out_ref.dtype)


def rim_kernel(rim_ref, low_ref, high_ref, all_ref, out_ref, made, sems):
    del all_ref
    quarter = GRP // 4
    made[:quarter] = (rim_ref[:quarter] + low_ref[...].astype(jnp.float32)).astype(made.dtype)
    first = pltpu.make_async_copy(made.at[:quarter], out_ref.at[:quarter], sems.at[0])
    first.start()
    made[quarter:] = (rim_ref[quarter:] + high_ref[...].astype(jnp.float32)).astype(made.dtype)
    second = pltpu.make_async_copy(made.at[quarter:], out_ref.at[3 * quarter :], sems.at[1])
    second.start()
    first.wait()
    second.wait()


def columns_kernel(at_ref, got_ref, basis_ref, cen_out, other_ref, own_out, power_ref, sub_ref, cen_ref, own_ref, sems):
    per_device = sub_ref.shape[1]
    core = at_ref[1]
    each = GRP // 2
    fetch = pltpu.make_async_copy(basis_ref, sub_ref, sems.at[0])
    fetch.start()

    def centre(i, sums):
        cols = pl.ds(pl.multiple_of(i * RUN, RUN), RUN)
        new = []
        for s in range(2):
            wide = got_ref[s * each : (s + 1) * each, :, cols].reshape(SUBJ, RUN).astype(jnp.float32)
            mean = jnp.sum(wide, axis=0, keepdims=True) * (1.0 / SUBJ)
            cen = (wide - mean).astype(cen_ref.dtype)
            cen_ref[s, :, cols] = cen
            back = cen.astype(jnp.float32)
            new.append(sums[s] + jnp.sum((back * back).reshape(SUBJ // 8, 8, RUN), axis=0))
        return tuple(new)

    zero = jnp.zeros((8, RUN), jnp.float32)
    sums = lax.fori_loop(0, per_device // RUN, centre, (zero, zero))
    keep = pltpu.make_async_copy(cen_ref, cen_out, sems.at[1])
    keep.start()
    line = lax.broadcasted_iota(jnp.int32, (8, RUN), 0)
    first = jnp.sum(sums[0], keepdims=True)
    second = jnp.sum(sums[1], keepdims=True)
    power_ref[...] = jnp.where(line == 0, first, jnp.where(line == 1, second, 0.0))

    fetch.wait()
    for which, out in ((core, own_ref), (1 - core, other_ref)):
        right = cen_ref[which]
        for lo in range(0, K, 400):
            out[lo : lo + 400, :] = lax.dot_general(
                sub_ref[lo : lo + 400, :], right, NT, preferred_element_type=jnp.float32
            ).astype(out.dtype)
        for s in range(2):
            lo = K + s * SUBJ
            out[lo : lo + SUBJ, :] = lax.dot_general(
                cen_ref[s], right, NT, preferred_element_type=jnp.float32
            ).astype(out.dtype)
        if out is own_ref:
            leave = pltpu.make_async_copy(own_ref, own_out, sems.at[2])
            leave.start()
    leave.wait()
    keep.wait()


def write_power(power, put):
    high = power.astype(jnp.bfloat16)
    put(slice(WIN, TALL), high)
    put(slice(TALL + WIN, 2 * TALL), (power - high.astype(jnp.float32)).astype(jnp.bfloat16))


def windows_kernel(own_ref, got_ref, power_ref, basis_ref, out_ref, whole, sem):
    fetch = pltpu.make_async_copy(own_ref, whole, sem)
    fetch.start()
    for g in range(GRP):
        out_ref[g, 2 * TALL :, :] = basis_ref[g]

        def put(rows, value, g=g):
            out_ref[g, rows, :] = value

        write_power(power_ref[...], put)
    fetch.wait()
    whole[...] = whole[...] + got_ref[...].astype(jnp.float32)
    for g in range(GRP):
        first = row_start(g * ROWS)
        for half in range(2):
            out_ref[g, half * TALL : half * TALL + WIN, :] = whole[
                first : first + WIN, half * RUN : (half + 1) * RUN
            ].astype(out_ref.dtype)


def total_kernel(got_ref, out_ref):
    total = got_ref[0].astype(jnp.float32)
    for g in range(1, GRP):
        total = total + got_ref[g].astype(jnp.float32)
    out_ref[...] = total.astype(out_ref.dtype)

    def put(rows, value):
        out_ref[rows, :] = value

    write_power(total[WIN:TALL] + total[TALL + WIN : 2 * TALL], put)


def slab_kernel(a_ref, b_ref, c_ref, d_ref, sum_ref, share_ref):
    refs = (a_ref, b_ref, c_ref, d_ref)
    total = refs[0][: 2 * TALL].astype(jnp.float32)
    for ref in refs[1:]:
        total = total + ref[: 2 * TALL].astype(jnp.float32)
    sum_ref[...] = total
    for k in range(4):
        share_ref[k] = refs[k][2 * TALL :]


def finish_kernel(count, at_ref, own_ref, got_ref, rows_ref, scale_ref, turned_ref):
    own, got = own_ref[...], got_ref[...]
    both = own + got
    scale_ref[...] = lax.rsqrt((both[WIN:TALL] + both[TALL + WIN :]) / count + epsilon)
    is_first = at_ref[1] == 0
    zero = jnp.where(is_first, own, got)
    one = jnp.where(is_first, got, own)
    rows = jnp.concatenate([zero[:TALL], zero[TALL:], one[:TALL], one[TALL:]], axis=1)
    first = at_ref[2] * ROWS
    shift = (TALL - (first - row_start(first))) % TALL
    rows = pltpu.roll(rows, shift, 0)
    rows_ref[...] = rows
    narrow = rows.astype(jnp.bfloat16)
    turned_ref[: K // ROWS] = jnp.zeros((K // ROWS, TALL, TALL), turned_ref.dtype)
    line = lax.broadcasted_iota(jnp.int32, (TALL, 2 * SUBJ), 0)
    lane = lax.broadcasted_iota(jnp.int32, (TALL, 2 * SUBJ), 1)
    for g in range(K // ROWS, GRP):
        pick = jnp.where(line + (g * ROWS - K) == lane, 1.0, 0.0).astype(jnp.bfloat16)
        turned_ref[g] = lax.dot_general(pick, narrow, NT, preferred_element_type=jnp.float32).astype(turned_ref.dtype)


def assemble_kernel(masked, at_ref, back_ref, rows_ref, scale_ref, mine_ref, other_ref, out_ref, basis, cross):
    x, core, grp = at_ref[0], at_ref[1], at_ref[2]
    first = grp * ROWS
    basis[...] = jnp.zeros_like(basis)
    cross[...] = jnp.zeros_like(cross)
    line = lax.broadcasted_iota(jnp.int32, (SHARE, 384), 0)
    lane = lax.broadcasted_iota(jnp.int32, (SHARE, 384), 1)
    for k in range(4):
        for share, which in ((mine_ref, core), (other_ref, 1 - core)):
            part = (x - k + 4) % 4 * 2 + which
            begin = part * PART // RUN * RUN
            put = jnp.where((line + (part * PART - begin) == lane) & (line < PART), 1.0, 0.0).astype(jnp.bfloat16)
            cols = pl.ds(pl.multiple_of(begin, RUN), 384)
            basis[:, cols] += lax.dot_general(
                share[k], put, (((0,), (0,)), ((), ())), preferred_element_type=jnp.float32
            )
    line = lax.broadcasted_iota(jnp.int32, (TALL, 256), 0)
    lane = lax.broadcasted_iota(jnp.int32, (TALL, 256), 1)
    for g in range(K // ROWS + 1):
        begin = g * ROWS // RUN * RUN
        ok = (line + (g * ROWS - begin) == lane) & (line < ROWS) & (line + g * ROWS < K)
        put = jnp.where(ok, 1.0, 0.0).astype(jnp.bfloat16)
        cross[:, begin : begin + 256] += jnp.dot(back_ref[g], put, preferred_element_type=jnp.float32)
    width = 1792
    row = first + lax.broadcasted_iota(jnp.int32, (TALL, 1), 0)
    left = jnp.where(row < K, basis[...], cross[...])
    base = K // RUN * RUN
    right = pltpu.roll(
        jnp.concatenate([rows_ref[...], jnp.zeros((TALL, RUN), jnp.float32)], axis=1), K - base, 1
    )
    zero, one = scale_ref[0:1, 0:1], scale_ref[1:2, 0:1]
    of_row = jnp.where(row < K, 1.0, jnp.where(row < K + SUBJ, zero, one))
    col = lax.broadcasted_iota(jnp.int32, (1, width), 1)
    of_col = jnp.where(col < K, 1.0, jnp.where(col < K + SUBJ, zero, one))
    out_ref[:, :base] = (left[:, :base] * (of_row * of_col[:, :base]) / masked)[:ROWS]
    edge = jnp.concatenate([left[:, base:], jnp.zeros((TALL, width - left.shape[1]), jnp.float32)], axis=1)
    values = jnp.where(col[:, base:] < K, edge, right)
    out_ref[:, base:] = (values * (of_row * of_col[:, base:]) / masked)[:ROWS, : KX - base]


def rotate_kernel(tile, scale_ref, base_ref, turn_ref, cen_ref, out_ref, held, sems):
    step = pl.program_id(0)
    steps = pl.num_programs(0)

    def fetch(i):
        rows = pl.ds(pl.multiple_of(i * tile, 16), tile)
        return pltpu.make_async_copy(base_ref.at[rows], held.at[i % 2], sems.at[i % 2])

    @pl.when(step == 0)
    def _():
        fetch(step).start()

    @pl.when(step + 1 < steps)
    def _():
        fetch(step + 1).start()

    fetch(step).wait()
    slot = step % 2
    for lo in range(0, out_ref.shape[1], 256):
        cols = slice(lo, lo + 256)
        first = jnp.dot(turn_ref[:, :SUBJ], cen_ref[0, :, cols], preferred_element_type=jnp.float32)
        second = jnp.dot(turn_ref[:, SUBJ:], cen_ref[1, :, cols], preferred_element_type=jnp.float32)
        base = held[slot, :, cols].astype(jnp.float32)
        out_ref[:, cols] = (base + scale_ref[0:1, 0:1] * first + scale_ref[1:2, 0:1] * second).astype(out_ref.dtype)


def copies(value, axis, count):
    return lax.all_to_all(jnp.broadcast_to(value[None], (count, *value.shape)), axis, 0, 0, tiled=True)


def body(raw_frames, mask_index, subspace, rotation):
    depth = raw_frames.shape[1]
    extent = raw_frames.shape[2]
    per_device = subspace.shape[1]
    slab = ("x", "core")
    masked = per_device * 8 * GRP
    bf16 = jnp.bfloat16
    f32 = jnp.float32
    like = jax.ShapeDtypeStruct
    swap = [(0, 1), (1, 0)]
    turns = [[(i, (i + k) % 4) for i in range(4)] for k in range(4)]
    at = jnp.stack([lax.axis_index("x"), lax.axis_index("core"), lax.axis_index("grp")]).astype(jnp.int32)

    slab_at = lax.axis_index("x") * 2 + lax.axis_index("core")
    tiles = mask_index.reshape(-1, RUN)[:, 0] // RUN - slab_at * (depth * extent // RUN)
    up = [(i, i + 1) for i in range(7)]
    down = [(i + 1, i) for i in range(7)]
    packed = jnp.stack([tiles, lax.ppermute(tiles, slab, up), lax.ppermute(tiles, slab, down)])
    at_ss, _ = lax.optimization_barrier((at, packed))
    held = [pltpu.VMEM((4 * WIDE, per_device), bf16)]
    other_ss = pl.pallas_call(
        basis_other_kernel,
        out_shape=like((4 * WIDE, K), bf16),
        in_specs=[smem(), *vmem(1)],
        out_specs=vmem(1)[0],
        scratch_shapes=held,
        compiler_params=params(24),
        name="basis_other",
    )(at_ss, subspace)
    every, other_ss = lax.optimization_barrier((copies(packed, "grp", GRP), other_ss))
    own = every[:, 0].reshape(-1)
    near = jnp.concatenate([every[: GRP // 4, 2].reshape(-1), every[3 * GRP // 4 :, 1].reshape(-1)])

    middles, rim, to_up, to_down = smooth(own, near, jnp.transpose(raw_frames, (1, 0, 2)))
    from_low, from_high = lax.ppermute(to_up, slab, up), lax.ppermute(to_down, slab, down)
    placed = pl.pallas_call(
        rim_kernel,
        out_shape=like(middles.shape, bf16),
        in_specs=[*vmem(3), hbm()],
        out_specs=hbm(),
        scratch_shapes=[pltpu.VMEM(rim.shape, bf16), pltpu.SemaphoreType.DMA((2,))],
        input_output_aliases={3: 0},
        compiler_params=params(16),
        name="rim",
    )(rim, from_low, from_high, middles)
    regrouped = lax.all_to_all(placed, "grp", 0, 0, tiled=True)

    got_ss = lax.ppermute(other_ss, "core", swap)
    at_own, _ = lax.optimization_barrier((at, placed))
    own_ss, next_ss, far_ss, back_ss = pl.pallas_call(
        basis_own_kernel,
        out_shape=[like((WIDE, K), bf16), like((WIDE, K), bf16), like((2, HALF, K), bf16), like((WIDE, K), bf16)],
        in_specs=[smem(), *vmem(2)],
        out_specs=vmem(4),
        scratch_shapes=held,
        compiler_params=params(24),
        name="basis_own",
    )(at_own, subspace, got_ss)
    ahead, behind = turns[1], turns[3]
    next_ss, back_ss = pl.pallas_call(
        basis_relay_kernel,
        out_shape=[like((WIDE, K), bf16)] * 2,
        in_specs=vmem(4),
        out_specs=vmem(2),
        compiler_params=params(16),
        name="basis_relay",
    )(next_ss, back_ss, lax.ppermute(far_ss[0], "x", ahead), lax.ppermute(far_ss[1], "x", behind))
    regrouped, _, _ = lax.optimization_barrier((regrouped, next_ss, back_ss))
    went_on = lax.ppermute(next_ss, "x", ahead)
    went_back = lax.ppermute(back_ss, "x", behind)
    by_row = pl.pallas_call(
        basis_rows_kernel,
        out_shape=like((GRP, SHARE, RUN), bf16),
        in_specs=[smem(), *vmem(3)],
        out_specs=vmem(1)[0],
        scratch_shapes=[pltpu.VMEM((WIDE, 1408), f32)],
        compiler_params=params(16),
        name="basis_rows",
    )(at, own_ss, went_on, went_back)

    centered, other_c, own_c, power = pl.pallas_call(
        columns_kernel,
        out_shape=[like((2, SUBJ, per_device), bf16), like((KX, SUBJ), bf16), like((KX, SUBJ), f32), like((8, RUN), f32)],
        in_specs=[smem(), *vmem(1), hbm()],
        out_specs=[hbm(), *vmem(1), hbm(), *vmem(1)],
        scratch_shapes=[
            pltpu.VMEM((K, per_device), bf16),
            pltpu.VMEM((2, SUBJ, per_device), bf16),
            pltpu.VMEM((KX, SUBJ), f32),
            pltpu.SemaphoreType.DMA((3,)),
        ],
        compiler_params=params(47),
        name="columns",
    )(at, regrouped, subspace)
    sent = pl.pallas_call(
        windows_kernel,
        out_shape=like((GRP, 2 * TALL + SHARE, RUN), bf16),
        in_specs=[hbm(), *vmem(3)],
        out_specs=vmem(1)[0],
        scratch_shapes=[pltpu.VMEM((KX, SUBJ), f32), pltpu.SemaphoreType.DMA],
        compiler_params=params(16),
        name="windows",
    )(own_c, lax.ppermute(other_c, "core", swap), power, by_row)
    summed = lax.all_to_all(sent, "grp", 0, 0, tiled=True)

    rotation_b, _ = lax.optimization_barrier((rotation, sent))
    contract = (((0,), (0,)), ((), ()))
    from_basis = lax.dot_general(rotation_b[:K], subspace, contract, preferred_element_type=f32).astype(bf16)
    summed, from_basis, turn = lax.optimization_barrier((summed, from_basis, rotation_b[K:].T))

    total = pl.pallas_call(
        total_kernel,
        out_shape=like((2 * TALL + SHARE, RUN), bf16),
        in_specs=vmem(1),
        out_specs=vmem(1)[0],
        compiler_params=params(16),
        name="total",
    )(summed)
    sum_c, share = pl.pallas_call(
        slab_kernel,
        out_shape=[like((2 * TALL, RUN), f32), like((4, SHARE, RUN), bf16)],
        in_specs=vmem(4),
        out_specs=vmem(2),
        compiler_params=params(16),
        name="slab",
    )(total, *[lax.ppermute(total, "x", turns[k]) for k in range(1, 4)])
    rows_c, scales, turned = pl.pallas_call(
        functools.partial(finish_kernel, float(masked * SUBJ)),
        out_shape=[like((TALL, 2 * SUBJ), f32), like((8, RUN), f32), like((GRP, TALL, TALL), bf16)],
        in_specs=[smem(), *vmem(2)],
        out_specs=vmem(3),
        compiler_params=params(16),
        name="finish",
    )(at, sum_c, lax.ppermute(sum_c, "core", swap))

    back = lax.all_to_all(turned, "grp", 0, 0, tiled=True)
    gram_rows = pl.pallas_call(
        functools.partial(assemble_kernel, float(masked)),
        out_shape=like((ROWS, KX), f32),
        in_specs=[smem(), *vmem(5)],
        out_specs=vmem(1)[0],
        scratch_shapes=[pltpu.VMEM((TALL, 1408), f32), pltpu.VMEM((TALL, 1408), f32)],
        compiler_params=params(16),
        name="assemble",
    )(at, back, rows_c, scales, share, lax.ppermute(share, "core", swap))

    tile = 240
    new_subspace = pl.pallas_call(
        functools.partial(rotate_kernel, tile),
        out_shape=like((K, per_device), bf16),
        grid=(K // tile,),
        in_specs=[
            pl.BlockSpec((8, RUN), lambda i: (0, 0)),
            hbm(),
            pl.BlockSpec((tile, 2 * SUBJ), lambda i: (i, 0)),
            pl.BlockSpec((2, SUBJ, per_device), lambda i: (0, 0, 0)),
        ],
        out_specs=pl.BlockSpec((tile, per_device), lambda i: (i, 0)),
        scratch_shapes=[pltpu.VMEM((2, tile, per_device), bf16), pltpu.SemaphoreType.DMA((2,))],
        compiler_params=params(BIG),
        name="rotate",
    )(scales, from_basis, turn, centered)
    return (gram_rows, new_subspace)


def solution(mesh):
    fine = Mesh(mesh.devices.reshape(4, 2, GRP), ("x", "core", "grp"))
    slab = ("x", "core")
    placed = (P("grp", slab, None), P((*slab, "grp")), P(None, (*slab, "grp")), P())
    return jax.shard_map(
        body,
        mesh=fine,
        in_specs=placed,
        out_specs=(P("grp", None), P(None, (*slab, "grp"))),
        check_vma=False,
    )
```

```python
import functools
import math

import jax
import jax.numpy as jnp
import numpy as np
from jax import lax
from jax.experimental import pallas as pl
from jax.experimental.pallas import tpu as pltpu
from jax.sharding import Mesh
from jax.sharding import PartitionSpec as P


NX = 96
RUN = 128
RAD = 3
K = 1200
KX = 1712
SUBJ = 256
ROWS = 107
WIN = 120
TALL = 128
PART = 150
WIDE = 176
SHARE = 152
SMOOTH_MIB = 48
BIG = 50
TURNED = 112
LEAD = 384
BLOCK = 256
PHASES = 3
GRP = 16
TAB = 64
TAB_MID = 31

smooth_sigma = 1.0617
epsilon = 1e-06


def tap_weights():
    unscaled = [
        math.exp(-offset * offset / (2.0 * smooth_sigma * smooth_sigma))
        for offset in range(-RAD, RAD + 1)
    ]
    summed = sum(unscaled)
    return [weight / summed for weight in unscaled]


def plane_matrix():
    taps = np.array(tap_weights())
    cells_in = np.arange(LEAD + BLOCK + LEAD)[:, None]
    cells_out = np.arange(BLOCK)[None, :]
    parts = []
    for phase in range(PHASES):
        column = (phase * BLOCK + cells_out) % NX
        reach = cells_in - LEAD - cells_out
        rows = np.floor((reach + NX // 2) / NX).astype(np.int64)
        along = reach - rows * NX
        ok = (np.abs(rows) <= RAD) & (np.abs(along) <= RAD) & (column + along >= 0) & (column + along < NX)
        weight = taps[np.clip(rows + RAD, 0, 2 * RAD)] * taps[np.clip(along + RAD, 0, 2 * RAD)]
        parts.append(np.where(ok, weight, 0.0))
    return np.stack(parts).astype(np.float32)


def depth_table():
    table = np.zeros((TAB,), np.float32)
    table[TAB_MID - RAD : TAB_MID + RAD + 1] = tap_weights()
    return table


def smooth_kernel(own_ref, near_ref, tab_ref, taps_ref, raw_ref, all_ref, rim_ref, up_ref, down_ref, pad, planar, mid_ref, mat_ref, sems, mid_sem, mat_sem):
    depth, frames, extent = raw_ref.shape
    step = PHASES * BLOCK
    steps = extent // step
    tiles = extent // RUN

    def fetch(i):
        return pltpu.make_async_copy(
            raw_ref.at[:, :, pl.ds(i * step, step)],
            pad.at[:, :, pl.ds(LEAD + i * step, step)],
            sems.at[i],
        )

    plan = pltpu.make_async_copy(taps_ref, mat_ref, mat_sem)
    plan.start()
    for i in range(steps):
        fetch(i).start()
    edge = jnp.zeros((depth, frames, LEAD), pad.dtype)
    pad[:, :, :LEAD] = edge
    pad[:, :, LEAD + extent :] = edge
    plan.wait()
    fetch(0).wait()

    def block(i, carry):
        @pl.when(i + 1 < steps)
        def _():
            fetch(i + 1).wait()

        for phase in range(PHASES):
            start = pl.multiple_of(i * step + phase * BLOCK, BLOCK)
            cells = pad[:, :, pl.ds(start, LEAD + BLOCK + LEAD)].reshape(depth * frames, LEAD + BLOCK + LEAD)
            out = jnp.dot(cells, mat_ref[phase], preferred_element_type=jnp.float32)
            planar[:, :, pl.ds(start, BLOCK)] = out.reshape(depth, frames, BLOCK)
        return carry

    lax.fori_loop(0, steps, block, 0)

    taps = tap_weights()

    def place(tile):
        plane = tile // tiles
        return plane, pl.multiple_of((tile - plane * tiles) * RUN, RUN)

    per = mid_ref.shape[2] // RUN

    def middle(g, carry):
        for j in range(per):
            plane, lane = place(own_ref[(g + GRP // 4) * per + j])
            total = taps[0] * planar[plane - RAD, :, pl.ds(lane, RUN)]
            for k in range(1, 2 * RAD + 1):
                total = total + taps[k] * planar[plane - RAD + k, :, pl.ds(lane, RUN)]
            mid_ref[g, :, j * RUN : (j + 1) * RUN] = total.astype(mid_ref.dtype)
        return carry

    def some(tile, first, count, shift):
        plane, lane = place(tile)
        total = None
        for q in range(first, first + count):
            weight = tab_ref[q - plane + shift + TAB_MID]
            term = weight * planar[q, :, pl.ds(lane, RUN)]
            total = term if total is None else total + term
        return total

    def rims(g, carry):
        for j in range(per):
            cols = slice(j * RUN, (j + 1) * RUN)
            at = g * per + j
            up_ref[g, :, cols] = some(near_ref[at], depth - RAD, RAD, -depth).astype(up_ref.dtype)
            down_ref[g, :, cols] = some(near_ref[GRP // 4 * per + at], 0, RAD, depth).astype(down_ref.dtype)
            rim_ref[g, :, cols] = some(own_ref[at], 0, 2 * RAD, 0)
            rim_ref[GRP // 4 + g, :, cols] = some(own_ref[GRP * 3 // 4 * per + at], depth - 2 * RAD, 2 * RAD, 0)
        return carry

    lax.fori_loop(0, GRP // 2, middle, 0)
    keep = pltpu.make_async_copy(mid_ref, all_ref.at[GRP // 4 : GRP * 3 // 4], mid_sem)
    keep.start()
    lax.fori_loop(0, GRP // 4, rims, 0)
    keep.wait()


def smooth(own, near, raw):
    depth, frames, extent = raw.shape
    per_device = own.shape[0] // GRP * RUN
    quarter = (GRP // 4, frames, per_device)
    half = (GRP // 2, frames, per_device)
    return pl.pallas_call(
        smooth_kernel,
        out_shape=[
            jax.ShapeDtypeStruct((GRP, frames, per_device), jnp.bfloat16),
            jax.ShapeDtypeStruct(half, jnp.float32),
            jax.ShapeDtypeStruct(quarter, jnp.bfloat16),
            jax.ShapeDtypeStruct(quarter, jnp.bfloat16),
        ],
        in_specs=[smem()] * 3 + [hbm(), hbm()],
        out_specs=[hbm(), *vmem(3)],
        scratch_shapes=[
            pltpu.VMEM((depth, frames, extent + 2 * LEAD), jnp.bfloat16),
            pltpu.VMEM((depth, frames, extent), jnp.float32),
            pltpu.VMEM(half, jnp.bfloat16),
            pltpu.VMEM((PHASES, LEAD + BLOCK + LEAD, BLOCK), jnp.bfloat16),
            pltpu.SemaphoreType.DMA((extent // (PHASES * BLOCK),)),
            pltpu.SemaphoreType.DMA,
            pltpu.SemaphoreType.DMA,
        ],
        compiler_params=params(SMOOTH_MIB),
        name="smooth",
    )(own, near, jnp.asarray(depth_table()), jnp.asarray(plane_matrix()).astype(jnp.bfloat16), raw)


NT = (((1,), (1,)), ((), ()))


def row_start(first):
    return min(first // 8 * 8, KX - WIN) if isinstance(first, int) else jnp.minimum(first // 8 * 8, KX - WIN)


def part_start(part):
    return jnp.minimum(part * PART // 16 * 16, K - WIDE)


def vmem(count):
    return [pl.BlockSpec(memory_space=pltpu.VMEM)] * count


def smem():
    return pl.BlockSpec(memory_space=pltpu.SMEM)


def params(mib):
    return pltpu.CompilerParams(vmem_limit_bytes=mib * 1024 * 1024)


def hbm():
    return pl.BlockSpec(memory_space=pltpu.HBM)


HALF = WIDE // 2


def gather_parts(x, which, sub_ref, left):
    for k in range(4):
        start = pl.multiple_of(part_start((x + k) % 4 * 2 + which), 16)
        left[k * WIDE : (k + 1) * WIDE, :] = sub_ref[pl.ds(start, WIDE), :]


def basis_other_kernel(at_ref, sub_ref, out_ref, left):
    gather_parts(at_ref[0], 1 - at_ref[1], sub_ref, left)
    out_ref[...] = lax.dot_general(left[...], sub_ref[...], NT, preferred_element_type=jnp.float32).astype(out_ref.dtype)


def basis_own_kernel(at_ref, sub_ref, got_ref, own_ref, next_ref, far_ref, back_ref, made_ref, left):
    made_ref[...] = jnp.zeros_like(made_ref)
    gather_parts(at_ref[0], at_ref[1], sub_ref, left)
    part = lax.dot_general(left[...], sub_ref[...], NT, preferred_element_type=jnp.float32)
    part = (part + got_ref[...].astype(jnp.float32)).astype(own_ref.dtype)
    own_ref[...] = part[:WIDE]
    next_ref[...] = part[WIDE : 2 * WIDE]
    far_ref[...] = part[2 * WIDE : 3 * WIDE].reshape(2, HALF, K)
    back_ref[...] = part[3 * WIDE :]


def basis_relay_kernel(next_ref, back_ref, low_ref, high_ref, next_out, back_out):
    next_out[:HALF] = (next_ref[:HALF].astype(jnp.float32) + low_ref[...].astype(jnp.float32)).astype(next_out.dtype)
    next_out[HALF:] = next_ref[HALF:]
    back_out[:HALF] = back_ref[:HALF]
    back_out[HALF:] = (back_ref[HALF:].astype(jnp.float32) + high_ref[...].astype(jnp.float32)).astype(back_out.dtype)


def basis_rows_kernel(at_ref, a_ref, b_ref, c_ref, out_ref, flat):
    part = at_ref[0] * 2 + at_ref[1]
    total = a_ref[...].astype(jnp.float32) + b_ref[...].astype(jnp.float32) + c_ref[...].astype(jnp.float32)
    flat[:, K // RUN * RUN :] = jnp.zeros((flat.shape[0], flat.shape[1] - K // RUN * RUN), jnp.float32)
    flat[:, :K] = total
    shift = (WIDE - (part * PART - part_start(part))) % WIDE
    narrow = pltpu.roll(flat[...], shift, 0)[:SHARE].astype(jnp.bfloat16)
    line = lax.broadcasted_iota(jnp.int32, (256, RUN), 0)
    lane = lax.broadcasted_iota(jnp.int32, (256, RUN), 1)
    for g in range(GRP):
        begin = g * ROWS // RUN * RUN
        if g * ROWS < K:
            pick = jnp.where((line == lane + (g * ROWS - begin)) & (lane < ROWS), 1.0, 0.0).astype(jnp.bfloat16)
            out_ref[g] = jnp.dot(narrow[:, begin : begin + 256], pick, preferred_element_type=jnp.float32).astype(
                out_ref.dtype
            )
        else:
            out_ref[g] = jnp.zeros((SHARE, RUN), out_ref.dtype)


def rim_kernel(rim_ref, low_ref, high_ref, all_ref, after_ref, out_ref, made, sems):
    del all_ref, after_ref
    quarter = GRP // 4
    made[:quarter] = (rim_ref[:quarter] + low_ref[...].astype(jnp.float32)).astype(made.dtype)
    first = pltpu.make_async_copy(made.at[:quarter], out_ref.at[:quarter], sems.at[0])
    first.start()
    made[quarter:] = (rim_ref[quarter:] + high_ref[...].astype(jnp.float32)).astype(made.dtype)
    second = pltpu.make_async_copy(made.at[quarter:], out_ref.at[3 * quarter :], sems.at[1])
    second.start()
    first.wait()
    second.wait()


def columns_kernel(at_ref, got_ref, basis_ref, cen_out, other_ref, own_out, power_ref, sub_ref, cen_ref, own_ref, sems):
    per_device = sub_ref.shape[1]
    core = at_ref[1]
    each = GRP // 2
    fetch = pltpu.make_async_copy(basis_ref, sub_ref, sems.at[0])
    fetch.start()

    def centre(i, sums):
        cols = pl.ds(pl.multiple_of(i * RUN, RUN), RUN)
        new = []
        for s in range(2):
            wide = got_ref[s * each : (s + 1) * each, :, cols].reshape(SUBJ, RUN).astype(jnp.float32)
            mean = jnp.sum(wide, axis=0, keepdims=True) * (1.0 / SUBJ)
            cen = (wide - mean).astype(cen_ref.dtype)
            cen_ref[s, :, cols] = cen
            back = cen.astype(jnp.float32)
            new.append(sums[s] + jnp.sum((back * back).reshape(SUBJ // 8, 8, RUN), axis=0))
        return tuple(new)

    zero = jnp.zeros((8, RUN), jnp.float32)
    sums = lax.fori_loop(0, per_device // RUN, centre, (zero, zero))
    keep = pltpu.make_async_copy(cen_ref, cen_out, sems.at[1])
    keep.start()
    line = lax.broadcasted_iota(jnp.int32, (8, RUN), 0)
    first = jnp.sum(sums[0], keepdims=True)
    second = jnp.sum(sums[1], keepdims=True)
    power_ref[...] = jnp.where(line == 0, first, jnp.where(line == 1, second, 0.0))

    fetch.wait()
    for which, out in ((core, own_ref), (1 - core, other_ref)):
        right = cen_ref[which]
        for lo in range(0, K, 400):
            out[lo : lo + 400, :] = lax.dot_general(
                sub_ref[lo : lo + 400, :], right, NT, preferred_element_type=jnp.float32
            ).astype(out.dtype)
        for s in range(2):
            lo = K + s * SUBJ
            out[lo : lo + SUBJ, :] = lax.dot_general(
                cen_ref[s], right, NT, preferred_element_type=jnp.float32
            ).astype(out.dtype)
        if out is own_ref:
            leave = pltpu.make_async_copy(own_ref, own_out, sems.at[2])
            leave.start()
    leave.wait()
    keep.wait()


def write_power(power, put):
    high = power.astype(jnp.bfloat16)
    put(slice(WIN, TALL), high)
    put(slice(TALL + WIN, 2 * TALL), (power - high.astype(jnp.float32)).astype(jnp.bfloat16))


def windows_kernel(own_ref, got_ref, power_ref, out_ref, whole, sem):
    fetch = pltpu.make_async_copy(own_ref, whole, sem)
    fetch.start()
    for g in range(GRP):
        def put(rows, value, g=g):
            out_ref[g, rows, :] = value

        write_power(power_ref[...], put)
    fetch.wait()
    whole[...] = whole[...] + got_ref[...].astype(jnp.float32)
    for g in range(GRP):
        first = row_start(g * ROWS)
        for half in range(2):
            out_ref[g, half * TALL : half * TALL + WIN, :] = whole[
                first : first + WIN, half * RUN : (half + 1) * RUN
            ].astype(out_ref.dtype)


def total_kernel(got_ref, share_ref, out_ref):
    def summed(ref):
        total = ref[0].astype(jnp.float32)
        for g in range(1, GRP):
            total = total + ref[g].astype(jnp.float32)
        return total

    total = summed(got_ref)
    out_ref[: 2 * TALL] = total.astype(out_ref.dtype)
    out_ref[2 * TALL :] = summed(share_ref).astype(out_ref.dtype)

    def put(rows, value):
        out_ref[rows, :] = value

    write_power(total[WIN:TALL] + total[TALL + WIN :], put)


def slab_kernel(a_ref, b_ref, c_ref, d_ref, sum_ref, share_ref):
    refs = (a_ref, b_ref, c_ref, d_ref)
    total = refs[0][: 2 * TALL].astype(jnp.float32)
    for ref in refs[1:]:
        total = total + ref[: 2 * TALL].astype(jnp.float32)
    sum_ref[...] = total
    for k in range(4):
        share_ref[k] = refs[k][2 * TALL :]


def finish_kernel(count, at_ref, own_ref, got_ref, rows_ref, scale_ref, turned_ref):
    own, got = own_ref[...], got_ref[...]
    both = own + got
    scale_ref[...] = lax.rsqrt((both[WIN:TALL] + both[TALL + WIN :]) / count + epsilon)
    is_first = at_ref[1] == 0
    zero = jnp.where(is_first, own, got)
    one = jnp.where(is_first, got, own)
    rows = jnp.concatenate([zero[:TALL], zero[TALL:], one[:TALL], one[TALL:]], axis=1)
    first = at_ref[2] * ROWS
    shift = (TALL - (first - row_start(first))) % TALL
    rows = pltpu.roll(rows, shift, 0)
    rows_ref[...] = rows
    narrow = rows.astype(jnp.bfloat16)
    turned_ref[: K // ROWS] = jnp.zeros((K // ROWS, TURNED, TALL), turned_ref.dtype)
    line = lax.broadcasted_iota(jnp.int32, (TURNED, 2 * SUBJ), 0)
    lane = lax.broadcasted_iota(jnp.int32, (TURNED, 2 * SUBJ), 1)
    for g in range(K // ROWS, GRP):
        pick = jnp.where(line + (g * ROWS - K) == lane, 1.0, 0.0).astype(jnp.bfloat16)
        turned_ref[g] = lax.dot_general(pick, narrow, NT, preferred_element_type=jnp.float32).astype(turned_ref.dtype)


def assemble_kernel(masked, at_ref, back_ref, rows_ref, scale_ref, mine_ref, other_ref, out_ref, basis, cross):
    x, core, grp = at_ref[0], at_ref[1], at_ref[2]
    first = grp * ROWS
    basis[...] = jnp.zeros_like(basis)
    cross[...] = jnp.zeros_like(cross)
    line = lax.broadcasted_iota(jnp.int32, (SHARE, 384), 0)
    lane = lax.broadcasted_iota(jnp.int32, (SHARE, 384), 1)
    for k in range(4):
        for share, which in ((mine_ref, core), (other_ref, 1 - core)):
            part = (x - k + 4) % 4 * 2 + which
            begin = part * PART // RUN * RUN
            put = jnp.where((line + (part * PART - begin) == lane) & (line < PART), 1.0, 0.0).astype(jnp.bfloat16)
            cols = pl.ds(pl.multiple_of(begin, RUN), 384)
            basis[:, cols] += lax.dot_general(
                share[k], put, (((0,), (0,)), ((), ())), preferred_element_type=jnp.float32
            )
    line = lax.broadcasted_iota(jnp.int32, (TALL, 256), 0)
    lane = lax.broadcasted_iota(jnp.int32, (TALL, 256), 1)
    for g in range(K // ROWS + 1):
        begin = g * ROWS // RUN * RUN
        ok = (line + (g * ROWS - begin) == lane) & (line < ROWS) & (line + g * ROWS < K)
        put = jnp.where(ok, 1.0, 0.0).astype(jnp.bfloat16)
        cross[:TURNED, begin : begin + 256] += jnp.dot(back_ref[g], put, preferred_element_type=jnp.float32)
    width = 1792
    row = first + lax.broadcasted_iota(jnp.int32, (TALL, 1), 0)
    left = jnp.where(row < K, basis[...], cross[...])
    base = K // RUN * RUN
    right = pltpu.roll(
        jnp.concatenate([rows_ref[...], jnp.zeros((TALL, RUN), jnp.float32)], axis=1), K - base, 1
    )
    zero, one = scale_ref[0:1, 0:1], scale_ref[1:2, 0:1]
    of_row = jnp.where(row < K, 1.0, jnp.where(row < K + SUBJ, zero, one))
    col = lax.broadcasted_iota(jnp.int32, (1, width), 1)
    of_col = jnp.where(col < K, 1.0, jnp.where(col < K + SUBJ, zero, one))
    out_ref[:, :base] = (left[:, :base] * (of_row * of_col[:, :base]) / masked)[:ROWS]
    edge = jnp.concatenate([left[:, base:], jnp.zeros((TALL, width - left.shape[1]), jnp.float32)], axis=1)
    values = jnp.where(col[:, base:] < K, edge, right)
    out_ref[:, base:] = (values * (of_row * of_col[:, base:]) / masked)[:ROWS, : KX - base]


def rotate_kernel(tile, scale_ref, base_ref, turn_ref, cen_ref, out_ref, held, sems):
    step = pl.program_id(0)
    steps = pl.num_programs(0)

    def fetch(i):
        rows = pl.ds(pl.multiple_of(i * tile, 16), tile)
        return pltpu.make_async_copy(base_ref.at[rows], held.at[i % 2], sems.at[i % 2])

    @pl.when(step == 0)
    def _():
        fetch(step).start()

    @pl.when(step + 1 < steps)
    def _():
        fetch(step + 1).start()

    fetch(step).wait()
    slot = step % 2
    for lo in range(0, out_ref.shape[1], 256):
        cols = slice(lo, lo + 256)
        first = jnp.dot(turn_ref[:, :SUBJ], cen_ref[0, :, cols], preferred_element_type=jnp.float32)
        second = jnp.dot(turn_ref[:, SUBJ:], cen_ref[1, :, cols], preferred_element_type=jnp.float32)
        base = held[slot, :, cols].astype(jnp.float32)
        out_ref[:, cols] = (base + scale_ref[0:1, 0:1] * first + scale_ref[1:2, 0:1] * second).astype(out_ref.dtype)


def copies(value, axis, count):
    return lax.all_to_all(jnp.broadcast_to(value[None], (count, *value.shape)), axis, 0, 0, tiled=True)


def body(raw_frames, mask_index, subspace, rotation):
    depth = raw_frames.shape[1]
    extent = raw_frames.shape[2]
    per_device = subspace.shape[1]
    slab = ("x", "core")
    masked = per_device * 8 * GRP
    bf16 = jnp.bfloat16
    f32 = jnp.float32
    like = jax.ShapeDtypeStruct
    swap = [(0, 1), (1, 0)]
    turns = [[(i, (i + k) % 4) for i in range(4)] for k in range(4)]
    at = jnp.stack([lax.axis_index("x"), lax.axis_index("core"), lax.axis_index("grp")]).astype(jnp.int32)

    slab_at = lax.axis_index("x") * 2 + lax.axis_index("core")
    tiles = mask_index.reshape(-1, RUN)[:, 0] // RUN - slab_at * (depth * extent // RUN)
    up = [(i, i + 1) for i in range(7)]
    down = [(i + 1, i) for i in range(7)]
    packed = jnp.stack([tiles, lax.ppermute(tiles, slab, up), lax.ppermute(tiles, slab, down)])
    at_ss, _ = lax.optimization_barrier((at, packed))
    held = [pltpu.VMEM((4 * WIDE, per_device), bf16)]
    other_ss = pl.pallas_call(
        basis_other_kernel,
        out_shape=like((4 * WIDE, K), bf16),
        in_specs=[smem(), *vmem(1)],
        out_specs=vmem(1)[0],
        scratch_shapes=held,
        compiler_params=params(24),
        name="basis_other",
    )(at_ss, subspace)
    every, other_ss = lax.optimization_barrier((copies(packed, "grp", GRP), other_ss))
    own = every[:, 0].reshape(-1)
    near = jnp.concatenate([every[: GRP // 4, 2].reshape(-1), every[3 * GRP // 4 :, 1].reshape(-1)])

    middles, rim, to_up, to_down = smooth(own, near, jnp.transpose(raw_frames, (1, 0, 2)))
    got_ss = lax.ppermute(other_ss, "core", swap)
    at_own, _ = lax.optimization_barrier((at, to_down))
    own_ss, next_ss, far_ss, back_ss, made = pl.pallas_call(
        basis_own_kernel,
        out_shape=[like((WIDE, K), bf16), like((WIDE, K), bf16), like((2, HALF, K), bf16), like((WIDE, K), bf16), like((8, RUN), f32)],
        in_specs=[smem(), *vmem(2)],
        out_specs=vmem(5),
        scratch_shapes=held,
        compiler_params=params(24),
        name="basis_own",
    )(at_own, subspace, got_ss)
    from_low, from_high = lax.ppermute(to_up, slab, up), lax.ppermute(to_down, slab, down)
    placed = pl.pallas_call(
        rim_kernel,
        out_shape=like(middles.shape, bf16),
        in_specs=[*vmem(3), hbm(), *vmem(1)],
        out_specs=hbm(),
        scratch_shapes=[pltpu.VMEM(rim.shape, bf16), pltpu.SemaphoreType.DMA((2,))],
        input_output_aliases={3: 0},
        compiler_params=params(16),
        name="rim",
    )(rim, from_low, from_high, middles, made)
    regrouped = lax.all_to_all(placed, "grp", 0, 0, tiled=True)

    ahead, behind = turns[1], turns[3]
    next_ss, back_ss = pl.pallas_call(
        basis_relay_kernel,
        out_shape=[like((WIDE, K), bf16)] * 2,
        in_specs=vmem(4),
        out_specs=vmem(2),
        compiler_params=params(16),
        name="basis_relay",
    )(next_ss, back_ss, lax.ppermute(far_ss[0], "x", ahead), lax.ppermute(far_ss[1], "x", behind))
    regrouped, _, _ = lax.optimization_barrier((regrouped, next_ss, back_ss))
    went_on = lax.ppermute(next_ss, "x", ahead)
    went_back = lax.ppermute(back_ss, "x", behind)
    at_rows, _ = lax.optimization_barrier((at, regrouped))
    by_row = pl.pallas_call(
        basis_rows_kernel,
        out_shape=like((GRP, SHARE, RUN), bf16),
        in_specs=[smem(), *vmem(3)],
        out_specs=vmem(1)[0],
        scratch_shapes=[pltpu.VMEM((WIDE, 1408), f32)],
        compiler_params=params(16),
        name="basis_rows",
    )(at_rows, own_ss, went_on, went_back)
    gathered = lax.all_to_all(by_row, "grp", 0, 0, tiled=True)

    centered, other_c, own_c, power = pl.pallas_call(
        columns_kernel,
        out_shape=[like((2, SUBJ, per_device), bf16), like((KX, SUBJ), bf16), like((KX, SUBJ), f32), like((8, RUN), f32)],
        in_specs=[smem(), *vmem(1), hbm()],
        out_specs=[hbm(), *vmem(1), hbm(), *vmem(1)],
        scratch_shapes=[
            pltpu.VMEM((K, per_device), bf16),
            pltpu.VMEM((2, SUBJ, per_device), bf16),
            pltpu.VMEM((KX, SUBJ), f32),
            pltpu.SemaphoreType.DMA((3,)),
        ],
        compiler_params=params(52),
        name="columns",
    )(at, regrouped, subspace)
    sent = pl.pallas_call(
        windows_kernel,
        out_shape=like((GRP, 2 * TALL, RUN), bf16),
        in_specs=[hbm(), *vmem(2)],
        out_specs=vmem(1)[0],
        scratch_shapes=[pltpu.VMEM((KX, SUBJ), f32), pltpu.SemaphoreType.DMA],
        compiler_params=params(16),
        name="windows",
    )(own_c, lax.ppermute(other_c, "core", swap), power)
    sent, gathered = lax.optimization_barrier((sent, gathered))
    summed = lax.all_to_all(sent, "grp", 0, 0, tiled=True)

    rotation_b, _ = lax.optimization_barrier((rotation, sent))
    contract = (((0,), (0,)), ((), ()))
    from_basis = lax.dot_general(rotation_b[:K], subspace, contract, preferred_element_type=f32).astype(bf16)
    summed, from_basis, turn = lax.optimization_barrier((summed, from_basis, rotation_b[K:].T))

    total = pl.pallas_call(
        total_kernel,
        out_shape=like((2 * TALL + SHARE, RUN), bf16),
        in_specs=vmem(2),
        out_specs=vmem(1)[0],
        compiler_params=params(16),
        name="total",
    )(summed, gathered)
    sum_c, share = pl.pallas_call(
        slab_kernel,
        out_shape=[like((2 * TALL, RUN), f32), like((4, SHARE, RUN), bf16)],
        in_specs=vmem(4),
        out_specs=vmem(2),
        compiler_params=params(16),
        name="slab",
    )(total, *[lax.ppermute(total, "x", turns[k]) for k in range(1, 4)])
    rows_c, scales, turned = pl.pallas_call(
        functools.partial(finish_kernel, float(masked * SUBJ)),
        out_shape=[like((TALL, 2 * SUBJ), f32), like((8, RUN), f32), like((GRP, TURNED, TALL), bf16)],
        in_specs=[smem(), *vmem(2)],
        out_specs=vmem(3),
        compiler_params=params(16),
        name="finish",
    )(at, sum_c, lax.ppermute(sum_c, "core", swap))

    back = lax.all_to_all(turned, "grp", 0, 0, tiled=True)
    gram_rows = pl.pallas_call(
        functools.partial(assemble_kernel, float(masked)),
        out_shape=like((ROWS, KX), f32),
        in_specs=[smem(), *vmem(5)],
        out_specs=vmem(1)[0],
        scratch_shapes=[pltpu.VMEM((TALL, 1408), f32), pltpu.VMEM((TALL, 1408), f32)],
        compiler_params=params(16),
        name="assemble",
    )(at, back, rows_c, scales, share, lax.ppermute(share, "core", swap))

    tile = 240
    new_subspace = pl.pallas_call(
        functools.partial(rotate_kernel, tile),
        out_shape=like((K, per_device), bf16),
        grid=(K // tile,),
        in_specs=[
            pl.BlockSpec((8, RUN), lambda i: (0, 0)),
            hbm(),
            pl.BlockSpec((tile, 2 * SUBJ), lambda i: (i, 0)),
            pl.BlockSpec((2, SUBJ, per_device), lambda i: (0, 0, 0)),
        ],
        out_specs=pl.BlockSpec((tile, per_device), lambda i: (i, 0)),
        scratch_shapes=[pltpu.VMEM((2, tile, per_device), bf16), pltpu.SemaphoreType.DMA((2,))],
        compiler_params=params(BIG),
        name="rotate",
    )(scales, from_basis, turn, centered)
    return (gram_rows, new_subspace)


def solution(mesh):
    fine = Mesh(mesh.devices.reshape(4, 2, GRP), ("x", "core", "grp"))
    slab = ("x", "core")
    placed = (P("grp", slab, None), P((*slab, "grp")), P(None, (*slab, "grp")), P())
    return jax.shard_map(
        body,
        mesh=fine,
        in_specs=placed,
        out_specs=(P("grp", None), P(None, (*slab, "grp"))),
        check_vma=False,
    )
```

```python
import functools
import math

import jax
import jax.numpy as jnp
import numpy as np
from jax import lax
from jax.experimental import pallas as pl
from jax.experimental.pallas import tpu as pltpu
from jax.sharding import Mesh
from jax.sharding import PartitionSpec as P


NX = 96
RUN = 128
RAD = 3
K = 1200
KX = 1712
SUBJ = 256
ROWS = 107
WIN = 120
TALL = 128
PART = 150
WIDE = 176
SHARE = 152
SMOOTH_MIB = 48
BIG = 50
TURNED = 112
LEAD = 384
BLOCK = 256
PHASES = 3
GRP = 16
TAB = 64
TAB_MID = 31

smooth_sigma = 1.0617
epsilon = 1e-06


def tap_weights():
    unscaled = [
        math.exp(-offset * offset / (2.0 * smooth_sigma * smooth_sigma))
        for offset in range(-RAD, RAD + 1)
    ]
    summed = sum(unscaled)
    return [weight / summed for weight in unscaled]


def plane_matrix():
    taps = np.array(tap_weights())
    cells_in = np.arange(LEAD + BLOCK + LEAD)[:, None]
    cells_out = np.arange(BLOCK)[None, :]
    parts = []
    for phase in range(PHASES):
        column = (phase * BLOCK + cells_out) % NX
        reach = cells_in - LEAD - cells_out
        rows = np.floor((reach + NX // 2) / NX).astype(np.int64)
        along = reach - rows * NX
        ok = (np.abs(rows) <= RAD) & (np.abs(along) <= RAD) & (column + along >= 0) & (column + along < NX)
        weight = taps[np.clip(rows + RAD, 0, 2 * RAD)] * taps[np.clip(along + RAD, 0, 2 * RAD)]
        parts.append(np.where(ok, weight, 0.0))
    return np.stack(parts).astype(np.float32)


def depth_table():
    table = np.zeros((TAB,), np.float32)
    table[TAB_MID - RAD : TAB_MID + RAD + 1] = tap_weights()
    return table


def smooth_kernel(own_ref, near_ref, tab_ref, taps_ref, raw_ref, all_ref, rim_ref, up_ref, down_ref, pad, planar, mid_ref, mat_ref, sems, mid_sem, mat_sem):
    depth, frames, extent = raw_ref.shape
    step = PHASES * BLOCK
    steps = extent // step
    tiles = extent // RUN

    def fetch(i):
        return pltpu.make_async_copy(
            raw_ref.at[:, :, pl.ds(i * step, step)],
            pad.at[:, :, pl.ds(LEAD + i * step, step)],
            sems.at[i],
        )

    plan = pltpu.make_async_copy(taps_ref, mat_ref, mat_sem)
    plan.start()
    for i in range(steps):
        fetch(i).start()
    edge = jnp.zeros((depth, frames, LEAD), pad.dtype)
    pad[:, :, :LEAD] = edge
    pad[:, :, LEAD + extent :] = edge
    plan.wait()
    fetch(0).wait()

    def block(i, carry):
        @pl.when(i + 1 < steps)
        def _():
            fetch(i + 1).wait()

        for phase in range(PHASES):
            start = pl.multiple_of(i * step + phase * BLOCK, BLOCK)
            cells = pad[:, :, pl.ds(start, LEAD + BLOCK + LEAD)].reshape(depth * frames, LEAD + BLOCK + LEAD)
            out = jnp.dot(cells, mat_ref[phase], preferred_element_type=jnp.float32)
            planar[:, :, pl.ds(start, BLOCK)] = out.reshape(depth, frames, BLOCK)
        return carry

    lax.fori_loop(0, steps, block, 0)

    taps = tap_weights()

    def place(tile):
        plane = tile // tiles
        return plane, pl.multiple_of((tile - plane * tiles) * RUN, RUN)

    per = mid_ref.shape[2] // RUN

    def middle(g, carry):
        for j in range(per):
            plane, lane = place(own_ref[(g + GRP // 4) * per + j])
            total = taps[0] * planar[plane - RAD, :, pl.ds(lane, RUN)]
            for k in range(1, 2 * RAD + 1):
                total = total + taps[k] * planar[plane - RAD + k, :, pl.ds(lane, RUN)]
            mid_ref[g, :, j * RUN : (j + 1) * RUN] = total.astype(mid_ref.dtype)
        return carry

    def some(tile, first, count, shift):
        plane, lane = place(tile)
        total = None
        for q in range(first, first + count):
            weight = tab_ref[q - plane + shift + TAB_MID]
            term = weight * planar[q, :, pl.ds(lane, RUN)]
            total = term if total is None else total + term
        return total

    def rims(g, carry):
        for j in range(per):
            cols = slice(j * RUN, (j + 1) * RUN)
            at = g * per + j
            up_ref[g, :, cols] = some(near_ref[at], depth - RAD, RAD, -depth).astype(up_ref.dtype)
            down_ref[g, :, cols] = some(near_ref[GRP // 4 * per + at], 0, RAD, depth).astype(down_ref.dtype)
            rim_ref[g, :, cols] = some(own_ref[at], 0, 2 * RAD, 0)
            rim_ref[GRP // 4 + g, :, cols] = some(own_ref[GRP * 3 // 4 * per + at], depth - 2 * RAD, 2 * RAD, 0)
        return carry

    lax.fori_loop(0, GRP // 2, middle, 0)
    keep = pltpu.make_async_copy(mid_ref, all_ref.at[GRP // 4 : GRP * 3 // 4], mid_sem)
    keep.start()
    lax.fori_loop(0, GRP // 4, rims, 0)
    keep.wait()


def smooth(own, near, raw):
    depth, frames, extent = raw.shape
    per_device = own.shape[0] // GRP * RUN
    quarter = (GRP // 4, frames, per_device)
    half = (GRP // 2, frames, per_device)
    return pl.pallas_call(
        smooth_kernel,
        out_shape=[
            jax.ShapeDtypeStruct((GRP, frames, per_device), jnp.bfloat16),
            jax.ShapeDtypeStruct(half, jnp.float32),
            jax.ShapeDtypeStruct(quarter, jnp.bfloat16),
            jax.ShapeDtypeStruct(quarter, jnp.bfloat16),
        ],
        in_specs=[smem()] * 3 + [hbm(), hbm()],
        out_specs=[hbm(), *vmem(3)],
        scratch_shapes=[
            pltpu.VMEM((depth, frames, extent + 2 * LEAD), jnp.bfloat16),
            pltpu.VMEM((depth, frames, extent), jnp.float32),
            pltpu.VMEM(half, jnp.bfloat16),
            pltpu.VMEM((PHASES, LEAD + BLOCK + LEAD, BLOCK), jnp.bfloat16),
            pltpu.SemaphoreType.DMA((extent // (PHASES * BLOCK),)),
            pltpu.SemaphoreType.DMA,
            pltpu.SemaphoreType.DMA,
        ],
        compiler_params=params(SMOOTH_MIB),
        name="smooth",
    )(own, near, jnp.asarray(depth_table()), jnp.asarray(plane_matrix()).astype(jnp.bfloat16), raw)


NT = (((1,), (1,)), ((), ()))


def row_start(first):
    return min(first // 8 * 8, KX - WIN) if isinstance(first, int) else jnp.minimum(first // 8 * 8, KX - WIN)


def part_start(part):
    return jnp.minimum(part * PART // 16 * 16, K - WIDE)


def vmem(count):
    return [pl.BlockSpec(memory_space=pltpu.VMEM)] * count


def smem():
    return pl.BlockSpec(memory_space=pltpu.SMEM)


def params(mib):
    return pltpu.CompilerParams(vmem_limit_bytes=mib * 1024 * 1024)


def hbm():
    return pl.BlockSpec(memory_space=pltpu.HBM)


HALF = WIDE // 2


def gather_parts(x, which, sub_ref, left):
    for k in range(4):
        start = pl.multiple_of(part_start((x + k) % 4 * 2 + which), 16)
        left[k * WIDE : (k + 1) * WIDE, :] = sub_ref[pl.ds(start, WIDE), :]


def basis_other_kernel(at_ref, sub_ref, out_ref, left):
    gather_parts(at_ref[0], 1 - at_ref[1], sub_ref, left)
    out_ref[...] = lax.dot_general(left[...], sub_ref[...], NT, preferred_element_type=jnp.float32).astype(out_ref.dtype)


def basis_own_kernel(at_ref, sub_ref, got_ref, own_ref, next_ref, far_ref, back_ref, made_ref, left):
    made_ref[...] = jnp.zeros_like(made_ref)
    gather_parts(at_ref[0], at_ref[1], sub_ref, left)
    part = lax.dot_general(left[...], sub_ref[...], NT, preferred_element_type=jnp.float32)
    part = (part + got_ref[...].astype(jnp.float32)).astype(own_ref.dtype)
    own_ref[...] = part[:WIDE]
    next_ref[...] = part[WIDE : 2 * WIDE]
    far_ref[...] = part[2 * WIDE : 3 * WIDE].reshape(2, HALF, K)
    back_ref[...] = part[3 * WIDE :]


def basis_relay_kernel(next_ref, back_ref, low_ref, high_ref, next_out, back_out):
    next_out[:HALF] = (next_ref[:HALF].astype(jnp.float32) + low_ref[...].astype(jnp.float32)).astype(next_out.dtype)
    next_out[HALF:] = next_ref[HALF:]
    back_out[:HALF] = back_ref[:HALF]
    back_out[HALF:] = (back_ref[HALF:].astype(jnp.float32) + high_ref[...].astype(jnp.float32)).astype(back_out.dtype)


def basis_rows_kernel(at_ref, a_ref, b_ref, c_ref, out_ref, flat):
    part = at_ref[0] * 2 + at_ref[1]
    total = a_ref[...].astype(jnp.float32) + b_ref[...].astype(jnp.float32) + c_ref[...].astype(jnp.float32)
    flat[:, K // RUN * RUN :] = jnp.zeros((flat.shape[0], flat.shape[1] - K // RUN * RUN), jnp.float32)
    flat[:, :K] = total
    shift = (WIDE - (part * PART - part_start(part))) % WIDE
    narrow = pltpu.roll(flat[...], shift, 0)[:SHARE].astype(jnp.bfloat16)
    line = lax.broadcasted_iota(jnp.int32, (256, RUN), 0)
    lane = lax.broadcasted_iota(jnp.int32, (256, RUN), 1)
    for g in range(GRP):
        begin = g * ROWS // RUN * RUN
        if g * ROWS < K:
            pick = jnp.where((line == lane + (g * ROWS - begin)) & (lane < ROWS), 1.0, 0.0).astype(jnp.bfloat16)
            out_ref[g] = jnp.dot(narrow[:, begin : begin + 256], pick, preferred_element_type=jnp.float32).astype(
                out_ref.dtype
            )
        else:
            out_ref[g] = jnp.zeros((SHARE, RUN), out_ref.dtype)


def rim_kernel(rim_ref, low_ref, high_ref, all_ref, after_ref, out_ref, made, sems):
    del all_ref, after_ref
    quarter = GRP // 4
    made[:quarter] = (rim_ref[:quarter] + low_ref[...].astype(jnp.float32)).astype(made.dtype)
    first = pltpu.make_async_copy(made.at[:quarter], out_ref.at[:quarter], sems.at[0])
    first.start()
    made[quarter:] = (rim_ref[quarter:] + high_ref[...].astype(jnp.float32)).astype(made.dtype)
    second = pltpu.make_async_copy(made.at[quarter:], out_ref.at[3 * quarter :], sems.at[1])
    second.start()
    first.wait()
    second.wait()


def columns_kernel(at_ref, got_ref, basis_ref, cen_out, other_ref, own_out, power_ref, sub_ref, cen_ref, own_ref, sems):
    per_device = sub_ref.shape[1]
    core = at_ref[1]
    each = GRP // 2
    fetch = pltpu.make_async_copy(basis_ref, sub_ref, sems.at[0])
    fetch.start()

    def centre(i, sums):
        cols = pl.ds(pl.multiple_of(i * RUN, RUN), RUN)
        new = []
        for s in range(2):
            wide = got_ref[s * each : (s + 1) * each, :, cols].reshape(SUBJ, RUN).astype(jnp.float32)
            mean = jnp.sum(wide, axis=0, keepdims=True) * (1.0 / SUBJ)
            cen = (wide - mean).astype(cen_ref.dtype)
            cen_ref[s, :, cols] = cen
            back = cen.astype(jnp.float32)
            new.append(sums[s] + jnp.sum((back * back).reshape(SUBJ // 8, 8, RUN), axis=0))
        return tuple(new)

    zero = jnp.zeros((8, RUN), jnp.float32)
    sums = lax.fori_loop(0, per_device // RUN, centre, (zero, zero))
    keep = pltpu.make_async_copy(cen_ref, cen_out, sems.at[1])
    keep.start()
    line = lax.broadcasted_iota(jnp.int32, (8, RUN), 0)
    first = jnp.sum(sums[0], keepdims=True)
    second = jnp.sum(sums[1], keepdims=True)
    power_ref[...] = jnp.where(line == 0, first, jnp.where(line == 1, second, 0.0))

    fetch.wait()
    for which, out in ((core, own_ref), (1 - core, other_ref)):
        right = cen_ref[which]
        for lo in range(0, K, 400):
            out[lo : lo + 400, :] = lax.dot_general(
                sub_ref[lo : lo + 400, :], right, NT, preferred_element_type=jnp.float32
            ).astype(out.dtype)
        for s in range(2):
            lo = K + s * SUBJ
            out[lo : lo + SUBJ, :] = lax.dot_general(
                cen_ref[s], right, NT, preferred_element_type=jnp.float32
            ).astype(out.dtype)
        if out is own_ref:
            leave = pltpu.make_async_copy(own_ref, own_out, sems.at[2])
            leave.start()
    leave.wait()
    keep.wait()


def write_power(power, put):
    high = power.astype(jnp.bfloat16)
    put(slice(WIN, TALL), high)
    put(slice(TALL + WIN, 2 * TALL), (power - high.astype(jnp.float32)).astype(jnp.bfloat16))


def windows_kernel(own_ref, got_ref, power_ref, basis_ref, out_ref, whole, sem):
    fetch = pltpu.make_async_copy(own_ref, whole, sem)
    fetch.start()
    for g in range(GRP):
        out_ref[g, 2 * TALL :, :] = basis_ref[g]

        def put(rows, value, g=g):
            out_ref[g, rows, :] = value

        write_power(power_ref[...], put)
    fetch.wait()
    whole[...] = whole[...] + got_ref[...].astype(jnp.float32)
    for g in range(GRP):
        first = row_start(g * ROWS)
        for half in range(2):
            out_ref[g, half * TALL : half * TALL + WIN, :] = whole[
                first : first + WIN, half * RUN : (half + 1) * RUN
            ].astype(out_ref.dtype)


def total_kernel(got_ref, out_ref):
    total = got_ref[0].astype(jnp.float32)
    for g in range(1, GRP):
        total = total + got_ref[g].astype(jnp.float32)
    out_ref[...] = total.astype(out_ref.dtype)

    def put(rows, value):
        out_ref[rows, :] = value

    write_power(total[WIN:TALL] + total[TALL + WIN : 2 * TALL], put)


def slab_kernel(a_ref, b_ref, c_ref, d_ref, sum_ref, share_ref):
    refs = (a_ref, b_ref, c_ref, d_ref)
    total = refs[0][: 2 * TALL].astype(jnp.float32)
    for ref in refs[1:]:
        total = total + ref[: 2 * TALL].astype(jnp.float32)
    sum_ref[...] = total
    for k in range(4):
        share_ref[k] = refs[k][2 * TALL :]


def finish_kernel(count, at_ref, own_ref, got_ref, rows_ref, scale_ref, turned_ref):
    own, got = own_ref[...], got_ref[...]
    both = own + got
    scale_ref[...] = lax.rsqrt((both[WIN:TALL] + both[TALL + WIN :]) / count + epsilon)
    is_first = at_ref[1] == 0
    zero = jnp.where(is_first, own, got)
    one = jnp.where(is_first, got, own)
    rows = jnp.concatenate([zero[:TALL], zero[TALL:], one[:TALL], one[TALL:]], axis=1)
    first = at_ref[2] * ROWS
    shift = (TALL - (first - row_start(first))) % TALL
    rows = pltpu.roll(rows, shift, 0)
    rows_ref[...] = rows
    narrow = rows.astype(jnp.bfloat16)
    turned_ref[: K // ROWS] = jnp.zeros((K // ROWS, TURNED, TALL), turned_ref.dtype)
    line = lax.broadcasted_iota(jnp.int32, (TURNED, 2 * SUBJ), 0)
    lane = lax.broadcasted_iota(jnp.int32, (TURNED, 2 * SUBJ), 1)
    for g in range(K // ROWS, GRP):
        pick = jnp.where(line + (g * ROWS - K) == lane, 1.0, 0.0).astype(jnp.bfloat16)
        turned_ref[g] = lax.dot_general(pick, narrow, NT, preferred_element_type=jnp.float32).astype(turned_ref.dtype)


def assemble_kernel(masked, at_ref, back_ref, rows_ref, scale_ref, mine_ref, other_ref, out_ref, basis, cross):
    x, core, grp = at_ref[0], at_ref[1], at_ref[2]
    first = grp * ROWS
    basis[...] = jnp.zeros_like(basis)
    cross[...] = jnp.zeros_like(cross)
    line = lax.broadcasted_iota(jnp.int32, (SHARE, 384), 0)
    lane = lax.broadcasted_iota(jnp.int32, (SHARE, 384), 1)
    for k in range(4):
        for share, which in ((mine_ref, core), (other_ref, 1 - core)):
            part = (x - k + 4) % 4 * 2 + which
            begin = part * PART // RUN * RUN
            put = jnp.where((line + (part * PART - begin) == lane) & (line < PART), 1.0, 0.0).astype(jnp.bfloat16)
            cols = pl.ds(pl.multiple_of(begin, RUN), 384)
            basis[:, cols] += lax.dot_general(
                share[k], put, (((0,), (0,)), ((), ())), preferred_element_type=jnp.float32
            )
    line = lax.broadcasted_iota(jnp.int32, (TALL, 256), 0)
    lane = lax.broadcasted_iota(jnp.int32, (TALL, 256), 1)
    for g in range(K // ROWS + 1):
        begin = g * ROWS // RUN * RUN
        ok = (line + (g * ROWS - begin) == lane) & (line < ROWS) & (line + g * ROWS < K)
        put = jnp.where(ok, 1.0, 0.0).astype(jnp.bfloat16)
        cross[:TURNED, begin : begin + 256] += jnp.dot(back_ref[g], put, preferred_element_type=jnp.float32)
    width = 1792
    row = first + lax.broadcasted_iota(jnp.int32, (TALL, 1), 0)
    left = jnp.where(row < K, basis[...], cross[...])
    base = K // RUN * RUN
    right = pltpu.roll(
        jnp.concatenate([rows_ref[...], jnp.zeros((TALL, RUN), jnp.float32)], axis=1), K - base, 1
    )
    zero, one = scale_ref[0:1, 0:1], scale_ref[1:2, 0:1]
    of_row = jnp.where(row < K, 1.0, jnp.where(row < K + SUBJ, zero, one))
    col = lax.broadcasted_iota(jnp.int32, (1, width), 1)
    of_col = jnp.where(col < K, 1.0, jnp.where(col < K + SUBJ, zero, one))
    out_ref[:, :base] = (left[:, :base] * (of_row * of_col[:, :base]) / masked)[:ROWS]
    edge = jnp.concatenate([left[:, base:], jnp.zeros((TALL, width - left.shape[1]), jnp.float32)], axis=1)
    values = jnp.where(col[:, base:] < K, edge, right)
    out_ref[:, base:] = (values * (of_row * of_col[:, base:]) / masked)[:ROWS, : KX - base]


def rotate_kernel(tile, scale_ref, base_ref, turn_ref, cen_ref, out_ref, held, sems):
    step = pl.program_id(0)
    steps = pl.num_programs(0)

    def fetch(i):
        rows = pl.ds(pl.multiple_of(i * tile, 16), tile)
        return pltpu.make_async_copy(base_ref.at[rows], held.at[i % 2], sems.at[i % 2])

    @pl.when(step == 0)
    def _():
        fetch(step).start()

    @pl.when(step + 1 < steps)
    def _():
        fetch(step + 1).start()

    fetch(step).wait()
    slot = step % 2
    for lo in range(0, out_ref.shape[1], 256):
        cols = slice(lo, lo + 256)
        first = jnp.dot(turn_ref[:, :SUBJ], cen_ref[0, :, cols], preferred_element_type=jnp.float32)
        second = jnp.dot(turn_ref[:, SUBJ:], cen_ref[1, :, cols], preferred_element_type=jnp.float32)
        base = held[slot, :, cols].astype(jnp.float32)
        out_ref[:, cols] = (base + scale_ref[0:1, 0:1] * first + scale_ref[1:2, 0:1] * second).astype(out_ref.dtype)


def copies(value, axis, count):
    return lax.all_to_all(jnp.broadcast_to(value[None], (count, *value.shape)), axis, 0, 0, tiled=True)


def body(raw_frames, mask_index, subspace, rotation):
    depth = raw_frames.shape[1]
    extent = raw_frames.shape[2]
    per_device = subspace.shape[1]
    slab = ("x", "core")
    masked = per_device * 8 * GRP
    bf16 = jnp.bfloat16
    f32 = jnp.float32
    like = jax.ShapeDtypeStruct
    swap = [(0, 1), (1, 0)]
    turns = [[(i, (i + k) % 4) for i in range(4)] for k in range(4)]
    at = jnp.stack([lax.axis_index("x"), lax.axis_index("core"), lax.axis_index("grp")]).astype(jnp.int32)

    slab_at = lax.axis_index("x") * 2 + lax.axis_index("core")
    tiles = mask_index.reshape(-1, RUN)[:, 0] // RUN - slab_at * (depth * extent // RUN)
    up = [(i, i + 1) for i in range(7)]
    down = [(i + 1, i) for i in range(7)]
    packed = jnp.stack([tiles, lax.ppermute(tiles, slab, up), lax.ppermute(tiles, slab, down)])
    at_ss, _ = lax.optimization_barrier((at, packed))
    held = [pltpu.VMEM((4 * WIDE, per_device), bf16)]
    other_ss = pl.pallas_call(
        basis_other_kernel,
        out_shape=like((4 * WIDE, K), bf16),
        in_specs=[smem(), *vmem(1)],
        out_specs=vmem(1)[0],
        scratch_shapes=held,
        compiler_params=params(24),
        name="basis_other",
    )(at_ss, subspace)
    every, other_ss = lax.optimization_barrier((copies(packed, "grp", GRP), other_ss))
    own = every[:, 0].reshape(-1)
    near = jnp.concatenate([every[: GRP // 4, 2].reshape(-1), every[3 * GRP // 4 :, 1].reshape(-1)])

    middles, rim, to_up, to_down = smooth(own, near, jnp.transpose(raw_frames, (1, 0, 2)))
    got_ss = lax.ppermute(other_ss, "core", swap)
    at_own, _ = lax.optimization_barrier((at, to_down))
    own_ss, next_ss, far_ss, back_ss, made = pl.pallas_call(
        basis_own_kernel,
        out_shape=[like((WIDE, K), bf16), like((WIDE, K), bf16), like((2, HALF, K), bf16), like((WIDE, K), bf16), like((8, RUN), f32)],
        in_specs=[smem(), *vmem(2)],
        out_specs=vmem(5),
        scratch_shapes=held,
        compiler_params=params(24),
        name="basis_own",
    )(at_own, subspace, got_ss)
    from_low, from_high = lax.ppermute(to_up, slab, up), lax.ppermute(to_down, slab, down)
    placed = pl.pallas_call(
        rim_kernel,
        out_shape=like(middles.shape, bf16),
        in_specs=[*vmem(3), hbm(), *vmem(1)],
        out_specs=hbm(),
        scratch_shapes=[pltpu.VMEM(rim.shape, bf16), pltpu.SemaphoreType.DMA((2,))],
        input_output_aliases={3: 0},
        compiler_params=params(16),
        name="rim",
    )(rim, from_low, from_high, middles, made)
    regrouped = lax.all_to_all(placed, "grp", 0, 0, tiled=True)

    ahead, behind = turns[1], turns[3]
    next_ss, back_ss = pl.pallas_call(
        basis_relay_kernel,
        out_shape=[like((WIDE, K), bf16)] * 2,
        in_specs=vmem(4),
        out_specs=vmem(2),
        compiler_params=params(16),
        name="basis_relay",
    )(next_ss, back_ss, lax.ppermute(far_ss[0], "x", ahead), lax.ppermute(far_ss[1], "x", behind))
    regrouped, _, _ = lax.optimization_barrier((regrouped, next_ss, back_ss))
    went_on = lax.ppermute(next_ss, "x", ahead)
    went_back = lax.ppermute(back_ss, "x", behind)
    by_row = pl.pallas_call(
        basis_rows_kernel,
        out_shape=like((GRP, SHARE, RUN), bf16),
        in_specs=[smem(), *vmem(3)],
        out_specs=vmem(1)[0],
        scratch_shapes=[pltpu.VMEM((WIDE, 1408), f32)],
        compiler_params=params(16),
        name="basis_rows",
    )(at, own_ss, went_on, went_back)

    centered, other_c, own_c, power = pl.pallas_call(
        columns_kernel,
        out_shape=[like((2, SUBJ, per_device), bf16), like((KX, SUBJ), bf16), like((KX, SUBJ), f32), like((8, RUN), f32)],
        in_specs=[smem(), *vmem(1), hbm()],
        out_specs=[hbm(), *vmem(1), hbm(), *vmem(1)],
        scratch_shapes=[
            pltpu.VMEM((K, per_device), bf16),
            pltpu.VMEM((2, SUBJ, per_device), bf16),
            pltpu.VMEM((KX, SUBJ), f32),
            pltpu.SemaphoreType.DMA((3,)),
        ],
        compiler_params=params(50),
        name="columns",
    )(at, regrouped, subspace)
    sent = pl.pallas_call(
        windows_kernel,
        out_shape=like((GRP, 2 * TALL + SHARE, RUN), bf16),
        in_specs=[hbm(), *vmem(3)],
        out_specs=vmem(1)[0],
        scratch_shapes=[pltpu.VMEM((KX, SUBJ), f32), pltpu.SemaphoreType.DMA],
        compiler_params=params(16),
        name="windows",
    )(own_c, lax.ppermute(other_c, "core", swap), power, by_row)
    summed = lax.all_to_all(sent, "grp", 0, 0, tiled=True)

    rotation_b, _ = lax.optimization_barrier((rotation, sent))
    contract = (((0,), (0,)), ((), ()))
    from_basis = lax.dot_general(rotation_b[:K], subspace, contract, preferred_element_type=f32).astype(bf16)
    summed, from_basis, turn = lax.optimization_barrier((summed, from_basis, rotation_b[K:].T))

    total = pl.pallas_call(
        total_kernel,
        out_shape=like((2 * TALL + SHARE, RUN), bf16),
        in_specs=vmem(1),
        out_specs=vmem(1)[0],
        compiler_params=params(16),
        name="total",
    )(summed)
    sum_c, share = pl.pallas_call(
        slab_kernel,
        out_shape=[like((2 * TALL, RUN), f32), like((4, SHARE, RUN), bf16)],
        in_specs=vmem(4),
        out_specs=vmem(2),
        compiler_params=params(16),
        name="slab",
    )(total, *[lax.ppermute(total, "x", turns[k]) for k in range(1, 4)])
    rows_c, scales, turned = pl.pallas_call(
        functools.partial(finish_kernel, float(masked * SUBJ)),
        out_shape=[like((TALL, 2 * SUBJ), f32), like((8, RUN), f32), like((GRP, TURNED, TALL), bf16)],
        in_specs=[smem(), *vmem(2)],
        out_specs=vmem(3),
        compiler_params=params(16),
        name="finish",
    )(at, sum_c, lax.ppermute(sum_c, "core", swap))

    back = lax.all_to_all(turned, "grp", 0, 0, tiled=True)
    gram_rows = pl.pallas_call(
        functools.partial(assemble_kernel, float(masked)),
        out_shape=like((ROWS, KX), f32),
        in_specs=[smem(), *vmem(5)],
        out_specs=vmem(1)[0],
        scratch_shapes=[pltpu.VMEM((TALL, 1408), f32), pltpu.VMEM((TALL, 1408), f32)],
        compiler_params=params(16),
        name="assemble",
    )(at, back, rows_c, scales, share, lax.ppermute(share, "core", swap))

    tile = 240
    new_subspace = pl.pallas_call(
        functools.partial(rotate_kernel, tile),
        out_shape=like((K, per_device), bf16),
        grid=(K // tile,),
        in_specs=[
            pl.BlockSpec((8, RUN), lambda i: (0, 0)),
            hbm(),
            pl.BlockSpec((tile, 2 * SUBJ), lambda i: (i, 0)),
            pl.BlockSpec((2, SUBJ, per_device), lambda i: (0, 0, 0)),
        ],
        out_specs=pl.BlockSpec((tile, per_device), lambda i: (i, 0)),
        scratch_shapes=[pltpu.VMEM((2, tile, per_device), bf16), pltpu.SemaphoreType.DMA((2,))],
        compiler_params=params(BIG),
        name="rotate",
    )(scales, from_basis, turn, centered)
    return (gram_rows, new_subspace)


def solution(mesh):
    fine = Mesh(mesh.devices.reshape(4, 2, GRP), ("x", "core", "grp"))
    slab = ("x", "core")
    placed = (P("grp", slab, None), P((*slab, "grp")), P(None, (*slab, "grp")), P())
    return jax.shard_map(
        body,
        mesh=fine,
        in_specs=placed,
        out_specs=(P("grp", None), P(None, (*slab, "grp"))),
        check_vma=False,
    )
```
